128 devices in a mesh: row: 8 (over y, core), col: 16 (over z, x).
Axes of the slice: x: 4, y: 4, z: 4, core: 2. Of those that a mesh axis runs over, the one named last changes fastest.
Arguments:
- hidden_states: bfloat16 [1024, 2048], P('col', 'row'), may hold values from -20 to 20
- input_gain: float32 [2, 2048], P(None, 'row'), may hold values from 0.25 to 1.75
- inner_weight: bfloat16 [2, 2048, 2, 4096], P(None, 'row', None, 'col'), may hold values from -0.125 to 0.125
- proj_weight: bfloat16 [2, 2048, 256], P(None, 'row'), may hold values from -0.125 to 0.125
- step_weight: bfloat16 [2, 2048, 64], P(None, 'row', 'col'), may hold values from -0.125 to 0.125
- inner_kernel: float32 [2, 4, 4096], P(None, None, 'col'), may hold values from -3 to 3
- proj_kernel: float32 [2, 4, 256], replicated, may hold values from -3 to 3
- step_bias: float32 [2, 64], P(None, 'col'), may hold values from -5 to -1
- decay_log: float32 [2, 64], P(None, 'col'), may hold values from -2 to 1
- skip_gain: float32 [2, 64], P(None, 'col'), may hold values from 0.5 to 1.5
- norm_gain: float32 [2, 4096], P(None, 'col'), may hold values from 0.25 to 1.75
- out_weight: bfloat16 [2, 4096, 2048], P(None, 'col', 'row'), may hold values from -0.09375 to 0.09375
- inner_cache: bfloat16 [2, 64, 3, 4096], P(None, 'row', None, 'col'), may hold values from -6 to 6
- proj_cache: bfloat16 [2, 64, 3, 256], P(None, 'row'), may hold values from -6 to 6
- state_cache: float32 [2, 64, 64, 64, 128], P(None, 'row', 'col'), may hold values from -1.2 to 1.2
- accepted: int32 [64], P('row'), may hold values from 1 to 16
- owners: int32 [64], P('row'), may hold values from 0 to 15, as said below
- tenant_ranges: int32 [4, 2], replicated, may hold values from 0 to 64, as said below
Outputs:
- hidden_output: bfloat16 [1024, 2048], P('col', 'row')
- step_states: bfloat16 [2, 64, 16, 64, 64, 128], P(None, 'row', None, 'col')
- owned_states: bfloat16 [8, 16, 2, 2, 64, 64, 128], P('row', 'col')
The draws below stay inside these ranges and needn't reach their ends.
Inputs may be any that keep to these rules, and one draw needn't show every extreme that they name: `owners`: within the requests of one index of row (aligned blocks of 8) no owner appears more than 2 times, and in every block some owner appears exactly 2 times. `tenant_ranges`: the ranges are in order, disjoint and not empty; exactly 8 requests lie in no range.
All inputs are finite; a program needn't handle non-finite values.
Results may differ from the reference program's by a relative error of at most 0.024.
Values may be sent and summed in bfloat16 or wider, within the bound.
No kernel may reach another device: no remote copies, remote signals or barrier semaphores. Data moves between devices by JAX's collectives and lax.ppermute only.
A program may use at most 128 MiB of HBM per device.

```python
import jax
import jax.numpy as jnp
from jax import lax

D = 2048
H = 64
P_SIZE = 64
N = 128
K = 4
L = 2
S = 16
TENANTS = 4
SEND_CAP = 2
REQ_ROW = 8
DI = 4096
REQ = 64
TOK = 1024
GROUPS = 8
OWNERS = 16


def draw_hidden_states(key, part):
    first_key = jax.random.fold_in(key, 0)
    column_scale = 0.5 + jnp.arange(D, dtype=jnp.float32) / D
    drawn = jax.random.truncated_normal(first_key, -4.0, 4.0, (TOK, D), jnp.float32) * column_scale
    return drawn.astype(jnp.bfloat16)


def draw_owners(key, part):

    def one_block(block_key):
        sub_keys = jax.random.split(block_key, 3)
        shuffled = jax.random.permutation(sub_keys[0], OWNERS).astype(jnp.int32)
        others = jnp.repeat(shuffled[1:], SEND_CAP, total_repeat_length=(OWNERS - 1) * SEND_CAP)
        others = jax.random.permutation(sub_keys[1], others)
        listing = jnp.concatenate([jnp.full((SEND_CAP,), shuffled[0], dtype=jnp.int32), others.astype(jnp.int32)])[:REQ_ROW]
        return jax.random.permutation(sub_keys[2], listing)
    block_keys = jax.random.split(key, GROUPS)
    return jax.vmap(one_block)(block_keys).reshape(REQ).astype(jnp.int32)


def composition(key, amount, pieces):
    cut_points = jnp.sort(jax.random.randint(key, (pieces - 1,), 0, amount + 1))
    edge_points = jnp.concatenate([jnp.zeros((1,), jnp.int32), cut_points.astype(jnp.int32), jnp.full((1,), amount, jnp.int32)])
    return edge_points[1:] - edge_points[:-1]


def draw_tenant_ranges(key, part):
    dead_count = REQ // 8
    live_count = REQ - dead_count
    first_key, second_key = jax.random.split(key)
    lengths = composition(first_key, live_count - TENANTS, TENANTS) + 1
    gap_sizes = composition(second_key, dead_count, TENANTS + 1)
    starts = jnp.cumsum(gap_sizes[:TENANTS]) + jnp.concatenate([jnp.zeros((1,), jnp.int32), jnp.cumsum(lengths)[:-1].astype(jnp.int32)])
    end_points = starts + lengths
    return jnp.stack([starts, end_points], axis=1).astype(jnp.int32)


def plant(array, key, least, high):
    dims = array.shape
    place = [jax.random.randint(jax.random.fold_in(key, axis), (), 0, dims[axis]) for axis in range(len(dims))]
    array = array.at[tuple(place)].set(least)
    longest = dims.index(max(dims))
    place[longest] = (place[longest] + 1) % dims[longest]
    return array.at[tuple(place)].set(high)


def steps_of(key, extent, shards, smallest, largest):
    def one(axis_at, shards_of):
        steps = jax.random.uniform(jax.random.fold_in(jax.random.fold_in(key, 6), axis_at), (shards_of,), jnp.float32, smallest / len(shards), largest / len(shards))
        return jnp.repeat(jnp.exp(steps), extent[axis_at] // shards_of).reshape((-1,) + (1,) * (len(extent) - axis_at - 1))

    factor_of = one(*shards[0])
    for cut in shards[1:]:
        factor_of = factor_of * one(*cut)
    return factor_of


def scatter_about(own_key, extent, scale, most, cuts=(), kind=jnp.bfloat16):
    array = scale * jax.random.normal(own_key, extent, jnp.float32)
    if cuts:
        array = array * steps_of(own_key, extent, cuts, -0.22, 0.18)
    return jnp.clip(array, -most, most).astype(kind)


def setup_inputs(seed: int = 0) -> dict:
    keys = jax.random.split(jax.random.key(seed), 19)
    return {
        "hidden_states": draw_hidden_states(jax.random.fold_in(keys[18], 71), 0),
        "input_gain": jnp.clip(1.0 + 0.15 * jax.random.normal(keys[1], (L, D), jnp.float32), 0.25, 1.75),
        "inner_weight": scatter_about(keys[2], (L, D, 2, DI), D ** -0.5, 0.125, ((1, 8), (3, 16))),
        "proj_weight": scatter_about(keys[3], (L, D, 2 * N), D ** -0.5, 0.125, ((1, 8),)),
        "step_weight": scatter_about(keys[4], (L, D, H), D ** -0.5, 0.125, ((1, 8), (2, 16))),
        "inner_kernel": scatter_about(keys[5], (L, K, DI), K ** -0.5, 3.0, ((2, 16),), jnp.float32),
        "proj_kernel": scatter_about(keys[6], (L, K, 2 * N), K ** -0.5, 3.0, (), jnp.float32),
        "step_bias": jnp.clip(-5.0 + 4.0 * jax.random.uniform(keys[7], (L, H), jnp.float32) ** steps_of(keys[7], (L, H), ((1, 16),), -0.2, 0.2), -5.0, -1.0),
        "decay_log": jnp.clip(-2.0 + 3.0 * jax.random.uniform(keys[8], (L, H), jnp.float32) ** steps_of(keys[8], (L, H), ((1, 16),), -0.2, 0.2), -2.0, 1.0),
        "skip_gain": jnp.clip(0.5 + 1.0 * jax.random.uniform(keys[9], (L, H), jnp.float32) ** steps_of(keys[9], (L, H), ((1, 16),), -0.2, 0.2), 0.5, 1.5),
        "norm_gain": jnp.clip(1.0 + 0.15 * jax.random.normal(keys[10], (L, DI), jnp.float32), 0.25, 1.75),
        "out_weight": scatter_about(keys[11], (L, DI, D), DI ** -0.5, 0.09375, ((1, 16), (2, 8))),
        "inner_cache": scatter_about(keys[12], (L, REQ, K - 1, DI), 1.0, 6.0, ((1, 8), (3, 16))),
        "proj_cache": scatter_about(keys[13], (L, REQ, K - 1, 2 * N), 1.0, 6.0, ((1, 8),)),
        "state_cache": scatter_about(keys[14], (L, REQ, H, P_SIZE, N), 0.2, 1.2, ((1, 8), (2, 16)), jnp.float32),
        "accepted": plant(jax.random.randint(keys[15], (REQ,), 1, S + 1), jax.random.fold_in(keys[15], 1), 1, S).astype(jnp.int32),
        "owners": draw_owners(jax.random.fold_in(keys[18], 71), 0),
        "tenant_ranges": draw_tenant_ranges(jax.random.fold_in(keys[18], 71), 0),
    }


EPSILON = 1e-05

def conv_silu(prefix, incoming, kernel):
    joined = jnp.concatenate([prefix, incoming], axis=1)
    length = incoming.shape[1]
    summed = joined[:, 0:length, :] * kernel[0]
    for offset in range(1, kernel.shape[0]):
        summed = summed + joined[:, offset:offset + length, :] * kernel[offset]
    return jax.nn.silu(summed)

def ssm_scan(decays, deltas, inner_values, b_values, c_values, skip_values, start_state):

    def advance(carried, packed):
        decay_now, delta_now, value_now, b_now, c_now = packed
        updated = decay_now[:, :, None, None] * carried + (delta_now[:, :, None] * value_now)[:, :, :, None] * b_now[:, None, None, :]
        output = jnp.einsum('rhpn,rn->rhp', updated, c_now, precision=lax.Precision.HIGHEST) + skip_values[None, :, None] * value_now
        return (updated, (output, updated.astype(jnp.bfloat16)))
    time_major = tuple((jnp.moveaxis(member, 1, 0) for member in (decays, deltas, inner_values, b_values, c_values)))
    last_state, (outputs, states) = lax.scan(advance, start_state, time_major)
    return (jnp.moveaxis(outputs, 0, 1), jnp.moveaxis(states, 0, 1))

def mamba_layer(hidden, input_gain, inner_weight, proj_weight, step_weight, inner_kernel, proj_kernel, step_bias, decay_log, skip_gain, norm_gain, out_weight, inner_cache, proj_cache, state_cache):
    requests = state_cache.shape[0]
    tokens_f = hidden.astype(jnp.float32)
    inverse_rms = lax.rsqrt(lax.optimization_barrier(jnp.sum(tokens_f * tokens_f, axis=1)) / D + EPSILON)
    scaled = (tokens_f * input_gain).astype(jnp.bfloat16)
    inner_vals = jnp.dot(scaled, inner_weight.reshape(D, 2 * DI), preferred_element_type=jnp.float32) * inverse_rms[:, None]
    proj_vals = jnp.dot(scaled, proj_weight, preferred_element_type=jnp.float32) * inverse_rms[:, None]
    step_vals = jnp.dot(scaled, step_weight, preferred_element_type=jnp.float32) * inverse_rms[:, None]
    gate_vals = inner_vals[:, :DI]
    raw_inner = inner_vals[:, DI:].reshape(requests, S, DI)
    raw_proj = proj_vals.reshape(requests, S, 2 * N)
    conv_inner = conv_silu(inner_cache.astype(jnp.float32), raw_inner, inner_kernel)
    conv_proj = conv_silu(proj_cache.astype(jnp.float32), raw_proj, proj_kernel)
    deltas = jax.nn.softplus(step_vals.reshape(requests, S, H) + step_bias)
    decays = jnp.exp(-deltas * jnp.exp(decay_log))
    outputs, states = ssm_scan(decays, deltas, conv_inner.reshape(requests, S, H, P_SIZE), conv_proj[..., :N], conv_proj[..., N:], skip_gain, state_cache)
    gated_raw = outputs.reshape(requests * S, DI) * jax.nn.silu(gate_vals)
    gate_square = lax.optimization_barrier(jnp.sum(gated_raw * gated_raw, axis=1))
    gated = (gated_raw * norm_gain * lax.rsqrt(gate_square / DI + EPSILON)[:, None]).astype(jnp.bfloat16)
    result = (tokens_f + jnp.dot(gated, out_weight, preferred_element_type=jnp.float32)).astype(jnp.bfloat16)
    return (result, states)

def reference(hidden_states, input_gain, inner_weight, proj_weight, step_weight, inner_kernel, proj_kernel, step_bias, decay_log, skip_gain, norm_gain, out_weight, inner_cache, proj_cache, state_cache, accepted, owners, tenant_ranges):
    hidden = hidden_states
    request_ids = jnp.arange(REQ, dtype=jnp.int32)
    step_list = []
    chosen_list = []
    for layer_index in range(L):
        hidden, states = mamba_layer(hidden, input_gain[layer_index], inner_weight[layer_index], proj_weight[layer_index], step_weight[layer_index], inner_kernel[layer_index], proj_kernel[layer_index], step_bias[layer_index], decay_log[layer_index], skip_gain[layer_index], norm_gain[layer_index], out_weight[layer_index], inner_cache[layer_index], proj_cache[layer_index], state_cache[layer_index])
        step_list.append(states)
        chosen_list.append(states[request_ids, (accepted - 1).astype(jnp.int32)])
    live_mask = jnp.any((request_ids[:, None] >= tenant_ranges[None, :, 0]) & (request_ids[:, None] < tenant_ranges[None, :, 1]), axis=1)
    block_ids = (request_ids // REQ_ROW).astype(jnp.int32)
    earlier = (owners[:, None] == owners[None, :]) & (block_ids[:, None] == block_ids[None, :]) & (request_ids[None, :] < request_ids[:, None])
    slot_ranks = lax.optimization_barrier(jnp.sum(earlier.astype(jnp.int32), axis=1)).astype(jnp.int32)
    chosen_all = jnp.stack(chosen_list, axis=1)
    chosen_all = jnp.where(live_mask[:, None, None, None, None], chosen_all, jnp.zeros_like(chosen_all))
    owned_states = jnp.zeros((GROUPS, OWNERS, SEND_CAP, L, H, P_SIZE, N), jnp.bfloat16).at[block_ids, owners, slot_ranks].set(chosen_all)
    return (hidden, jnp.stack(step_list, axis=0), owned_states)
```

```python
import jax
import jax.numpy as jnp
from jax import lax
from jax.experimental import pallas as pl
from jax.experimental.pallas import tpu as pltpu
from jax.sharding import PartitionSpec as P

S = 16
SEND_CAP = 2
EPSILON = 1e-05
ROWS = 8
COLS = 16
BF = jnp.bfloat16
F32 = jnp.float32
SUM_ROWS = 16


def silu(v):
    return v / (1.0 + jnp.exp(-v))


def softplus(v):
    return jnp.maximum(v, 0.0) + jnp.log1p(jnp.exp(-jnp.abs(v)))


def mixer_body(
    layer,
    slots_ref,
    accepted_ref,
    bias_ref,
    decay_log_ref,
    skip_ref,
    hidden_ref,
    weight_ref,
    out_weight_ref,
    inner_kernel_ref,
    proj_kernel_ref,
    norm_gain_ref,
    inner_cache_ref,
    proj_cache_ref,
    state_ref,
    *rest,
):
    (
        steps_ref,
        send_ref,
        part_ref,
        z_s,
        x_pad,
        p_pad,
        x_s,
        dx_s,
        b_s,
        c_s,
        dec_s,
        ydiag_s,
        ecum_s,
        yg_s,
        g2_s,
    ) = rest[-15:]
    q = pl.program_id(0)
    requests = x_pad.shape[0]
    tokens = requests * S
    width = z_s.shape[1]
    state_size = b_s.shape[1]
    heads = dec_s.shape[1] // 128
    model_width = ROWS * hidden_ref.shape[2]
    block_tokens = hidden_ref.shape[1]
    lane = lax.broadcasted_iota(jnp.int32, (1, 128), 1)

    def spread(pieces):
        return jnp.concatenate(
            [jnp.where(lane < 64, pieces[2 * k], pieces[2 * k + 1]) for k in range(heads // 2)],
            axis=1,
        )

    @pl.when(q == 0)
    def _first():
        send_ref[...] = jnp.zeros(send_ref.shape, BF)
        total = jnp.zeros((tokens, weight_ref.shape[2]), F32)
        squares = jnp.zeros((tokens, 128), F32)
        for r in range(ROWS):
            rows_r = jnp.concatenate([hidden_ref[r], hidden_ref[ROWS + r]], axis=0)
            total = total + jnp.dot(rows_r, weight_ref[r], preferred_element_type=F32)
            wide = rows_r.astype(F32)
            wide = wide * wide
            squares = squares + wide[:, :128] + wide[:, 128:]
        inverse = lax.rsqrt(jnp.sum(squares, axis=1, keepdims=True) / model_width + EPSILON)
        total = total * inverse
        z_s[...] = total[:, :width]
        x_pad[:, 8:24, :] = total[:, width : 2 * width].reshape(requests, S, width)
        p_pad[:, 8:24, :] = total[:, 2 * width : 2 * width + 2 * state_size].reshape(
            requests, S, 2 * state_size
        )
        x_pad[:, 5:8, :] = inner_cache_ref[...].astype(F32)
        p_pad[:, 5:8, :] = proj_cache_ref[...].astype(F32)
        conv_x = x_pad[:, 5 : 5 + S, :] * inner_kernel_ref[0:1, :]
        conv_p = p_pad[:, 5 : 5 + S, :] * proj_kernel_ref[0:1, :]
        for i in range(1, 4):
            conv_x = conv_x + x_pad[:, 5 + i : 5 + i + S, :] * inner_kernel_ref[i : i + 1, :]
            conv_p = conv_p + p_pad[:, 5 + i : 5 + i + S, :] * proj_kernel_ref[i : i + 1, :]
        x_conv = silu(conv_x).reshape(tokens, width)
        p_conv = silu(conv_p).reshape(tokens, 2 * state_size)
        b_conv = p_conv[:, :state_size]
        c_conv = p_conv[:, state_size:]
        x_s[...] = x_conv
        b_s[...] = b_conv
        c_s[...] = c_conv.astype(BF)
        step_raw = total[:, 2 * width + 2 * state_size :]
        t_now = lax.broadcasted_iota(jnp.int32, (tokens, tokens), 0)
        t_then = lax.broadcasted_iota(jnp.int32, (tokens, tokens), 1)
        causal = (t_now // S == t_then // S) & (t_then <= t_now)
        lower = causal.astype(F32)
        scores = lax.dot_general(
            c_conv.astype(BF), b_conv.astype(BF), (((1,), (1,)), ((), ())),
            preferred_element_type=F32,
        )
        deltas = []
        cums = []
        mixes = []
        for h in range(heads):
            raw = jnp.broadcast_to(step_raw[:, h : h + 1], (tokens, 128))
            delta = softplus(raw + bias_ref[layer, h])
            rate = jnp.exp(jnp.full((1, 128), decay_log_ref[layer, h], F32))
            log_decay = -delta * rate
            dec_s[:, h * 128 : (h + 1) * 128] = jnp.exp(log_decay)
            cum = jnp.dot(
                lower, log_decay, precision=lax.Precision.HIGHEST, preferred_element_type=F32
            )
            gap = jnp.where(causal, cum - cum.T, 0.0)
            mixes.append((jnp.where(causal, jnp.exp(gap), 0.0) * scores).astype(BF))
            deltas.append(delta)
            cums.append(jnp.exp(cum))
        dx = x_conv * spread(deltas)
        dx_s[...] = dx
        ecum_s[...] = spread(cums)
        for k in range(heads // 2):
            dx_k = dx[:, 128 * k : 128 * (k + 1)].astype(BF)
            first = jnp.dot(mixes[2 * k], dx_k, preferred_element_type=F32)
            second = jnp.dot(mixes[2 * k + 1], dx_k, preferred_element_type=F32)
            ydiag_s[:, 128 * k : 128 * (k + 1)] = jnp.where(lane < 64, first, second)

    rows = pl.ds(pl.multiple_of(q * S, S), S)
    start = state_ref[...]
    flat = start.reshape(heads * start.shape[1], state_size)
    y_off = lax.dot_general(
        c_s[rows, :], flat.astype(BF), (((1,), (1,)), ((), ())), preferred_element_type=F32
    )
    skip = spread([jnp.full((1, 128), skip_ref[layer, h], F32) for h in range(heads)])
    y = ydiag_s[rows, :] + ecum_s[rows, :] * y_off + skip * x_s[rows, :]
    g = y * silu(z_s[rows, :])
    yg_s[rows, :] = (g * norm_gain_ref[layer : layer + 1, :]).astype(BF)
    g2_s[rows, :] = (g * g).astype(BF)

    dx_t = dx_s[rows, :].T
    b_q = b_s[rows, :]
    dec_q = dec_s[rows, :]
    head_size = start.shape[1]
    for h in range(heads):
        state = start[h]
        columns = dx_t[h * head_size : (h + 1) * head_size, :]
        for t in range(S):
            state = (
                state * dec_q[t : t + 1, h * 128 : (h + 1) * 128]
                + columns[:, t : t + 1] * b_q[t : t + 1, :]
            )
            steps_ref[t, h] = state.astype(BF)

    @pl.when(slots_ref[q] >= 0)
    def _choose():
        send_ref[slots_ref[q]] = steps_ref[accepted_ref[q] - 1]

    @pl.when(q == requests - 1)
    def _last():
        yg = yg_s[...]
        g2 = g2_s[...]
        ones = jnp.ones((SUM_ROWS, width), BF)
        sums = [
            lax.dot_general(
                ones,
                g2[b * block_tokens : (b + 1) * block_tokens, :],
                (((1,), (1,)), ((), ())),
                preferred_element_type=F32,
            ).astype(BF)
            for b in range(2)
        ]
        for r in range(ROWS):
            part = jnp.dot(yg, out_weight_ref[r], preferred_element_type=F32).astype(BF)
            for b in range(2):
                part_ref[b * ROWS + r, 0:block_tokens, :] = part[
                    b * block_tokens : (b + 1) * block_tokens, :
                ]
                part_ref[b * ROWS + r, block_tokens:, :] = jnp.zeros((SUM_ROWS, width), BF)
                part_ref[b * ROWS + r, block_tokens:, 0:block_tokens] = sums[b]


def mixer(layer, slots, accepted, bias, decay_log, skip, hidden, weight, out_weight,
          inner_kernel, proj_kernel, norm_gain, inner_cache, proj_cache, state, previous):
    layers, requests, heads, head_size, state_size = state.shape
    width = heads * head_size
    tokens = requests * S
    block_tokens = hidden.shape[1]
    smem = pl.BlockSpec(memory_space=pltpu.SMEM)

    def whole(shape):
        return pl.BlockSpec(shape, lambda q: (0,) * len(shape))

    in_specs = [
        smem, smem, smem, smem, smem,
        whole(hidden.shape),
        whole(weight.shape),
        pl.BlockSpec((ROWS, None) + out_weight.shape[2:], lambda q: (0, layer, 0, 0)),
        pl.BlockSpec((None,) + inner_kernel.shape[1:], lambda q: (layer, 0, 0)),
        pl.BlockSpec((None,) + proj_kernel.shape[1:], lambda q: (layer, 0, 0)),
        whole(norm_gain.shape),
        pl.BlockSpec((None,) + inner_cache.shape[1:], lambda q: (layer, 0, 0, 0)),
        pl.BlockSpec((None,) + proj_cache.shape[1:], lambda q: (layer, 0, 0, 0)),
        pl.BlockSpec((None, None, heads, head_size, state_size), lambda q: (layer, q, 0, 0, 0)),
    ]
    operands = [slots, accepted, bias, decay_log, skip, hidden, weight, out_weight,
                inner_kernel, proj_kernel, norm_gain, inner_cache, proj_cache, state]
    aliases = {}
    if previous is not None:
        in_specs.append(pl.BlockSpec(memory_space=pl.ANY))
        aliases = {len(operands): 0}
        operands.append(previous)
    return pl.pallas_call(
        lambda *refs: mixer_body(layer, *refs),
        name="mixer%d" % layer,
        grid=(requests,),
        in_specs=in_specs,
        out_specs=[
            pl.BlockSpec(
                (None, None, S, heads, head_size, state_size),
                lambda q: (layer, q, 0, 0, 0, 0),
            ),
            whole((COLS * SEND_CAP, heads, head_size, state_size)),
            whole((COLS, block_tokens + SUM_ROWS, width)),
        ],
        out_shape=[
            jax.ShapeDtypeStruct((layers, requests, S, heads, head_size, state_size), BF),
            jax.ShapeDtypeStruct((COLS * SEND_CAP, heads, head_size, state_size), BF),
            jax.ShapeDtypeStruct((COLS, block_tokens + SUM_ROWS, width), BF),
        ],
        scratch_shapes=[
            pltpu.VMEM((tokens, width), F32),
            pltpu.VMEM((requests, 24, width), F32),
            pltpu.VMEM((requests, 24, 2 * state_size), F32),
            pltpu.VMEM((tokens, width), F32),
            pltpu.VMEM((tokens, width), F32),
            pltpu.VMEM((tokens, state_size), F32),
            pltpu.VMEM((tokens, state_size), BF),
            pltpu.VMEM((tokens, heads * 128), F32),
            pltpu.VMEM((tokens, width), F32),
            pltpu.VMEM((tokens, width), F32),
            pltpu.VMEM((tokens, width), BF),
            pltpu.VMEM((tokens, width), BF),
        ],
        input_output_aliases=aliases,
        compiler_params=pltpu.CompilerParams(
            dimension_semantics=("arbitrary",), vmem_limit_bytes=48 * 1024 * 1024
        ),
    )(*operands)


def update_body(inner_width, received_ref, hidden_ref, out_ref):
    rows = hidden_ref.shape[0]
    total = received_ref[0].astype(F32)
    for c in range(1, COLS):
        total = total + received_ref[c].astype(F32)
    sums = total[rows:, 0:128].T[:rows, 0:1]
    scale = lax.rsqrt(sums / inner_width + EPSILON)
    fresh = (hidden_ref[...].astype(F32) + total[:rows, :] * scale).astype(BF)
    if len(out_ref.shape) == 3:
        for c in range(COLS):
            out_ref[c] = fresh
    else:
        out_ref[...] = fresh


def update(inner_width, received, hidden, spread):
    shape = ((COLS,) if spread else ()) + hidden.shape
    return pl.pallas_call(
        lambda *refs: update_body(inner_width, *refs),
        name="update_spread" if spread else "update_last",
        out_shape=jax.ShapeDtypeStruct(shape, BF),
    )(received, hidden)


def swap(x):
    return lax.all_to_all(x, "col", 0, 0, tiled=True)


def local(
    hidden_states,
    input_gain,
    inner_weight,
    proj_weight,
    step_weight,
    inner_kernel,
    proj_kernel,
    step_bias,
    decay_log,
    skip_gain,
    norm_gain,
    out_weight,
    inner_cache,
    proj_cache,
    state_cache,
    accepted,
    owners,
    tenant_ranges,
):
    layer_count = inner_weight.shape[0]
    row_width = inner_weight.shape[1]
    inner_local = inner_weight.shape[3]
    heads_local = step_weight.shape[2]
    requests_local = state_cache.shape[1]
    inner_width = inner_local * COLS
    local_ids = jnp.arange(requests_local, dtype=jnp.int32)
    request_ids = lax.axis_index("row") * requests_local + local_ids
    live_mask = jnp.any(
        (request_ids[:, None] >= tenant_ranges[None, :, 0])
        & (request_ids[:, None] < tenant_ranges[None, :, 1]),
        axis=1,
    )
    earlier = (owners[:, None] == owners[None, :]) & (local_ids[None, :] < local_ids[:, None])
    slot_ranks = jnp.sum(earlier.astype(jnp.int32), axis=1)
    slots = jnp.where(live_mask, owners * SEND_CAP + slot_ranks, -1)

    there = []
    for r in range(ROWS):
        for c in range(COLS):
            there.append((r * COLS + c, (c // 2) * COLS + (c % 2) * ROWS + r))
    back = [(b, a) for a, b in there]

    def packed(layer):
        joined = jnp.concatenate(
            [
                inner_weight[layer].reshape(row_width, 2 * inner_local),
                proj_weight[layer],
                jnp.pad(step_weight[layer], ((0, 0), (0, 128 - heads_local))),
            ],
            axis=1,
        )
        return (joined.astype(F32) * input_gain[layer][:, None]).astype(BF)

    weights = [lax.all_gather(packed(0), "row", axis=0)]
    out_all = lax.all_gather(out_weight, "row", axis=0)
    weights.append(lax.all_gather(packed(1), "row", axis=0))

    block = lax.ppermute(hidden_states, ("row", "col"), there)
    spread = jnp.broadcast_to(block[None], (COLS,) + block.shape)
    steps = None
    owned = []
    for layer in range(layer_count):
        everything = swap(spread)
        steps, send, part = mixer(
            layer, slots, accepted, step_bias, decay_log, skip_gain, everything,
            weights[layer], out_all, inner_kernel, proj_kernel, norm_gain,
            inner_cache, proj_cache, state_cache, steps,
        )
        received = swap(part)
        last = layer == layer_count - 1
        fresh = update(inner_width, received, block, not last)
        if not last:
            spread = fresh
            block = fresh[0]
        owned.append(swap(send.reshape((COLS, SEND_CAP) + send.shape[1:])))
    hidden = lax.ppermute(fresh, ("row", "col"), back)
    stacked = jnp.stack(owned, axis=0)
    stacked = jnp.transpose(stacked, (2, 0, 1, 3, 4, 5))
    owned_block = stacked.reshape(
        (1, 1, SEND_CAP, layer_count, COLS * heads_local) + stacked.shape[4:]
    )
    return (hidden, steps, owned_block)


def solution(mesh):
    placed = (
        P("col", "row"),
        P(None, "row"),
        P(None, "row", None, "col"),
        P(None, "row", None),
        P(None, "row", "col"),
        P(None, None, "col"),
        P(),
        P(None, "col"),
        P(None, "col"),
        P(None, "col"),
        P(None, "col"),
        P(None, "col", "row"),
        P(None, "row", None, "col"),
        P(None, "row", None, None),
        P(None, "row", "col", None, None),
        P("row"),
        P("row"),
        P(),
    )
    return jax.shard_map(
        local,
        mesh=mesh,
        in_specs=placed,
        out_specs=(
            P("col", "row"),
            P(None, "row", None, "col", None, None),
            P("row", "col", None, None, None, None, None),
        ),
        check_vma=False,
    )
```

```python
import jax
import jax.numpy as jnp
from jax import lax
from jax.experimental import pallas as pl
from jax.experimental.pallas import tpu as pltpu
from jax.sharding import PartitionSpec as P

S = 16
SEND_CAP = 2
EPSILON = 1e-05
ROWS = 8
COLS = 16
BF = jnp.bfloat16
F32 = jnp.float32
SUM_ROWS = 16


def silu(v):
    return v / (1.0 + jnp.exp(-v))


def softplus(v):
    return jnp.maximum(v, 0.0) + jnp.log1p(jnp.exp(-jnp.abs(v)))


def route(q, ints_ref, requests):
    owners, ranges = 1 + requests, 1 + 2 * requests
    request = ints_ref[0] + q
    live = (request >= ints_ref[ranges]) & (request < ints_ref[ranges + 1])
    for k in range(ranges + 2, ints_ref.shape[0], 2):
        live = live | ((request >= ints_ref[k]) & (request < ints_ref[k + 1]))
    owner = ints_ref[owners + q]
    rank = jnp.int32(0)
    for other in range(q):
        rank = rank + jnp.where(ints_ref[owners + other] == owner, 1, 0)
    return live, owner, jnp.minimum(rank, SEND_CAP - 1)


def put_start(out_ref, owner, rank, start):
    heads, head_size, _ = start.shape
    span = heads // 2 * head_size
    first = pl.multiple_of(rank * span, span)
    for k in range(heads // 2):
        pair = jnp.concatenate([start[2 * k], start[2 * k + 1]], axis=1)
        out_ref[owner, pl.ds(first + k * head_size, head_size), :] = pair.astype(BF)


def front_body(
    layer,
    head_rows,
    ints_ref,
    floats_ref,
    hidden_ref,
    weight_ref,
    inner_kernel_ref,
    proj_kernel_ref,
    norm_gain_ref,
    inner_cache_ref,
    proj_cache_ref,
    state_ref,
    part_ref,
    dx_ref,
    b_ref,
    dec_ref,
    x_pad,
    p_pad,
):
    requests, heads, head_size, state_size = state_ref.shape
    tokens = requests * S
    width = heads * head_size
    model_width = ROWS * hidden_ref.shape[2]
    block_tokens = hidden_ref.shape[1]
    in_cols = 2 * width + 2 * state_size + 128
    lane = lax.broadcasted_iota(jnp.int32, (1, 128), 1)

    def spread(pieces):
        return jnp.concatenate(
            [jnp.where(lane < 64, pieces[2 * k], pieces[2 * k + 1]) for k in range(heads // 2)],
            axis=1,
        )

    total = jnp.zeros((tokens, in_cols), F32)
    squares = jnp.zeros((tokens, 128), F32)
    for r in range(ROWS):
        rows_r = jnp.concatenate([hidden_ref[r], hidden_ref[ROWS + r]], axis=0)
        total = total + jnp.dot(rows_r, weight_ref[r, :, :in_cols], preferred_element_type=F32)
        wide = rows_r.astype(F32)
        wide = wide * wide
        squares = squares + wide[:, :128] + wide[:, 128:]
    inverse = lax.rsqrt(jnp.sum(squares, axis=1, keepdims=True) / model_width + EPSILON)
    total = total * inverse
    z = total[:, :width]
    x_pad[:, 8:24, :] = total[:, width : 2 * width].reshape(requests, S, width)
    p_pad[:, 8:24, :] = total[:, 2 * width : 2 * width + 2 * state_size].reshape(
        requests, S, 2 * state_size
    )
    x_pad[:, 5:8, :] = inner_cache_ref[...].astype(F32)
    p_pad[:, 5:8, :] = proj_cache_ref[...].astype(F32)
    conv_x = x_pad[:, 5 : 5 + S, :] * inner_kernel_ref[0:1, :]
    conv_p = p_pad[:, 5 : 5 + S, :] * proj_kernel_ref[0:1, :]
    for i in range(1, 4):
        conv_x = conv_x + x_pad[:, 5 + i : 5 + i + S, :] * inner_kernel_ref[i : i + 1, :]
        conv_p = conv_p + p_pad[:, 5 + i : 5 + i + S, :] * proj_kernel_ref[i : i + 1, :]
    x_conv = silu(conv_x).reshape(tokens, width)
    p_conv = silu(conv_p).reshape(tokens, 2 * state_size)
    b_conv = p_conv[:, :state_size]
    c_conv = p_conv[:, state_size:].astype(BF)
    b_ref[...] = b_conv
    step_raw = total[:, 2 * width + 2 * state_size :]
    t_now = lax.broadcasted_iota(jnp.int32, (tokens, tokens), 0)
    t_then = lax.broadcasted_iota(jnp.int32, (tokens, tokens), 1)
    causal = (t_now // S == t_then // S) & (t_then <= t_now)
    lower = causal.astype(F32)
    scores = lax.dot_general(
        c_conv, b_conv.astype(BF), (((1,), (1,)), ((), ())), preferred_element_type=F32
    )
    deltas = []
    sums_log = []
    mixes = []
    for h in range(heads):
        raw = jnp.broadcast_to(step_raw[:, h : h + 1], (tokens, 128))
        delta = softplus(raw + floats_ref[layer, h])
        rate = jnp.exp(jnp.full((1, 128), floats_ref[layer, heads + h], F32))
        log_decay = -delta * rate
        dec_ref[:, h * 128 : (h + 1) * 128] = jnp.exp(log_decay)
        cum = jnp.dot(
            lower, log_decay, precision=lax.Precision.HIGHEST, preferred_element_type=F32
        )
        gap = jnp.where(causal, cum - cum.T, 0.0)
        mixes.append((jnp.where(causal, jnp.exp(gap), 0.0) * scores).astype(BF))
        deltas.append(delta)
        sums_log.append(cum)
    dx = x_conv * spread(deltas)
    cum_all = spread(sums_log)
    grown = jnp.exp(cum_all)
    dx_ref[...] = dx
    y_diag = []
    for k in range(heads // 2):
        dx_k = dx[:, 128 * k : 128 * (k + 1)].astype(BF)
        first = jnp.dot(mixes[2 * k], dx_k, preferred_element_type=F32)
        second = jnp.dot(mixes[2 * k + 1], dx_k, preferred_element_type=F32)
        y_diag.append(jnp.where(lane < 64, first, second))
    y_off = []
    for q in range(requests):
        flat = state_ref[q].reshape(width, state_size).astype(BF)
        y_off.append(
            lax.dot_general(
                c_conv[q * S : (q + 1) * S, :], flat, (((1,), (1,)), ((), ())),
                preferred_element_type=F32,
            )
        )
    skip = spread([jnp.full((1, 128), floats_ref[layer, 2 * heads + h], F32) for h in range(heads)])
    y = (
        jnp.concatenate(y_diag, axis=1)
        + grown * jnp.concatenate(y_off, axis=0)
        + skip * x_conv
    )
    g = y * silu(z)
    yg = (g * norm_gain_ref[layer : layer + 1, :]).astype(BF)
    g2 = (g * g).astype(BF)
    ones = jnp.ones((SUM_ROWS, width), BF)
    part_row = head_rows + SEND_CAP * 2 * S
    sum_row = part_row + block_tokens
    part_ref[:, :part_row, :] = jnp.zeros((COLS, part_row, width), BF)
    for b in range(2):
        sums = lax.dot_general(
            ones,
            g2[b * block_tokens : (b + 1) * block_tokens, :],
            (((1,), (1,)), ((), ())),
            preferred_element_type=F32,
        ).astype(BF)
        for r in range(ROWS):
            part_ref[b * ROWS + r, sum_row:, :] = jnp.zeros((SUM_ROWS, width), BF)
            part_ref[b * ROWS + r, sum_row:, 0:block_tokens] = sums
    for r in range(ROWS):
        part = jnp.dot(yg, weight_ref[r, :, in_cols:], preferred_element_type=F32).astype(BF)
        for b in range(2):
            part_ref[b * ROWS + r, part_row:sum_row, :] = part[
                b * block_tokens : (b + 1) * block_tokens, :
            ]
    step = lax.broadcasted_iota(jnp.int32, (S, 1), 0)
    for q in range(requests):
        live, owner, rank = route(q, ints_ref, requests)
        taken = ints_ref[1 + q] - 1
        rows = slice(q * S, (q + 1) * S)
        cum_q = cum_all[rows, :]
        cum_end = jnp.sum(jnp.where(step == taken, cum_q, 0.0), axis=0, keepdims=True)
        inside = step <= taken
        weight = jnp.where(inside, jnp.exp(jnp.where(inside, cum_end - cum_q, 0.0)), 0.0)
        scale = jnp.exp(cum_end)
        high = scale.astype(BF).astype(F32)
        low = scale - high
        extra = jnp.where(
            step == 0,
            high[:, :128],
            jnp.where(
                step == 1, high[:, 128:], jnp.where(step == 2, low[:, :128], low[:, 128:])
            ),
        )
        first = pl.multiple_of(head_rows + rank * 2 * S, 2 * S)

        @pl.when(live)
        def _send():
            part_ref[owner, pl.ds(first, S), :] = (dx[rows, :] * weight).astype(BF)
            part_ref[owner, pl.ds(first + S, S), :] = jnp.concatenate(
                [b_conv[rows, :], extra], axis=1
            ).astype(BF)
            if head_rows:
                put_start(part_ref, owner, rank, state_ref[q])


def front(layer, head_rows, hidden_at, ints, floats, hidden, weight, inner_kernel, proj_kernel,
          norm_gain, inner_cache, proj_cache, state):
    layers, requests, heads, head_size, state_size = state.shape
    width = heads * head_size
    tokens = requests * S
    smem = pl.BlockSpec(memory_space=pltpu.SMEM)

    def whole(shape):
        return pl.BlockSpec(shape, lambda i: (0,) * len(shape))

    def layer_of(shape):
        return pl.BlockSpec((None,) + shape[1:], lambda i: (layer,) + (0,) * (len(shape) - 1))

    block_tokens = tokens // 2
    out_shapes = [
        ((COLS, head_rows + SEND_CAP * 2 * S + block_tokens + SUM_ROWS, width), BF),
        ((tokens, width), F32),
        ((tokens, state_size), F32),
        ((tokens, heads * 128), F32),
    ]
    return pl.pallas_call(
        lambda *refs: front_body(layer, head_rows, *refs),
        name="front%d" % layer,
        grid=(1,),
        in_specs=[
            smem, smem,
            pl.BlockSpec((COLS, block_tokens, hidden.shape[2]), lambda i: (0, hidden_at, 0)),
            whole(weight.shape),
            layer_of(inner_kernel.shape),
            layer_of(proj_kernel.shape),
            whole(norm_gain.shape),
            layer_of(inner_cache.shape),
            layer_of(proj_cache.shape),
            layer_of(state.shape),
        ],
        out_specs=[whole(shape) for shape, _ in out_shapes],
        out_shape=[jax.ShapeDtypeStruct(shape, kind) for shape, kind in out_shapes],
        scratch_shapes=[
            pltpu.VMEM((requests, 24, width), F32),
            pltpu.VMEM((requests, 24, 2 * state_size), F32),
        ],
        compiler_params=pltpu.CompilerParams(
            dimension_semantics=("arbitrary",), vmem_limit_bytes=40 * 1024 * 1024
        ),
    )(ints, floats, hidden, weight, inner_kernel, proj_kernel, norm_gain,
      inner_cache, proj_cache, state)


def states_body(dx_ref, b_ref, dec_ref, state_ref, *rest):
    steps_ref = rest[-1]
    heads, head_size, state_size = state_ref.shape
    dx_t = dx_ref[...].T
    for h in range(heads):
        state = state_ref[h]
        columns = dx_t[h * head_size : (h + 1) * head_size, :]
        for t in range(S):
            state = (
                state * dec_ref[t : t + 1, h * 128 : (h + 1) * 128]
                + columns[:, t : t + 1] * b_ref[t : t + 1, :]
            )
            steps_ref[t, h] = state.astype(BF)


def states(layer, dx, b, dec, state, previous):
    layers, requests, heads, head_size, state_size = state.shape
    width = heads * head_size
    in_specs = [
        pl.BlockSpec((S, width), lambda q: (q, 0)),
        pl.BlockSpec((S, state_size), lambda q: (q, 0)),
        pl.BlockSpec((S, heads * 128), lambda q: (q, 0)),
        pl.BlockSpec((None, None, heads, head_size, state_size), lambda q: (layer, q, 0, 0, 0)),
    ]
    operands = [dx, b, dec, state]
    aliases = {}
    if previous is not None:
        in_specs.append(pl.BlockSpec(memory_space=pl.ANY))
        aliases = {len(operands): 0}
        operands.append(previous)
    return pl.pallas_call(
        states_body,
        name="states%d" % layer,
        grid=(requests,),
        in_specs=in_specs,
        out_specs=pl.BlockSpec(
            (None, None, S, heads, head_size, state_size), lambda q: (layer, q, 0, 0, 0, 0)
        ),
        out_shape=jax.ShapeDtypeStruct(
            (layers, requests, S, heads, head_size, state_size), BF
        ),
        input_output_aliases=aliases,
        compiler_params=pltpu.CompilerParams(
            dimension_semantics=("arbitrary",), vmem_limit_bytes=24 * 1024 * 1024
        ),
    )(*operands)


def starts_body(ints_ref, state_ref, hidden_ref, send_ref):
    rows = send_ref.shape[1] - hidden_ref.shape[0]
    send_ref[:, :rows, :] = jnp.zeros((COLS, rows, send_ref.shape[2]), BF)
    hidden = hidden_ref[...]
    for c in range(COLS):
        send_ref[c, rows:, :] = hidden
    requests = state_ref.shape[0]
    for q in range(requests):
        live, owner, rank = route(q, ints_ref, requests)

        @pl.when(live)
        def _put():
            put_start(send_ref, owner, rank, state_ref[q])


def starts(layer, head_rows, ints, state, hidden):
    shape = (COLS, head_rows + hidden.shape[0], hidden.shape[1])
    return pl.pallas_call(
        starts_body,
        name="starts",
        grid=(1,),
        in_specs=[
            pl.BlockSpec(memory_space=pltpu.SMEM),
            pl.BlockSpec((None,) + state.shape[1:], lambda i: (layer, 0, 0, 0, 0)),
            pl.BlockSpec(hidden.shape, lambda i: (0, 0)),
        ],
        out_specs=pl.BlockSpec(shape, lambda i: (0, 0, 0)),
        out_shape=jax.ShapeDtypeStruct(shape, BF),
        compiler_params=pltpu.CompilerParams(
            dimension_semantics=("arbitrary",), vmem_limit_bytes=24 * 1024 * 1024
        ),
    )(ints, state, hidden)


def owned_body(starts_ref, factors_ref, *rest):
    out_ref = rest[-1]
    group = starts_ref.shape[0]
    slots, group_heads, head_size, state_size = out_ref.shape
    heads = group_heads // group
    span = heads // 2 * head_size
    for g in range(group):
        for slot in range(slots):
            row = slot * 2 * S
            dx = factors_ref[g, row : row + S, :]
            other = factors_ref[g, row + S : row + 2 * S, :]
            added = lax.dot_general(
                dx, other[:, :state_size], (((0,), (0,)), ((), ())), preferred_element_type=F32
            )
            tail = other[:, state_size:].astype(F32)
            for h in range(heads):
                k, half = h // 2, h % 2
                lane = half * 64
                scale = tail[k : k + 1, lane : lane + 1] + tail[k + 2 : k + 3, lane : lane + 1]
                at = slot * span + k * head_size
                begun = starts_ref[
                    g, at : at + head_size, half * state_size : (half + 1) * state_size
                ]
                out_ref[slot, g * heads + h] = (
                    begun.astype(F32) * scale + added[h * head_size : (h + 1) * head_size, :]
                ).astype(BF)


def owned_states(layer, state, head_rows, begun, factors, factors_at, previous):
    layers, _, heads, head_size, state_size = state.shape
    group = 4
    in_specs = [
        pl.BlockSpec((group, head_rows, begun.shape[2]), lambda i: (i, 0, 0)),
        pl.BlockSpec((group, SEND_CAP * 2 * S, begun.shape[2]), lambda i: (i, factors_at, 0)),
    ]
    operands = [begun, factors]
    aliases = {}
    if previous is not None:
        in_specs.append(pl.BlockSpec(memory_space=pl.ANY))
        aliases = {len(operands): 0}
        operands.append(previous)
    return pl.pallas_call(
        owned_body,
        name="owned%d" % layer,
        grid=(COLS // group,),
        in_specs=in_specs,
        out_specs=pl.BlockSpec(
            (SEND_CAP, None, group * heads, head_size, state_size),
            lambda i: (0, layer, i, 0, 0),
        ),
        out_shape=jax.ShapeDtypeStruct(
            (SEND_CAP, layers, COLS * heads, head_size, state_size), BF
        ),
        input_output_aliases=aliases,
        compiler_params=pltpu.CompilerParams(
            dimension_semantics=("arbitrary",), vmem_limit_bytes=16 * 1024 * 1024
        ),
    )(*operands)


def update_body(inner_width, part_ref, sums_ref, hidden_ref, out_ref):
    rows = hidden_ref.shape[0]
    total = part_ref[0].astype(F32)
    sums = sums_ref[0, :, 0:128].astype(F32)
    for c in range(1, COLS):
        total = total + part_ref[c].astype(F32)
        sums = sums + sums_ref[c, :, 0:128].astype(F32)
    scale = lax.rsqrt(sums.T[:rows, 0:1] / inner_width + EPSILON)
    fresh = (hidden_ref[...].astype(F32) + total * scale).astype(BF)
    if len(out_ref.shape) == 3:
        for c in range(COLS):
            out_ref[c] = fresh
    else:
        out_ref[...] = fresh


def update(inner_width, head_rows, received, hidden, spread):
    rows, lanes = hidden.shape
    shape = ((COLS,) if spread else ()) + hidden.shape
    part_at = (head_rows + SEND_CAP * 2 * S) // rows
    sums_at = (head_rows + SEND_CAP * 2 * S + rows) // SUM_ROWS
    return pl.pallas_call(
        lambda *refs: update_body(inner_width, *refs),
        name="update_spread" if spread else "update_last",
        grid=(1,),
        in_specs=[
            pl.BlockSpec((COLS, rows, lanes), lambda i: (0, part_at, 0)),
            pl.BlockSpec((COLS, SUM_ROWS, lanes), lambda i: (0, sums_at, 0)),
            pl.BlockSpec(hidden.shape, lambda i: (0, 0)),
        ],
        out_specs=pl.BlockSpec(shape, lambda i: (0,) * len(shape)),
        out_shape=jax.ShapeDtypeStruct(shape, BF),
    )(received, received, hidden)


def swap(x):
    return lax.all_to_all(x, "col", 0, 0, tiled=True)


def local(
    hidden_states,
    input_gain,
    inner_weight,
    proj_weight,
    step_weight,
    inner_kernel,
    proj_kernel,
    step_bias,
    decay_log,
    skip_gain,
    norm_gain,
    out_weight,
    inner_cache,
    proj_cache,
    state_cache,
    accepted,
    owners,
    tenant_ranges,
):
    layer_count = inner_weight.shape[0]
    row_width = inner_weight.shape[1]
    inner_local = inner_weight.shape[3]
    heads_local = step_weight.shape[2]
    requests_local = state_cache.shape[1]
    inner_width = inner_local * COLS
    base = (lax.axis_index("row") * requests_local).astype(jnp.int32).reshape(1)
    ints = jnp.concatenate([base, accepted, owners, tenant_ranges.reshape(-1)])
    floats = jnp.concatenate([step_bias, decay_log, skip_gain], axis=1)

    there = []
    for r in range(ROWS):
        for c in range(COLS):
            there.append((r * COLS + c, (c // 2) * COLS + (c % 2) * ROWS + r))
    back = [(b, a) for a, b in there]

    def packed(layer, inner, proj, step, gain, out):
        joined = jnp.concatenate(
            [
                inner[layer].reshape(row_width, 2 * inner_local),
                proj[layer],
                jnp.pad(step[layer], ((0, 0), (0, 128 - heads_local))),
            ],
            axis=1,
        )
        scaled = (joined.astype(F32) * gain[layer][:, None]).astype(BF)
        return jnp.concatenate([scaled, out[layer]], axis=1)

    raw = (inner_weight, proj_weight, step_weight, input_gain, out_weight)
    weights = [lax.all_gather(packed(0, *raw), "row", axis=0)]
    block = lax.ppermute(hidden_states, ("row", "col"), there)
    head_size, state_size = state_cache.shape[3:]
    start_rows = SEND_CAP * heads_local * head_size * state_size // block.shape[1]
    begun = swap(starts(0, start_rows, ints, state_cache, block))
    later = lax.optimization_barrier(raw + (block,))
    weights.append(lax.all_gather(packed(1, *later[:-1]), "row", axis=0))

    everything = begun
    hidden_at = start_rows // block.shape[0]
    steps = None
    owned = None
    for layer in range(layer_count):
        last = layer == layer_count - 1
        head_rows = start_rows if last else 0
        part, dx, b_conv, decay = front(
            layer, head_rows, hidden_at, ints, floats, everything, weights[layer], inner_kernel,
            proj_kernel, norm_gain, inner_cache, proj_cache, state_cache,
        )
        received = swap(part)
        steps = states(layer, dx, b_conv, decay, state_cache, steps)
        if last:
            received, steps, owned = lax.optimization_barrier((received, steps, owned))
            begun = received
        else:
            received, steps = lax.optimization_barrier((received, steps))
        fresh = update(inner_width, head_rows, received, block, not last)
        owned = owned_states(
            layer, state_cache, start_rows, begun, received, head_rows // (SEND_CAP * 2 * S), owned
        )
        if not last:
            block = fresh[0]
            everything = swap(fresh)
            hidden_at = 0
    hidden = lax.ppermute(fresh, ("row", "col"), back)
    owned_block = owned[None, None]
    return (hidden, steps, owned_block)


def solution(mesh):
    placed = (
        P("col", "row"),
        P(None, "row"),
        P(None, "row", None, "col"),
        P(None, "row", None),
        P(None, "row", "col"),
        P(None, None, "col"),
        P(),
        P(None, "col"),
        P(None, "col"),
        P(None, "col"),
        P(None, "col"),
        P(None, "col", "row"),
        P(None, "row", None, "col"),
        P(None, "row", None, None),
        P(None, "row", "col", None, None),
        P("row"),
        P("row"),
        P(),
    )
    return jax.shard_map(
        local,
        mesh=mesh,
        in_specs=placed,
        out_specs=(
            P("col", "row"),
            P(None, "row", None, "col", None, None),
            P("row", "col", None, None, None, None, None),
        ),
        check_vma=False,
    )
```

```python
import jax
import jax.numpy as jnp
from jax import lax
from jax.experimental import pallas as pl
from jax.experimental.pallas import tpu as pltpu
from jax.sharding import PartitionSpec as P

S = 16
SEND_CAP = 2
EPSILON = 1e-05
ROWS = 8
COLS = 16
BF = jnp.bfloat16
F32 = jnp.float32
SUM_ROWS = 16
VMEM_BYTES = 58 * 1024 * 1024


def silu(v):
    return v / (1.0 + jnp.exp(-v))


def softplus(v):
    return jnp.maximum(v, 0.0) + jnp.log1p(jnp.exp(-jnp.abs(v)))


def route(q, ints_ref, requests):
    owners, ranges = 2 + requests, 2 + 2 * requests
    request = ints_ref[0] + q
    live = (request >= ints_ref[ranges]) & (request < ints_ref[ranges + 1])
    for k in range(ranges + 2, ints_ref.shape[0], 2):
        live = live | ((request >= ints_ref[k]) & (request < ints_ref[k + 1]))
    owner = ints_ref[owners + q]
    rank = jnp.int32(0)
    for other in range(q):
        rank = rank + jnp.where(ints_ref[owners + other] == owner, 1, 0)
    return live, owner, jnp.minimum(rank, SEND_CAP - 1)


def front_body(
    layer,
    ints_ref,
    floats_ref,
    hidden_ref,
    weight_ref,
    inner_kernel_ref,
    proj_kernel_ref,
    norm_gain_ref,
    inner_cache_ref,
    proj_cache_ref,
    state_ref,
    part_ref,
    dx_ref,
    b_ref,
    dec_ref,
    x_pad,
    p_pad,
    misc_ref,
):
    requests, heads, head_size, state_size = state_ref.shape
    tokens = requests * S
    width = heads * head_size
    model_width = ROWS * hidden_ref.shape[2]
    block_tokens = hidden_ref.shape[1]
    in_cols = 2 * width + 2 * state_size + 128
    lane = lax.broadcasted_iota(jnp.int32, (1, 128), 1)

    def spread(pieces):
        return jnp.concatenate(
            [jnp.where(lane < 64, pieces[2 * k], pieces[2 * k + 1]) for k in range(heads // 2)],
            axis=1,
        )

    total = jnp.zeros((tokens, in_cols), F32)
    squares = jnp.zeros((tokens, 128), F32)
    for r in range(ROWS):
        rows_r = jnp.concatenate([hidden_ref[r], hidden_ref[ROWS + r]], axis=0)
        total = total + jnp.dot(rows_r, weight_ref[r, :, :in_cols], preferred_element_type=F32)
        wide = rows_r.astype(F32)
        wide = wide * wide
        squares = squares + wide[:, :128] + wide[:, 128:]
    inverse = lax.rsqrt(jnp.sum(squares, axis=1, keepdims=True) / model_width + EPSILON)
    total = total * inverse
    z = total[:, :width]
    x_pad[:, 8:24, :] = total[:, width : 2 * width].reshape(requests, S, width)
    p_pad[:, 8:24, :] = total[:, 2 * width : 2 * width + 2 * state_size].reshape(
        requests, S, 2 * state_size
    )
    x_pad[:, 5:8, :] = inner_cache_ref[...].astype(F32)
    p_pad[:, 5:8, :] = proj_cache_ref[...].astype(F32)
    conv_x = x_pad[:, 5 : 5 + S, :] * inner_kernel_ref[0:1, :]
    conv_p = p_pad[:, 5 : 5 + S, :] * proj_kernel_ref[0:1, :]
    for i in range(1, 4):
        conv_x = conv_x + x_pad[:, 5 + i : 5 + i + S, :] * inner_kernel_ref[i : i + 1, :]
        conv_p = conv_p + p_pad[:, 5 + i : 5 + i + S, :] * proj_kernel_ref[i : i + 1, :]
    x_conv = silu(conv_x).reshape(tokens, width)
    p_conv = silu(conv_p).reshape(tokens, 2 * state_size)
    b_conv = p_conv[:, :state_size]
    c_conv = p_conv[:, state_size:].astype(BF)
    b_ref[...] = b_conv
    step_raw = total[:, 2 * width + 2 * state_size :]
    t_now = lax.broadcasted_iota(jnp.int32, (tokens, tokens), 0)
    t_then = lax.broadcasted_iota(jnp.int32, (tokens, tokens), 1)
    causal = (t_now // S == t_then // S) & (t_then <= t_now)
    lower = causal.astype(F32)
    scores = lax.dot_general(
        c_conv, b_conv.astype(BF), (((1,), (1,)), ((), ())), preferred_element_type=F32
    )
    deltas = []
    sums_log = []
    mixes = []
    for h in range(heads):
        raw = jnp.broadcast_to(step_raw[:, h : h + 1], (tokens, 128))
        delta = softplus(raw + floats_ref[layer, h])
        rate = jnp.exp(jnp.full((1, 128), floats_ref[layer, heads + h], F32))
        log_decay = -delta * rate
        dec_ref[:, h * 128 : (h + 1) * 128] = jnp.exp(log_decay)
        cum = jnp.dot(
            lower, log_decay, precision=lax.Precision.HIGHEST, preferred_element_type=F32
        )
        gap = jnp.where(causal, cum - cum.T, 0.0)
        mixes.append((jnp.where(causal, jnp.exp(gap), 0.0) * scores).astype(BF))
        deltas.append(delta)
        sums_log.append(cum)
    dx = x_conv * spread(deltas)
    cum_all = spread(sums_log)
    grown = jnp.exp(cum_all)
    dx_ref[...] = dx
    y_diag = []
    for k in range(heads // 2):
        dx_k = dx[:, 128 * k : 128 * (k + 1)].astype(BF)
        first = jnp.dot(mixes[2 * k], dx_k, preferred_element_type=F32)
        second = jnp.dot(mixes[2 * k + 1], dx_k, preferred_element_type=F32)
        y_diag.append(jnp.where(lane < 64, first, second))
    y_off = []
    for q in range(requests):
        flat = state_ref[q].reshape(width, state_size).astype(BF)
        y_off.append(
            lax.dot_general(
                c_conv[q * S : (q + 1) * S, :], flat, (((1,), (1,)), ((), ())),
                preferred_element_type=F32,
            )
        )
    skip = spread([jnp.full((1, 128), floats_ref[layer, 2 * heads + h], F32) for h in range(heads)])
    y = (
        jnp.concatenate(y_diag, axis=1)
        + grown * jnp.concatenate(y_off, axis=0)
        + skip * x_conv
    )
    g = y * silu(z)
    yg = (g * norm_gain_ref[layer : layer + 1, :]).astype(BF)
    g2 = (g * g).astype(BF)
    ones = jnp.ones((SUM_ROWS, width), BF)
    misc_row = block_tokens + SEND_CAP * S
    line = lax.broadcasted_iota(jnp.int32, (SUM_ROWS, 1), 0)
    part_ref[:, block_tokens:misc_row, :] = jnp.zeros((COLS, SEND_CAP * S, width), BF)
    nothing = jnp.zeros((SUM_ROWS, width - block_tokens), F32)
    for b in range(2):
        sums = lax.dot_general(
            ones,
            g2[b * block_tokens : (b + 1) * block_tokens, :],
            (((1,), (1,)), ((), ())),
            preferred_element_type=F32,
        )
        sums = jnp.where(line == 0, jnp.concatenate([sums, nothing], axis=1), 0.0)
        for r in range(ROWS):
            misc_ref[b * ROWS + r] = sums
    step = lax.broadcasted_iota(jnp.int32, (S, 1), 0)
    column = ints_ref[1]
    for q in range(requests):
        live, owner, rank = route(q, ints_ref, requests)
        taken = ints_ref[2 + q] - 1
        rows = slice(q * S, (q + 1) * S)
        cum_q = cum_all[rows, :]
        cum_end = jnp.sum(jnp.where(step == taken, cum_q, 0.0), axis=0, keepdims=True)
        inside = step <= taken
        weight = jnp.where(inside, jnp.exp(jnp.where(inside, cum_end - cum_q, 0.0)), 0.0)
        scale = jnp.exp(cum_end)
        high = scale.astype(BF).astype(F32)
        low = scale - high
        mine = jnp.sum(jnp.where(step == column, b_conv[rows, :], 0.0), axis=0, keepdims=True)
        mine = jnp.concatenate([mine, jnp.zeros((1, width - state_size), F32)], axis=1)
        at = 1 + 3 * rank
        extra = jnp.where(
            line == at,
            mine,
            jnp.where(line == at + 1, high, jnp.where(line == at + 2, low, 0.0)),
        )
        first = pl.multiple_of(block_tokens + rank * S, S)

        @pl.when(live)
        def _send():
            part_ref[owner, pl.ds(first, S), :] = (dx[rows, :] * weight).astype(BF)
            misc_ref[owner] = misc_ref[owner] + extra

    part_ref[:, misc_row:, :] = misc_ref[...].astype(BF)
    for r in range(ROWS):
        part = jnp.dot(yg, weight_ref[r, :, in_cols:], preferred_element_type=F32).astype(BF)
        for b in range(2):
            part_ref[b * ROWS + r, 0:block_tokens, :] = part[
                b * block_tokens : (b + 1) * block_tokens, :
            ]


def front(layer, ints, floats, hidden, weight, inner_kernel, proj_kernel,
          norm_gain, inner_cache, proj_cache, state):
    layers, requests, heads, head_size, state_size = state.shape
    width = heads * head_size
    tokens = requests * S
    smem = pl.BlockSpec(memory_space=pltpu.SMEM)

    def whole(shape):
        return pl.BlockSpec(shape, lambda i: (0,) * len(shape))

    def layer_of(shape):
        return pl.BlockSpec((None,) + shape[1:], lambda i: (layer,) + (0,) * (len(shape) - 1))

    block_tokens = tokens // 2
    out_shapes = [
        ((COLS, block_tokens + SEND_CAP * S + SUM_ROWS, width), BF),
        ((tokens, width), F32),
        ((tokens, state_size), F32),
        ((tokens, heads * 128), F32),
    ]
    return pl.pallas_call(
        lambda *refs: front_body(layer, *refs),
        name="front%d" % layer,
        grid=(1,),
        in_specs=[
            smem, smem,
            whole(hidden.shape),
            whole(weight.shape),
            layer_of(inner_kernel.shape),
            layer_of(proj_kernel.shape),
            whole(norm_gain.shape),
            layer_of(inner_cache.shape),
            layer_of(proj_cache.shape),
            layer_of(state.shape),
        ],
        out_specs=[whole(shape) for shape, _ in out_shapes],
        out_shape=[jax.ShapeDtypeStruct(shape, kind) for shape, kind in out_shapes],
        scratch_shapes=[
            pltpu.VMEM((requests, 24, width), F32),
            pltpu.VMEM((requests, 24, 2 * state_size), F32),
            pltpu.VMEM((COLS, SUM_ROWS, width), F32),
        ],
        compiler_params=pltpu.CompilerParams(
            dimension_semantics=("arbitrary",), vmem_limit_bytes=VMEM_BYTES
        ),
    )(ints, floats, hidden, weight, inner_kernel, proj_kernel, norm_gain,
      inner_cache, proj_cache, state)


def states_body(dx_ref, b_ref, dec_ref, state_ref, *rest):
    steps_ref = rest[-1]
    heads, head_size, state_size = state_ref.shape
    dx_t = dx_ref[...].T
    for h in range(heads):
        state = state_ref[h]
        columns = dx_t[h * head_size : (h + 1) * head_size, :]
        for t in range(S):
            state = (
                state * dec_ref[t : t + 1, h * 128 : (h + 1) * 128]
                + columns[:, t : t + 1] * b_ref[t : t + 1, :]
            )
            steps_ref[t, h] = state.astype(BF)


def states(layer, dx, b, dec, state, previous):
    layers, requests, heads, head_size, state_size = state.shape
    width = heads * head_size
    in_specs = [
        pl.BlockSpec((S, width), lambda q: (q, 0)),
        pl.BlockSpec((S, state_size), lambda q: (q, 0)),
        pl.BlockSpec((S, heads * 128), lambda q: (q, 0)),
        pl.BlockSpec((None, None, heads, head_size, state_size), lambda q: (layer, q, 0, 0, 0)),
    ]
    operands = [dx, b, dec, state]
    aliases = {}
    if previous is not None:
        in_specs.append(pl.BlockSpec(memory_space=pl.ANY))
        aliases = {len(operands): 0}
        operands.append(previous)
    return pl.pallas_call(
        states_body,
        name="states%d" % layer,
        grid=(requests,),
        in_specs=in_specs,
        out_specs=pl.BlockSpec(
            (None, None, S, heads, head_size, state_size), lambda q: (layer, q, 0, 0, 0, 0)
        ),
        out_shape=jax.ShapeDtypeStruct(
            (layers, requests, S, heads, head_size, state_size), BF
        ),
        input_output_aliases=aliases,
        compiler_params=pltpu.CompilerParams(
            dimension_semantics=("arbitrary",), vmem_limit_bytes=VMEM_BYTES
        ),
    )(*operands)


def starts_body(ints_ref, state_ref, send_ref):
    send_ref[...] = jnp.zeros(send_ref.shape, BF)
    requests = state_ref.shape[0]
    for q in range(requests):
        live, owner, rank = route(q, ints_ref, requests)

        @pl.when(live)
        def _put():
            send_ref[owner, rank] = state_ref[q].astype(BF)


def starts(layer, ints, state):
    shape = (COLS, SEND_CAP) + state.shape[2:]
    return pl.pallas_call(
        starts_body,
        name="starts%d" % layer,
        grid=(1,),
        in_specs=[
            pl.BlockSpec(memory_space=pltpu.SMEM),
            pl.BlockSpec((None,) + state.shape[1:], lambda i: (layer, 0, 0, 0, 0)),
        ],
        out_specs=pl.BlockSpec(shape, lambda i: (0, 0, 0, 0, 0)),
        out_shape=jax.ShapeDtypeStruct(shape, BF),
        compiler_params=pltpu.CompilerParams(
            dimension_semantics=("arbitrary",), vmem_limit_bytes=VMEM_BYTES
        ),
    )(ints, state)


def owned_body(starts_ref, dx_ref, misc_ref, *rest):
    out_ref = rest[-1]
    i = pl.program_id(0)
    group = starts_ref.shape[0]
    slots, group_heads, head_size, state_size = out_ref.shape
    heads = group_heads // group
    for slot in range(slots):
        row = 1 + 3 * slot
        b_all = misc_ref[:, row, 0:state_size]
        for g in range(group):
            dx = dx_ref[g, slot * S : (slot + 1) * S, :]
            added = lax.dot_general(
                dx, b_all, (((0,), (0,)), ((), ())), preferred_element_type=F32
            )
            scales = misc_ref[i * group + g, row + 1 : row + 3, :].astype(F32)
            scales = scales[0:1, :] + scales[1:2, :]
            for h in range(heads):
                scale = scales[:, h * head_size : h * head_size + 1]
                out_ref[slot, g * heads + h] = (
                    starts_ref[g, slot, h].astype(F32) * scale
                    + added[h * head_size : (h + 1) * head_size, :]
                ).astype(BF)


def owned_states(layer, state, begun, received, previous):
    layers, _, heads, head_size, state_size = state.shape
    group = 4
    width = received.shape[2]
    dx_rows = SEND_CAP * S
    block_tokens = received.shape[1] - dx_rows - SUM_ROWS
    dx_at = block_tokens // dx_rows
    misc_at = (block_tokens + dx_rows) // SUM_ROWS
    in_specs = [
        pl.BlockSpec((group,) + begun.shape[1:], lambda i: (i, 0, 0, 0, 0)),
        pl.BlockSpec((group, dx_rows, width), lambda i: (i, dx_at, 0)),
        pl.BlockSpec((COLS, SUM_ROWS, width), lambda i: (0, misc_at, 0)),
    ]
    operands = [begun, received, received]
    aliases = {}
    if previous is not None:
        in_specs.append(pl.BlockSpec(memory_space=pl.ANY))
        aliases = {len(operands): 0}
        operands.append(previous)
    return pl.pallas_call(
        owned_body,
        name="owned%d" % layer,
        grid=(COLS // group,),
        in_specs=in_specs,
        out_specs=pl.BlockSpec(
            (SEND_CAP, None, group * heads, head_size, state_size),
            lambda i: (0, layer, i, 0, 0),
        ),
        out_shape=jax.ShapeDtypeStruct(
            (SEND_CAP, layers, COLS * heads, head_size, state_size), BF
        ),
        input_output_aliases=aliases,
        compiler_params=pltpu.CompilerParams(
            dimension_semantics=("arbitrary",), vmem_limit_bytes=VMEM_BYTES
        ),
    )(*operands)


def update_body(inner_width, part_ref, sums_ref, hidden_ref, *outs):
    rows = hidden_ref.shape[0]
    total = part_ref[0].astype(F32)
    sums = sums_ref[0, :, 0:128].astype(F32)
    for c in range(1, COLS):
        total = total + part_ref[c].astype(F32)
        sums = sums + sums_ref[c, :, 0:128].astype(F32)
    scale = lax.rsqrt(sums.T[:rows, 0:1] / inner_width + EPSILON)
    fresh = (hidden_ref[...].astype(F32) + total * scale).astype(BF)
    outs[0][...] = fresh
    for spread_ref in outs[1:]:
        for c in range(COLS):
            spread_ref[c] = fresh


def update(inner_width, received, hidden, spread):
    rows, lanes = hidden.shape
    shapes = [hidden.shape] + ([(COLS,) + hidden.shape] if spread else [])
    sums_at = (rows + SEND_CAP * S) // SUM_ROWS

    def whole(shape):
        return pl.BlockSpec(shape, lambda i: (0,) * len(shape))

    return pl.pallas_call(
        lambda *refs: update_body(inner_width, *refs),
        name="update_spread" if spread else "update_last",
        grid=(1,),
        in_specs=[
            pl.BlockSpec((COLS, rows, lanes), lambda i: (0, 0, 0)),
            pl.BlockSpec((COLS, SUM_ROWS, lanes), lambda i: (0, sums_at, 0)),
            whole(hidden.shape),
        ],
        out_specs=[whole(shape) for shape in shapes],
        out_shape=[jax.ShapeDtypeStruct(shape, BF) for shape in shapes],
        compiler_params=pltpu.CompilerParams(
            dimension_semantics=("arbitrary",), vmem_limit_bytes=VMEM_BYTES
        ),
    )(received, received, hidden)


def swap(x):
    return lax.all_to_all(x, "col", 0, 0, tiled=True)


def local(
    hidden_states,
    input_gain,
    inner_weight,
    proj_weight,
    step_weight,
    inner_kernel,
    proj_kernel,
    step_bias,
    decay_log,
    skip_gain,
    norm_gain,
    out_weight,
    inner_cache,
    proj_cache,
    state_cache,
    accepted,
    owners,
    tenant_ranges,
):
    layer_count = inner_weight.shape[0]
    row_width = inner_weight.shape[1]
    inner_local = inner_weight.shape[3]
    heads_local = step_weight.shape[2]
    requests_local = state_cache.shape[1]
    inner_width = inner_local * COLS
    base = (lax.axis_index("row") * requests_local).astype(jnp.int32).reshape(1)
    column = lax.axis_index("col").astype(jnp.int32).reshape(1)
    ints = jnp.concatenate([base, column, accepted, owners, tenant_ranges.reshape(-1)])
    floats = jnp.concatenate([step_bias, decay_log, skip_gain], axis=1)

    there = []
    for r in range(ROWS):
        for c in range(COLS):
            there.append((r * COLS + c, (c // 2) * COLS + (c % 2) * ROWS + r))
    back = [(b, a) for a, b in there]

    def packed(layer, inner, proj, step, gain, out):
        joined = jnp.concatenate(
            [
                inner[layer].reshape(row_width, 2 * inner_local),
                proj[layer],
                jnp.pad(step[layer], ((0, 0), (0, 128 - heads_local))),
            ],
            axis=1,
        )
        scaled = (joined.astype(F32) * gain[layer][:, None]).astype(BF)
        return jnp.concatenate([scaled, out[layer]], axis=1)

    block = lax.ppermute(hidden_states, ("row", "col"), there)
    raw = (inner_weight, proj_weight, step_weight, input_gain, out_weight)
    first, block = lax.optimization_barrier((packed(0, *raw), block))
    weights = [lax.all_gather(first, "row", axis=0)]
    everything = swap(jnp.broadcast_to(block[None], (COLS,) + block.shape))
    sends = [starts(layer, ints, state_cache) for layer in range(layer_count)]
    everything, sends, raw = lax.optimization_barrier((everything, sends, raw))
    weights.append(lax.all_gather(packed(1, *raw), "row", axis=0))
    begun = swap(sends[0])
    send = sends[1]

    steps = None
    owned = None
    for layer in range(layer_count):
        last = layer == layer_count - 1
        part, dx, b_conv, decay = front(
            layer, ints, floats, everything, weights[layer], inner_kernel, proj_kernel,
            norm_gain, inner_cache, proj_cache, state_cache,
        )
        part, begun, owned = lax.optimization_barrier((part, begun, owned))
        received = swap(part)
        steps = states(layer, dx, b_conv, decay, state_cache, steps)
        received, steps = lax.optimization_barrier((received, steps))
        fresh = update(inner_width, received, block, not last)
        owned = owned_states(layer, state_cache, begun, received, owned)
        if not last:
            block = fresh[0]
            everything, send = lax.optimization_barrier((swap(fresh[1]), send))
            begun = swap(send)
    hidden = lax.ppermute(fresh[0], ("row", "col"), back)
    owned_block = owned[None, None]
    return (hidden, steps, owned_block)


def solution(mesh):
    placed = (
        P("col", "row"),
        P(None, "row"),
        P(None, "row", None, "col"),
        P(None, "row", None),
        P(None, "row", "col"),
        P(None, None, "col"),
        P(),
        P(None, "col"),
        P(None, "col"),
        P(None, "col"),
        P(None, "col"),
        P(None, "col", "row"),
        P(None, "row", None, "col"),
        P(None, "row", None, None),
        P(None, "row", "col", None, None),
        P("row"),
        P("row"),
        P(),
    )
    return jax.shard_map(
        local,
        mesh=mesh,
        in_specs=placed,
        out_specs=(
            P("col", "row"),
            P(None, "row", None, "col", None, None),
            P("row", "col", None, None, None, None, None),
        ),
        check_vma=False,
    )
```

```python
import jax
import jax.numpy as jnp
from jax import lax
from jax.experimental import pallas as pl
from jax.experimental.pallas import tpu as pltpu
from jax.sharding import PartitionSpec as P

S = 16
SEND_CAP = 2
EPSILON = 1e-05
ROWS = 8
COLS = 16
BF = jnp.bfloat16
F32 = jnp.float32
SUM_ROWS = 16
VMEM_BYTES = 58 * 1024 * 1024
SMALL_VMEM_BYTES = 12 * 1024 * 1024


def silu(v):
    return v / (1.0 + jnp.exp(-v))


def softplus(v):
    return jnp.maximum(v, 0.0) + jnp.log1p(jnp.exp(-jnp.abs(v)))


def pack_body(layer, inner_ref, proj_ref, step_ref, gain_ref, out_ref, packed_ref):
    rows, width = out_ref.shape
    states = proj_ref.shape[1]
    gain = jnp.broadcast_to(gain_ref[layer : layer + 1, :], (8, rows)).T[:, 0:1]
    step = step_ref[...].astype(F32)
    step = jnp.concatenate([step, jnp.zeros((128 - step.shape[0], rows), F32)], axis=0).T
    at = 0
    for piece in (inner_ref[0], inner_ref[1], proj_ref[...], step):
        end = at + piece.shape[1]
        packed_ref[:, at:end] = (piece.astype(F32) * gain).astype(BF)
        at = end
    packed_ref[:, at:] = out_ref[...]


def pack(layer, inner, proj, step, gain, out):
    rows, width = inner.shape[2:]
    cols = 2 * width + proj.shape[2] + 128 + out.shape[2]

    def layer_of(shape):
        return pl.BlockSpec((None,) + shape[1:], lambda i: (layer,) + (0,) * (len(shape) - 1))

    return pl.pallas_call(
        lambda *refs: pack_body(layer, *refs),
        name="pack%d" % layer,
        grid=(1,),
        in_specs=[
            layer_of(inner.shape),
            layer_of(proj.shape),
            layer_of(step.shape),
            pl.BlockSpec(gain.shape, lambda i: (0, 0)),
            layer_of(out.shape),
        ],
        out_specs=pl.BlockSpec((rows, cols), lambda i: (0, 0)),
        out_shape=jax.ShapeDtypeStruct((rows, cols), BF),
        compiler_params=pltpu.CompilerParams(
            dimension_semantics=("arbitrary",), vmem_limit_bytes=VMEM_BYTES
        ),
    )(inner, proj, step, gain, out)


def route(q, ints_ref, requests):
    owners, ranges = 2 + requests, 2 + 2 * requests
    request = ints_ref[0] + q
    live = (request >= ints_ref[ranges]) & (request < ints_ref[ranges + 1])
    for k in range(ranges + 2, ints_ref.shape[0], 2):
        live = live | ((request >= ints_ref[k]) & (request < ints_ref[k + 1]))
    owner = ints_ref[owners + q]
    rank = jnp.int32(0)
    for other in range(q):
        rank = rank + jnp.where(ints_ref[owners + other] == owner, 1, 0)
    return live, owner, jnp.minimum(rank, SEND_CAP - 1)


def front_body(
    layer,
    ints_ref,
    floats_ref,
    hidden_ref,
    weight_ref,
    inner_kernel_ref,
    proj_kernel_ref,
    norm_gain_ref,
    inner_cache_ref,
    proj_cache_ref,
    state_ref,
    part_ref,
    dx_ref,
    b_ref,
    dec_ref,
    x_pad,
    p_pad,
    misc_ref,
):
    requests, heads, head_size, state_size = state_ref.shape
    tokens = requests * S
    width = heads * head_size
    model_width = ROWS * hidden_ref.shape[2]
    block_tokens = hidden_ref.shape[1]
    in_cols = 2 * width + 2 * state_size + 128
    lane = lax.broadcasted_iota(jnp.int32, (1, 128), 1)

    def spread(pieces):
        return jnp.concatenate(
            [jnp.where(lane < 64, pieces[2 * k], pieces[2 * k + 1]) for k in range(heads // 2)],
            axis=1,
        )

    total = jnp.zeros((tokens, in_cols), F32)
    squares = jnp.zeros((tokens, 128), F32)
    for r in range(ROWS):
        rows_r = jnp.concatenate([hidden_ref[r], hidden_ref[ROWS + r]], axis=0)
        total = total + jnp.dot(rows_r, weight_ref[r, :, :in_cols], preferred_element_type=F32)
        wide = rows_r.astype(F32)
        wide = wide * wide
        squares = squares + wide[:, :128] + wide[:, 128:]
    inverse = lax.rsqrt(jnp.sum(squares, axis=1, keepdims=True) / model_width + EPSILON)
    total = total * inverse
    z = total[:, :width]
    x_pad[:, 8:24, :] = total[:, width : 2 * width].reshape(requests, S, width)
    p_pad[:, 8:24, :] = total[:, 2 * width : 2 * width + 2 * state_size].reshape(
        requests, S, 2 * state_size
    )
    x_pad[:, 5:8, :] = inner_cache_ref[...].astype(F32)
    p_pad[:, 5:8, :] = proj_cache_ref[...].astype(F32)
    conv_x = x_pad[:, 5 : 5 + S, :] * inner_kernel_ref[0:1, :]
    conv_p = p_pad[:, 5 : 5 + S, :] * proj_kernel_ref[0:1, :]
    for i in range(1, 4):
        conv_x = conv_x + x_pad[:, 5 + i : 5 + i + S, :] * inner_kernel_ref[i : i + 1, :]
        conv_p = conv_p + p_pad[:, 5 + i : 5 + i + S, :] * proj_kernel_ref[i : i + 1, :]
    x_conv = silu(conv_x).reshape(tokens, width)
    p_conv = silu(conv_p).reshape(tokens, 2 * state_size)
    b_conv = p_conv[:, :state_size]
    c_conv = p_conv[:, state_size:].astype(BF)
    b_ref[...] = b_conv
    step_raw = total[:, 2 * width + 2 * state_size :]
    t_now = lax.broadcasted_iota(jnp.int32, (tokens, tokens), 0)
    t_then = lax.broadcasted_iota(jnp.int32, (tokens, tokens), 1)
    causal = (t_now // S == t_then // S) & (t_then <= t_now)
    lower = causal.astype(F32)
    scores = lax.dot_general(
        c_conv, b_conv.astype(BF), (((1,), (1,)), ((), ())), preferred_element_type=F32
    )
    deltas = []
    sums_log = []
    mixes = []
    for h in range(heads):
        raw = jnp.broadcast_to(step_raw[:, h : h + 1], (tokens, 128))
        delta = softplus(raw + floats_ref[layer, h])
        rate = jnp.exp(jnp.full((1, 128), floats_ref[layer, heads + h], F32))
        log_decay = -delta * rate
        dec_ref[:, h * 128 : (h + 1) * 128] = jnp.exp(log_decay)
        cum = jnp.dot(
            lower, log_decay, precision=lax.Precision.HIGHEST, preferred_element_type=F32
        )
        gap = jnp.where(causal, cum - cum.T, 0.0)
        mixes.append((jnp.where(causal, jnp.exp(gap), 0.0) * scores).astype(BF))
        deltas.append(delta)
        sums_log.append(cum)
    dx = x_conv * spread(deltas)
    cum_all = spread(sums_log)
    grown = jnp.exp(cum_all)
    dx_ref[...] = dx
    y_diag = []
    for k in range(heads // 2):
        dx_k = dx[:, 128 * k : 128 * (k + 1)].astype(BF)
        first = jnp.dot(mixes[2 * k], dx_k, preferred_element_type=F32)
        second = jnp.dot(mixes[2 * k + 1], dx_k, preferred_element_type=F32)
        y_diag.append(jnp.where(lane < 64, first, second))
    y_off = []
    for q in range(requests):
        flat = state_ref[q].reshape(width, state_size).astype(BF)
        y_off.append(
            lax.dot_general(
                c_conv[q * S : (q + 1) * S, :], flat, (((1,), (1,)), ((), ())),
                preferred_element_type=F32,
            )
        )
    skip = spread([jnp.full((1, 128), floats_ref[layer, 2 * heads + h], F32) for h in range(heads)])
    y = (
        jnp.concatenate(y_diag, axis=1)
        + grown * jnp.concatenate(y_off, axis=0)
        + skip * x_conv
    )
    g = y * silu(z)
    yg = (g * norm_gain_ref[layer : layer + 1, :]).astype(BF)
    g2 = (g * g).astype(BF)
    ones = jnp.ones((SUM_ROWS, width), BF)
    misc_row = block_tokens + SEND_CAP * S
    line = lax.broadcasted_iota(jnp.int32, (SUM_ROWS, 1), 0)
    part_ref[:, block_tokens:misc_row, :] = jnp.zeros((COLS, SEND_CAP * S, width), BF)
    nothing = jnp.zeros((SUM_ROWS, width - block_tokens), F32)
    for b in range(2):
        sums = lax.dot_general(
            ones,
            g2[b * block_tokens : (b + 1) * block_tokens, :],
            (((1,), (1,)), ((), ())),
            preferred_element_type=F32,
        )
        sums = jnp.where(line == 0, jnp.concatenate([sums, nothing], axis=1), 0.0)
        for r in range(ROWS):
            misc_ref[b * ROWS + r] = sums
    step = lax.broadcasted_iota(jnp.int32, (S, 1), 0)
    column = ints_ref[1]
    for q in range(requests):
        live, owner, rank = route(q, ints_ref, requests)
        taken = ints_ref[2 + q] - 1
        rows = slice(q * S, (q + 1) * S)
        cum_q = cum_all[rows, :]
        cum_end = jnp.sum(jnp.where(step == taken, cum_q, 0.0), axis=0, keepdims=True)
        inside = step <= taken
        weight = jnp.where(inside, jnp.exp(jnp.where(inside, cum_end - cum_q, 0.0)), 0.0)
        scale = jnp.exp(cum_end)
        high = scale.astype(BF).astype(F32)
        low = scale - high
        mine = jnp.sum(jnp.where(step == column, b_conv[rows, :], 0.0), axis=0, keepdims=True)
        mine = jnp.concatenate([mine, jnp.zeros((1, width - state_size), F32)], axis=1)
        at = 1 + 3 * rank
        extra = jnp.where(
            line == at,
            mine,
            jnp.where(line == at + 1, high, jnp.where(line == at + 2, low, 0.0)),
        )
        first = pl.multiple_of(block_tokens + rank * S, S)

        @pl.when(live)
        def _send():
            part_ref[owner, pl.ds(first, S), :] = (dx[rows, :] * weight).astype(BF)
            misc_ref[owner] = misc_ref[owner] + extra

    part_ref[:, misc_row:, :] = misc_ref[...].astype(BF)
    for r in range(ROWS):
        part = jnp.dot(yg, weight_ref[r, :, in_cols:], preferred_element_type=F32).astype(BF)
        for b in range(2):
            part_ref[b * ROWS + r, 0:block_tokens, :] = part[
                b * block_tokens : (b + 1) * block_tokens, :
            ]


def front(layer, ints, floats, hidden, weight, inner_kernel, proj_kernel,
          norm_gain, inner_cache, proj_cache, state):
    layers, requests, heads, head_size, state_size = state.shape
    width = heads * head_size
    tokens = requests * S
    smem = pl.BlockSpec(memory_space=pltpu.SMEM)

    def whole(shape):
        return pl.BlockSpec(shape, lambda i: (0,) * len(shape))

    def layer_of(shape):
        return pl.BlockSpec((None,) + shape[1:], lambda i: (layer,) + (0,) * (len(shape) - 1))

    block_tokens = tokens // 2
    out_shapes = [
        ((COLS, block_tokens + SEND_CAP * S + SUM_ROWS, width), BF),
        ((tokens, width), F32),
        ((tokens, state_size), F32),
        ((tokens, heads * 128), F32),
    ]
    return pl.pallas_call(
        lambda *refs: front_body(layer, *refs),
        name="front%d" % layer,
        grid=(1,),
        in_specs=[
            smem, smem,
            whole(hidden.shape),
            whole(weight.shape),
            layer_of(inner_kernel.shape),
            layer_of(proj_kernel.shape),
            whole(norm_gain.shape),
            layer_of(inner_cache.shape),
            layer_of(proj_cache.shape),
            layer_of(state.shape),
        ],
        out_specs=[whole(shape) for shape, _ in out_shapes],
        out_shape=[jax.ShapeDtypeStruct(shape, kind) for shape, kind in out_shapes],
        scratch_shapes=[
            pltpu.VMEM((requests, 24, width), F32),
            pltpu.VMEM((requests, 24, 2 * state_size), F32),
            pltpu.VMEM((COLS, SUM_ROWS, width), F32),
        ],
        compiler_params=pltpu.CompilerParams(
            dimension_semantics=("arbitrary",), vmem_limit_bytes=VMEM_BYTES
        ),
    )(ints, floats, hidden, weight, inner_kernel, proj_kernel, norm_gain,
      inner_cache, proj_cache, state)


def states_body(dx_ref, b_ref, dec_ref, state_ref, *rest):
    steps_ref = rest[-1]
    heads, head_size, state_size = state_ref.shape
    dx_t = dx_ref[...].T
    for h in range(heads):
        state = state_ref[h]
        columns = dx_t[h * head_size : (h + 1) * head_size, :]
        for t in range(S):
            state = (
                state * dec_ref[t : t + 1, h * 128 : (h + 1) * 128]
                + columns[:, t : t + 1] * b_ref[t : t + 1, :]
            )
            steps_ref[t, h] = state.astype(BF)


def states(layer, dx, b, dec, state, previous):
    layers, requests, heads, head_size, state_size = state.shape
    width = heads * head_size
    in_specs = [
        pl.BlockSpec((S, width), lambda q: (q, 0)),
        pl.BlockSpec((S, state_size), lambda q: (q, 0)),
        pl.BlockSpec((S, heads * 128), lambda q: (q, 0)),
        pl.BlockSpec((None, None, heads, head_size, state_size), lambda q: (layer, q, 0, 0, 0)),
    ]
    operands = [dx, b, dec, state]
    aliases = {}
    if previous is not None:
        in_specs.append(pl.BlockSpec(memory_space=pl.ANY))
        aliases = {len(operands): 0}
        operands.append(previous)
    return pl.pallas_call(
        states_body,
        name="states%d" % layer,
        grid=(requests,),
        in_specs=in_specs,
        out_specs=pl.BlockSpec(
            (None, None, S, heads, head_size, state_size), lambda q: (layer, q, 0, 0, 0, 0)
        ),
        out_shape=jax.ShapeDtypeStruct(
            (layers, requests, S, heads, head_size, state_size), BF
        ),
        input_output_aliases=aliases,
        compiler_params=pltpu.CompilerParams(
            dimension_semantics=("arbitrary",), vmem_limit_bytes=SMALL_VMEM_BYTES
        ),
    )(*operands)


def starts_body(ints_ref, state_ref, send_ref):
    send_ref[...] = jnp.zeros(send_ref.shape, BF)
    requests = state_ref.shape[0]
    for q in range(requests):
        live, owner, rank = route(q, ints_ref, requests)

        @pl.when(live)
        def _put():
            send_ref[owner, rank] = state_ref[q].astype(BF)


def starts(layer, ints, state):
    shape = (COLS, SEND_CAP) + state.shape[2:]
    return pl.pallas_call(
        starts_body,
        name="starts%d" % layer,
        grid=(1,),
        in_specs=[
            pl.BlockSpec(memory_space=pltpu.SMEM),
            pl.BlockSpec((None,) + state.shape[1:], lambda i: (layer, 0, 0, 0, 0)),
        ],
        out_specs=pl.BlockSpec(shape, lambda i: (0, 0, 0, 0, 0)),
        out_shape=jax.ShapeDtypeStruct(shape, BF),
        compiler_params=pltpu.CompilerParams(
            dimension_semantics=("arbitrary",), vmem_limit_bytes=VMEM_BYTES
        ),
    )(ints, state)


def owned_body(starts_ref, dx_ref, misc_ref, *rest):
    out_ref, b_s, scale_s = rest[-3:]
    i = pl.program_id(0)
    group = starts_ref.shape[0]
    slots, group_heads, head_size, state_size = out_ref.shape
    heads = group_heads // group

    @pl.when(i == 0)
    def _first():
        for slot in range(slots):
            row = 1 + 3 * slot
            for c in range(COLS):
                lines = misc_ref[c].astype(F32)
                b_s[slot, c : c + 1, :] = lines[row : row + 1, 0:state_size]
                scale_s[slot, c : c + 1, :] = (
                    lines[row + 1 : row + 2, :] + lines[row + 2 : row + 3, :]
                )

    for slot in range(slots):
        dx = jnp.concatenate(
            [dx_ref[g, slot * S : (slot + 1) * S, :] for g in range(group)], axis=1
        )
        added = lax.dot_general(
            dx, b_s[slot].astype(BF), (((0,), (0,)), ((), ())), preferred_element_type=F32
        )
        for g in range(group):
            scales = scale_s[slot, pl.ds(i * group + g, 1), :]
            for h in range(heads):
                scale = scales[:, h * head_size : h * head_size + 1]
                at = (g * heads + h) * head_size
                out_ref[slot, g * heads + h] = (
                    starts_ref[g, slot, h].astype(F32) * scale + added[at : at + head_size, :]
                ).astype(BF)


def owned_states(layer, state, begun, received, previous):
    layers, _, heads, head_size, state_size = state.shape
    group = 4
    width = received.shape[2]
    dx_rows = SEND_CAP * S
    block_tokens = received.shape[1] - dx_rows - SUM_ROWS
    dx_at = block_tokens // dx_rows
    misc_at = (block_tokens + dx_rows) // SUM_ROWS
    in_specs = [
        pl.BlockSpec((group,) + begun.shape[1:], lambda i: (i, 0, 0, 0, 0)),
        pl.BlockSpec((group, dx_rows, width), lambda i: (i, dx_at, 0)),
        pl.BlockSpec((COLS, SUM_ROWS, width), lambda i: (0, misc_at, 0)),
    ]
    operands = [begun, received, received]
    aliases = {}
    if previous is not None:
        in_specs.append(pl.BlockSpec(memory_space=pl.ANY))
        aliases = {len(operands): 0}
        operands.append(previous)
    return pl.pallas_call(
        owned_body,
        name="owned%d" % layer,
        grid=(COLS // group,),
        in_specs=in_specs,
        out_specs=pl.BlockSpec(
            (SEND_CAP, None, group * heads, head_size, state_size),
            lambda i: (0, layer, i, 0, 0),
        ),
        out_shape=jax.ShapeDtypeStruct(
            (SEND_CAP, layers, COLS * heads, head_size, state_size), BF
        ),
        scratch_shapes=[
            pltpu.VMEM((SEND_CAP, COLS, state_size), F32),
            pltpu.VMEM((SEND_CAP, COLS, width), F32),
        ],
        input_output_aliases=aliases,
        compiler_params=pltpu.CompilerParams(
            dimension_semantics=("arbitrary",), vmem_limit_bytes=SMALL_VMEM_BYTES
        ),
    )(*operands)


def update_body(inner_width, part_ref, sums_ref, hidden_ref, *outs):
    rows = hidden_ref.shape[0]
    total = part_ref[0].astype(F32)
    sums = sums_ref[0, :, 0:128].astype(F32)
    for c in range(1, COLS):
        total = total + part_ref[c].astype(F32)
        sums = sums + sums_ref[c, :, 0:128].astype(F32)
    scale = lax.rsqrt(sums.T[:rows, 0:1] / inner_width + EPSILON)
    fresh = (hidden_ref[...].astype(F32) + total * scale).astype(BF)
    outs[0][...] = fresh
    for spread_ref in outs[1:]:
        for c in range(COLS):
            spread_ref[c] = fresh


def update(inner_width, received, hidden, spread):
    rows, lanes = hidden.shape
    shapes = [hidden.shape] + ([(COLS,) + hidden.shape] if spread else [])
    sums_at = (rows + SEND_CAP * S) // SUM_ROWS

    def whole(shape):
        return pl.BlockSpec(shape, lambda i: (0,) * len(shape))

    return pl.pallas_call(
        lambda *refs: update_body(inner_width, *refs),
        name="update_spread" if spread else "update_last",
        grid=(1,),
        in_specs=[
            pl.BlockSpec((COLS, rows, lanes), lambda i: (0, 0, 0)),
            pl.BlockSpec((COLS, SUM_ROWS, lanes), lambda i: (0, sums_at, 0)),
            whole(hidden.shape),
        ],
        out_specs=[whole(shape) for shape in shapes],
        out_shape=[jax.ShapeDtypeStruct(shape, BF) for shape in shapes],
        compiler_params=pltpu.CompilerParams(
            dimension_semantics=("arbitrary",), vmem_limit_bytes=SMALL_VMEM_BYTES
        ),
    )(received, received, hidden)


def swap(x):
    return lax.all_to_all(x, "col", 0, 0, tiled=True)


def local(
    hidden_states,
    input_gain,
    inner_weight,
    proj_weight,
    step_weight,
    inner_kernel,
    proj_kernel,
    step_bias,
    decay_log,
    skip_gain,
    norm_gain,
    out_weight,
    inner_cache,
    proj_cache,
    state_cache,
    accepted,
    owners,
    tenant_ranges,
):
    layer_count = inner_weight.shape[0]
    inner_local = inner_weight.shape[3]
    heads_local = step_weight.shape[2]
    requests_local = state_cache.shape[1]
    inner_width = inner_local * COLS
    base = (lax.axis_index("row") * requests_local).astype(jnp.int32).reshape(1)
    column = lax.axis_index("col").astype(jnp.int32).reshape(1)
    ints = jnp.concatenate([base, column, accepted, owners, tenant_ranges.reshape(-1)])
    floats = jnp.concatenate([step_bias, decay_log, skip_gain], axis=1)

    there = []
    for r in range(ROWS):
        for c in range(COLS):
            there.append((r * COLS + c, (c // 2) * COLS + (c % 2) * ROWS + r))
    back = [(b, a) for a, b in there]

    block = lax.ppermute(hidden_states, ("row", "col"), there)
    raw = (
        jnp.transpose(inner_weight, (0, 2, 1, 3)),
        proj_weight,
        jnp.transpose(step_weight, (0, 2, 1)),
        input_gain,
        out_weight,
    )
    first, block = lax.optimization_barrier((pack(0, *raw), block))
    weights = [lax.all_gather(first, "row", axis=0)]
    everything = swap(jnp.broadcast_to(block[None], (COLS,) + block.shape))
    sends = [starts(layer, ints, state_cache) for layer in range(layer_count)]
    everything, sends, raw = lax.optimization_barrier((everything, sends, raw))
    weights.append(lax.all_gather(pack(1, *raw), "row", axis=0))
    begun = swap(sends[0])
    send = sends[1]

    steps = None
    owned = None
    for layer in range(layer_count):
        last = layer == layer_count - 1
        part, dx, b_conv, decay = front(
            layer, ints, floats, everything, weights[layer], inner_kernel, proj_kernel,
            norm_gain, inner_cache, proj_cache, state_cache,
        )
        part, begun, owned = lax.optimization_barrier((part, begun, owned))
        received = swap(part)
        steps = states(layer, dx, b_conv, decay, state_cache, steps)
        received, steps = lax.optimization_barrier((received, steps))
        fresh = update(inner_width, received, block, not last)
        owned = owned_states(layer, state_cache, begun, received, owned)
        if not last:
            block = fresh[0]
            everything, send = lax.optimization_barrier((swap(fresh[1]), send))
            begun = swap(send)
    hidden = lax.ppermute(fresh[0], ("row", "col"), back)
    owned_block = owned[None, None]
    return (hidden, steps, owned_block)


def solution(mesh):
    placed = (
        P("col", "row"),
        P(None, "row"),
        P(None, "row", None, "col"),
        P(None, "row", None),
        P(None, "row", "col"),
        P(None, None, "col"),
        P(),
        P(None, "col"),
        P(None, "col"),
        P(None, "col"),
        P(None, "col"),
        P(None, "col", "row"),
        P(None, "row", None, "col"),
        P(None, "row", None, None),
        P(None, "row", "col", None, None),
        P("row"),
        P("row"),
        P(),
    )
    return jax.shard_map(
        local,
        mesh=mesh,
        in_specs=placed,
        out_specs=(
            P("col", "row"),
            P(None, "row", None, "col", None, None),
            P("row", "col", None, None, None, None, None),
        ),
        check_vma=False,
    )
```

```python
import jax
import jax.numpy as jnp
from jax import lax
from jax.experimental import pallas as pl
from jax.experimental.pallas import tpu as pltpu
from jax.sharding import PartitionSpec as P

S = 16
SEND_CAP = 2
EPSILON = 1e-05
ROWS = 8
COLS = 16
BF = jnp.bfloat16
F32 = jnp.float32
SUM_ROWS = 16
VMEM_BYTES = 58 * 1024 * 1024
SMALL_VMEM_BYTES = 12 * 1024 * 1024


def silu(v):
    return v / (1.0 + jnp.exp(-v))


def softplus(v):
    return jnp.maximum(v, 0.0) + jnp.log1p(jnp.exp(-jnp.abs(v)))


def pack_body(layer, inner_ref, proj_ref, step_ref, gain_ref, out_ref, packed_ref):
    rows, width = out_ref.shape
    states = proj_ref.shape[1]
    gain = jnp.broadcast_to(gain_ref[layer : layer + 1, :], (8, rows)).T[:, 0:1]
    step = step_ref[...].astype(F32)
    step = jnp.concatenate([step, jnp.zeros((128 - step.shape[0], rows), F32)], axis=0).T
    at = 0
    for piece in (inner_ref[0], inner_ref[1], proj_ref[...], step):
        end = at + piece.shape[1]
        packed_ref[:, at:end] = (piece.astype(F32) * gain).astype(BF)
        at = end
    packed_ref[:, at:] = out_ref[...]


def pack(layer, inner, proj, step, gain, out):
    rows, width = inner.shape[2:]
    cols = 2 * width + proj.shape[2] + 128 + out.shape[2]

    def layer_of(shape):
        return pl.BlockSpec((None,) + shape[1:], lambda i: (layer,) + (0,) * (len(shape) - 1))

    return pl.pallas_call(
        lambda *refs: pack_body(layer, *refs),
        name="pack%d" % layer,
        grid=(1,),
        in_specs=[
            layer_of(inner.shape),
            layer_of(proj.shape),
            layer_of(step.shape),
            pl.BlockSpec(gain.shape, lambda i: (0, 0)),
            layer_of(out.shape),
        ],
        out_specs=pl.BlockSpec((rows, cols), lambda i: (0, 0)),
        out_shape=jax.ShapeDtypeStruct((rows, cols), BF),
        compiler_params=pltpu.CompilerParams(
            dimension_semantics=("arbitrary",), vmem_limit_bytes=VMEM_BYTES
        ),
    )(inner, proj, step, gain, out)


def route(q, ints_ref, requests):
    owners, ranges = 2 + requests, 2 + 2 * requests
    request = ints_ref[0] + q
    live = (request >= ints_ref[ranges]) & (request < ints_ref[ranges + 1])
    for k in range(ranges + 2, ints_ref.shape[0], 2):
        live = live | ((request >= ints_ref[k]) & (request < ints_ref[k + 1]))
    owner = ints_ref[owners + q]
    rank = jnp.int32(0)
    for other in range(q):
        rank = rank + jnp.where(ints_ref[owners + other] == owner, 1, 0)
    return live, owner, jnp.minimum(rank, SEND_CAP - 1)


def front_body(
    layer,
    ints_ref,
    floats_ref,
    hidden_ref,
    weight_ref,
    inner_kernel_ref,
    proj_kernel_ref,
    norm_gain_ref,
    inner_cache_ref,
    proj_cache_ref,
    state_ref,
    part_ref,
    dx_ref,
    b_ref,
    dec_ref,
    x_pad,
    p_pad,
    misc_ref,
):
    requests, heads, head_size, state_size = state_ref.shape
    tokens = requests * S
    width = heads * head_size
    model_width = ROWS * hidden_ref.shape[2]
    block_tokens = hidden_ref.shape[1]
    in_cols = 2 * width + 2 * state_size + 128
    lane = lax.broadcasted_iota(jnp.int32, (1, 128), 1)

    def spread(pieces):
        return jnp.concatenate(
            [jnp.where(lane < 64, pieces[2 * k], pieces[2 * k + 1]) for k in range(heads // 2)],
            axis=1,
        )

    total = jnp.zeros((tokens, in_cols), F32)
    squares = jnp.zeros((tokens, 128), F32)
    for r in range(ROWS):
        rows_r = jnp.concatenate([hidden_ref[r], hidden_ref[ROWS + r]], axis=0)
        total = total + jnp.dot(rows_r, weight_ref[r, :, :in_cols], preferred_element_type=F32)
        wide = rows_r.astype(F32)
        wide = wide * wide
        squares = squares + wide[:, :128] + wide[:, 128:]
    inverse = lax.rsqrt(jnp.sum(squares, axis=1, keepdims=True) / model_width + EPSILON)
    total = total * inverse
    z = total[:, :width]
    x_pad[:, 8:24, :] = total[:, width : 2 * width].reshape(requests, S, width)
    p_pad[:, 8:24, :] = total[:, 2 * width : 2 * width + 2 * state_size].reshape(
        requests, S, 2 * state_size
    )
    x_pad[:, 5:8, :] = inner_cache_ref[...].astype(F32)
    p_pad[:, 5:8, :] = proj_cache_ref[...].astype(F32)
    conv_x = x_pad[:, 5 : 5 + S, :] * inner_kernel_ref[0:1, :]
    conv_p = p_pad[:, 5 : 5 + S, :] * proj_kernel_ref[0:1, :]
    for i in range(1, 4):
        conv_x = conv_x + x_pad[:, 5 + i : 5 + i + S, :] * inner_kernel_ref[i : i + 1, :]
        conv_p = conv_p + p_pad[:, 5 + i : 5 + i + S, :] * proj_kernel_ref[i : i + 1, :]
    x_conv = silu(conv_x).reshape(tokens, width)
    p_conv = silu(conv_p).reshape(tokens, 2 * state_size)
    b_conv = p_conv[:, :state_size]
    c_conv = p_conv[:, state_size:].astype(BF)
    b_ref[...] = b_conv
    step_raw = total[:, 2 * width + 2 * state_size :]
    t_now = lax.broadcasted_iota(jnp.int32, (tokens, tokens), 0)
    t_then = lax.broadcasted_iota(jnp.int32, (tokens, tokens), 1)
    causal = (t_now // S == t_then // S) & (t_then <= t_now)
    lower = causal.astype(F32)
    scores = lax.dot_general(
        c_conv, b_conv.astype(BF), (((1,), (1,)), ((), ())), preferred_element_type=F32
    )
    deltas = []
    sums_log = []
    mixes = []
    for h in range(heads):
        raw = jnp.broadcast_to(step_raw[:, h : h + 1], (tokens, 128))
        delta = softplus(raw + floats_ref[layer, h])
        rate = jnp.exp(jnp.full((1, 128), floats_ref[layer, heads + h], F32))
        log_decay = -delta * rate
        dec_ref[:, h * 128 : (h + 1) * 128] = jnp.exp(log_decay)
        cum = jnp.dot(
            lower, log_decay, precision=lax.Precision.HIGHEST, preferred_element_type=F32
        )
        gap = jnp.where(causal, cum - cum.T, 0.0)
        mixes.append((jnp.where(causal, jnp.exp(gap), 0.0) * scores).astype(BF))
        deltas.append(delta)
        sums_log.append(cum)
    dx = x_conv * spread(deltas)
    cum_all = spread(sums_log)
    grown = jnp.exp(cum_all)
    dx_ref[...] = dx
    y_diag = []
    for k in range(heads // 2):
        dx_k = dx[:, 128 * k : 128 * (k + 1)].astype(BF)
        first = jnp.dot(mixes[2 * k], dx_k, preferred_element_type=F32)
        second = jnp.dot(mixes[2 * k + 1], dx_k, preferred_element_type=F32)
        y_diag.append(jnp.where(lane < 64, first, second))
    y_off = []
    for q in range(requests):
        flat = state_ref[q].reshape(width, state_size).astype(BF)
        y_off.append(
            lax.dot_general(
                c_conv[q * S : (q + 1) * S, :], flat, (((1,), (1,)), ((), ())),
                preferred_element_type=F32,
            )
        )
    skip = spread([jnp.full((1, 128), floats_ref[layer, 2 * heads + h], F32) for h in range(heads)])
    y = (
        jnp.concatenate(y_diag, axis=1)
        + grown * jnp.concatenate(y_off, axis=0)
        + skip * x_conv
    )
    g = y * silu(z)
    yg = (g * norm_gain_ref[layer : layer + 1, :]).astype(BF)
    g2 = (g * g).astype(BF)
    ones = jnp.ones((SUM_ROWS, width), BF)
    misc_row = block_tokens + SEND_CAP * S
    line = lax.broadcasted_iota(jnp.int32, (SUM_ROWS, 1), 0)
    part_ref[:, block_tokens:misc_row, :] = jnp.zeros((COLS, SEND_CAP * S, width), BF)
    nothing = jnp.zeros((SUM_ROWS, width - block_tokens), F32)
    for b in range(2):
        sums = lax.dot_general(
            ones,
            g2[b * block_tokens : (b + 1) * block_tokens, :],
            (((1,), (1,)), ((), ())),
            preferred_element_type=F32,
        )
        sums = jnp.where(line == 0, jnp.concatenate([sums, nothing], axis=1), 0.0)
        for r in range(ROWS):
            misc_ref[b * ROWS + r] = sums
    step = lax.broadcasted_iota(jnp.int32, (S, 1), 0)
    column = ints_ref[1]
    for q in range(requests):
        live, owner, rank = route(q, ints_ref, requests)
        taken = ints_ref[2 + q] - 1
        rows = slice(q * S, (q + 1) * S)
        cum_q = cum_all[rows, :]
        cum_end = jnp.sum(jnp.where(step == taken, cum_q, 0.0), axis=0, keepdims=True)
        inside = step <= taken
        weight = jnp.where(inside, jnp.exp(jnp.where(inside, cum_end - cum_q, 0.0)), 0.0)
        scale = jnp.exp(cum_end)
        high = scale.astype(BF).astype(F32)
        low = scale - high
        mine = jnp.sum(jnp.where(step == column, b_conv[rows, :], 0.0), axis=0, keepdims=True)
        mine = jnp.concatenate([mine, jnp.zeros((1, width - state_size), F32)], axis=1)
        at = 1 + 3 * rank
        extra = jnp.where(
            line == at,
            mine,
            jnp.where(line == at + 1, high, jnp.where(line == at + 2, low, 0.0)),
        )
        first = pl.multiple_of(block_tokens + rank * S, S)

        @pl.when(live)
        def _send():
            part_ref[owner, pl.ds(first, S), :] = (dx[rows, :] * weight).astype(BF)
            misc_ref[owner] = misc_ref[owner] + extra

    part_ref[:, misc_row:, :] = misc_ref[...].astype(BF)
    for r in range(ROWS):
        part = jnp.dot(yg, weight_ref[r, :, in_cols:], preferred_element_type=F32).astype(BF)
        for b in range(2):
            part_ref[b * ROWS + r, 0:block_tokens, :] = part[
                b * block_tokens : (b + 1) * block_tokens, :
            ]


def front(layer, ints, floats, hidden, weight, inner_kernel, proj_kernel,
          norm_gain, inner_cache, proj_cache, state):
    layers, requests, heads, head_size, state_size = state.shape
    width = heads * head_size
    tokens = requests * S
    smem = pl.BlockSpec(memory_space=pltpu.SMEM)

    def whole(shape):
        return pl.BlockSpec(shape, lambda i: (0,) * len(shape))

    def layer_of(shape):
        return pl.BlockSpec((None,) + shape[1:], lambda i: (layer,) + (0,) * (len(shape) - 1))

    block_tokens = tokens // 2
    out_shapes = [
        ((COLS, block_tokens + SEND_CAP * S + SUM_ROWS, width), BF),
        ((tokens, width), F32),
        ((tokens, state_size), F32),
        ((tokens, heads * 128), F32),
    ]
    return pl.pallas_call(
        lambda *refs: front_body(layer, *refs),
        name="front%d" % layer,
        grid=(1,),
        in_specs=[
            smem, smem,
            whole(hidden.shape),
            whole(weight.shape),
            layer_of(inner_kernel.shape),
            layer_of(proj_kernel.shape),
            whole(norm_gain.shape),
            layer_of(inner_cache.shape),
            layer_of(proj_cache.shape),
            layer_of(state.shape),
        ],
        out_specs=[whole(shape) for shape, _ in out_shapes],
        out_shape=[jax.ShapeDtypeStruct(shape, kind) for shape, kind in out_shapes],
        scratch_shapes=[
            pltpu.VMEM((requests, 24, width), F32),
            pltpu.VMEM((requests, 24, 2 * state_size), F32),
            pltpu.VMEM((COLS, SUM_ROWS, width), F32),
        ],
        compiler_params=pltpu.CompilerParams(
            dimension_semantics=("arbitrary",), vmem_limit_bytes=VMEM_BYTES
        ),
    )(ints, floats, hidden, weight, inner_kernel, proj_kernel, norm_gain,
      inner_cache, proj_cache, state)


def states_body(dx_ref, b_ref, dec_ref, state_ref, *rest):
    steps_ref = rest[-1]
    heads, head_size, state_size = state_ref.shape
    dx_t = dx_ref[...].T
    for h in range(heads):
        state = state_ref[h]
        columns = dx_t[h * head_size : (h + 1) * head_size, :]
        for t in range(S):
            state = (
                state * dec_ref[t : t + 1, h * 128 : (h + 1) * 128]
                + columns[:, t : t + 1] * b_ref[t : t + 1, :]
            )
            steps_ref[t, h] = state.astype(BF)


def states(layer, dx, b, dec, state, previous):
    layers, requests, heads, head_size, state_size = state.shape
    width = heads * head_size
    in_specs = [
        pl.BlockSpec((S, width), lambda q: (q, 0)),
        pl.BlockSpec((S, state_size), lambda q: (q, 0)),
        pl.BlockSpec((S, heads * 128), lambda q: (q, 0)),
        pl.BlockSpec((None, None, heads, head_size, state_size), lambda q: (layer, q, 0, 0, 0)),
    ]
    operands = [dx, b, dec, state]
    aliases = {}
    if previous is not None:
        in_specs.append(pl.BlockSpec(memory_space=pl.ANY))
        aliases = {len(operands): 0}
        operands.append(previous)
    return pl.pallas_call(
        states_body,
        name="states%d" % layer,
        grid=(requests,),
        in_specs=in_specs,
        out_specs=pl.BlockSpec(
            (None, None, S, heads, head_size, state_size), lambda q: (layer, q, 0, 0, 0, 0)
        ),
        out_shape=jax.ShapeDtypeStruct(
            (layers, requests, S, heads, head_size, state_size), BF
        ),
        input_output_aliases=aliases,
        compiler_params=pltpu.CompilerParams(
            dimension_semantics=("arbitrary",), vmem_limit_bytes=SMALL_VMEM_BYTES
        ),
    )(*operands)


def starts_body(ints_ref, state_ref, send_ref):
    send_ref[...] = jnp.zeros(send_ref.shape, BF)
    requests = state_ref.shape[0]
    for q in range(requests):
        live, owner, rank = route(q, ints_ref, requests)

        @pl.when(live)
        def _put():
            send_ref[owner, rank] = state_ref[q].astype(BF)


def starts(layer, ints, state):
    shape = (COLS, SEND_CAP) + state.shape[2:]
    return pl.pallas_call(
        starts_body,
        name="starts%d" % layer,
        grid=(1,),
        in_specs=[
            pl.BlockSpec(memory_space=pltpu.SMEM),
            pl.BlockSpec((None,) + state.shape[1:], lambda i: (layer, 0, 0, 0, 0)),
        ],
        out_specs=pl.BlockSpec(shape, lambda i: (0, 0, 0, 0, 0)),
        out_shape=jax.ShapeDtypeStruct(shape, BF),
        compiler_params=pltpu.CompilerParams(
            dimension_semantics=("arbitrary",), vmem_limit_bytes=VMEM_BYTES
        ),
    )(ints, state)


def owned_body(starts_ref, dx_ref, misc_ref, *rest):
    out_ref, b_s, scale_s = rest[-3:]
    i = pl.program_id(0)
    group = starts_ref.shape[0]
    slots, group_heads, head_size, state_size = out_ref.shape
    heads = group_heads // group

    @pl.when(i == 0)
    def _first():
        b_s[...] = jnp.zeros(b_s.shape, F32)
        for slot in range(slots):
            row = 1 + 3 * slot
            for c in range(COLS):
                lines = misc_ref[c].astype(F32)
                b_s[
                    slot * S + c : slot * S + c + 1, slot * state_size : (slot + 1) * state_size
                ] = lines[row : row + 1, 0:state_size]
                scale_s[slot, c : c + 1, :] = (
                    lines[row + 1 : row + 2, :] + lines[row + 2 : row + 3, :]
                )

    dx = jnp.concatenate([dx_ref[g] for g in range(group)], axis=1)
    added = lax.dot_general(
        dx, b_s[...].astype(BF), (((0,), (0,)), ((), ())), preferred_element_type=F32
    )
    for slot in range(slots):
        for g in range(group):
            scales = scale_s[slot, pl.ds(i * group + g, 1), :]
            for h in range(heads):
                scale = scales[:, h * head_size : h * head_size + 1]
                at = (g * heads + h) * head_size
                out_ref[slot, g * heads + h] = (
                    starts_ref[g, slot, h].astype(F32) * scale
                    + added[at : at + head_size, slot * state_size : (slot + 1) * state_size]
                ).astype(BF)


def owned_states(layer, state, begun, received, previous):
    layers, _, heads, head_size, state_size = state.shape
    group = 4
    width = received.shape[2]
    dx_rows = SEND_CAP * S
    block_tokens = received.shape[1] - dx_rows - SUM_ROWS
    dx_at = block_tokens // dx_rows
    misc_at = (block_tokens + dx_rows) // SUM_ROWS
    in_specs = [
        pl.BlockSpec((group,) + begun.shape[1:], lambda i: (i, 0, 0, 0, 0)),
        pl.BlockSpec((group, dx_rows, width), lambda i: (i, dx_at, 0)),
        pl.BlockSpec((COLS, SUM_ROWS, width), lambda i: (0, misc_at, 0)),
    ]
    operands = [begun, received, received]
    aliases = {}
    if previous is not None:
        in_specs.append(pl.BlockSpec(memory_space=pl.ANY))
        aliases = {len(operands): 0}
        operands.append(previous)
    return pl.pallas_call(
        owned_body,
        name="owned%d" % layer,
        grid=(COLS // group,),
        in_specs=in_specs,
        out_specs=pl.BlockSpec(
            (SEND_CAP, None, group * heads, head_size, state_size),
            lambda i: (0, layer, i, 0, 0),
        ),
        out_shape=jax.ShapeDtypeStruct(
            (SEND_CAP, layers, COLS * heads, head_size, state_size), BF
        ),
        scratch_shapes=[
            pltpu.VMEM((SEND_CAP * S, SEND_CAP * state_size), F32),
            pltpu.VMEM((SEND_CAP, COLS, width), F32),
        ],
        input_output_aliases=aliases,
        compiler_params=pltpu.CompilerParams(
            dimension_semantics=("arbitrary",), vmem_limit_bytes=SMALL_VMEM_BYTES
        ),
    )(*operands)


def update_body(inner_width, part_ref, sums_ref, hidden_ref, *outs):
    rows = hidden_ref.shape[0]
    total = part_ref[0].astype(F32)
    sums = sums_ref[0, :, 0:128].astype(F32)
    for c in range(1, COLS):
        total = total + part_ref[c].astype(F32)
        sums = sums + sums_ref[c, :, 0:128].astype(F32)
    scale = lax.rsqrt(sums.T[:rows, 0:1] / inner_width + EPSILON)
    fresh = (hidden_ref[...].astype(F32) + total * scale).astype(BF)
    outs[0][...] = fresh
    for spread_ref in outs[1:]:
        for c in range(COLS):
            spread_ref[c] = fresh


def update(inner_width, received, hidden, spread):
    rows, lanes = hidden.shape
    shapes = [hidden.shape] + ([(COLS,) + hidden.shape] if spread else [])
    sums_at = (rows + SEND_CAP * S) // SUM_ROWS

    def whole(shape):
        return pl.BlockSpec(shape, lambda i: (0,) * len(shape))

    return pl.pallas_call(
        lambda *refs: update_body(inner_width, *refs),
        name="update_spread" if spread else "update_last",
        grid=(1,),
        in_specs=[
            pl.BlockSpec((COLS, rows, lanes), lambda i: (0, 0, 0)),
            pl.BlockSpec((COLS, SUM_ROWS, lanes), lambda i: (0, sums_at, 0)),
            whole(hidden.shape),
        ],
        out_specs=[whole(shape) for shape in shapes],
        out_shape=[jax.ShapeDtypeStruct(shape, BF) for shape in shapes],
        compiler_params=pltpu.CompilerParams(
            dimension_semantics=("arbitrary",), vmem_limit_bytes=SMALL_VMEM_BYTES
        ),
    )(received, received, hidden)


def swap(x):
    return lax.all_to_all(x, "col", 0, 0, tiled=True)


def local(
    hidden_states,
    input_gain,
    inner_weight,
    proj_weight,
    step_weight,
    inner_kernel,
    proj_kernel,
    step_bias,
    decay_log,
    skip_gain,
    norm_gain,
    out_weight,
    inner_cache,
    proj_cache,
    state_cache,
    accepted,
    owners,
    tenant_ranges,
):
    layer_count = inner_weight.shape[0]
    inner_local = inner_weight.shape[3]
    heads_local = step_weight.shape[2]
    requests_local = state_cache.shape[1]
    inner_width = inner_local * COLS
    base = (lax.axis_index("row") * requests_local).astype(jnp.int32).reshape(1)
    column = lax.axis_index("col").astype(jnp.int32).reshape(1)
    ints = jnp.concatenate([base, column, accepted, owners, tenant_ranges.reshape(-1)])
    floats = jnp.concatenate([step_bias, decay_log, skip_gain], axis=1)

    there = []
    for r in range(ROWS):
        for c in range(COLS):
            there.append((r * COLS + c, (c // 2) * COLS + (c % 2) * ROWS + r))
    back = [(b, a) for a, b in there]

    block = lax.ppermute(hidden_states, ("row", "col"), there)
    raw = (
        jnp.transpose(inner_weight, (0, 2, 1, 3)),
        proj_weight,
        jnp.transpose(step_weight, (0, 2, 1)),
        input_gain,
        out_weight,
    )
    first, block = lax.optimization_barrier((pack(0, *raw), block))
    weights = [lax.all_gather(first, "row", axis=0)]
    everything = swap(jnp.broadcast_to(block[None], (COLS,) + block.shape))
    sends = [starts(layer, ints, state_cache) for layer in range(layer_count)]
    sends, raw = lax.optimization_barrier((sends, raw))
    second = pack(1, *raw)
    everything, sends, second = lax.optimization_barrier((everything, sends, second))
    weights.append(lax.all_gather(second, "row", axis=0))
    begun = swap(sends[0])
    send = sends[1]

    steps = None
    owned = None
    for layer in range(layer_count):
        last = layer == layer_count - 1
        part, dx, b_conv, decay = front(
            layer, ints, floats, everything, weights[layer], inner_kernel, proj_kernel,
            norm_gain, inner_cache, proj_cache, state_cache,
        )
        part, begun, owned = lax.optimization_barrier((part, begun, owned))
        received = swap(part)
        steps = states(layer, dx, b_conv, decay, state_cache, steps)
        received, steps = lax.optimization_barrier((received, steps))
        fresh = update(inner_width, received, block, not last)
        owned = owned_states(layer, state_cache, begun, received, owned)
        if not last:
            block = fresh[0]
            everything, send = lax.optimization_barrier((swap(fresh[1]), send))
            begun = swap(send)
    hidden = lax.ppermute(fresh[0], ("row", "col"), back)
    owned_block = owned[None, None]
    return (hidden, steps, owned_block)


def solution(mesh):
    placed = (
        P("col", "row"),
        P(None, "row"),
        P(None, "row", None, "col"),
        P(None, "row", None),
        P(None, "row", "col"),
        P(None, None, "col"),
        P(),
        P(None, "col"),
        P(None, "col"),
        P(None, "col"),
        P(None, "col"),
        P(None, "col", "row"),
        P(None, "row", None, "col"),
        P(None, "row", None, None),
        P(None, "row", "col", None, None),
        P("row"),
        P("row"),
        P(),
    )
    return jax.shard_map(
        local,
        mesh=mesh,
        in_specs=placed,
        out_specs=(
            P("col", "row"),
            P(None, "row", None, "col", None, None),
            P("row", "col", None, None, None, None, None),
        ),
        check_vma=False,
    )
```

```python
import jax
import jax.numpy as jnp
from jax import lax
from jax.experimental import pallas as pl
from jax.experimental.pallas import tpu as pltpu
from jax.sharding import PartitionSpec as P

S = 16
SEND_CAP = 2
EPSILON = 1e-05
ROWS = 8
COLS = 16
BF = jnp.bfloat16
F32 = jnp.float32
SUM_ROWS = 16
VMEM_BYTES = 58 * 1024 * 1024
SMALL_VMEM_BYTES = 12 * 1024 * 1024


def silu(v):
    return v / (1.0 + jnp.exp(-v))


def softplus(v):
    return jnp.maximum(v, 0.0) + jnp.log1p(jnp.exp(-jnp.abs(v)))


def pack_body(layer, inner_ref, proj_ref, step_ref, gain_ref, out_ref, packed_ref):
    rows, width = out_ref.shape
    states = proj_ref.shape[1]
    gain = jnp.broadcast_to(gain_ref[layer : layer + 1, :], (8, rows)).T[:, 0:1]
    step = step_ref[...].astype(F32)
    step = jnp.concatenate([step, jnp.zeros((128 - step.shape[0], rows), F32)], axis=0).T
    at = 0
    for piece in (inner_ref[0], inner_ref[1], proj_ref[...], step):
        end = at + piece.shape[1]
        packed_ref[:, at:end] = (piece.astype(F32) * gain).astype(BF)
        at = end
    packed_ref[:, at:] = out_ref[...]


def pack(layer, inner, proj, step, gain, out):
    rows, width = inner.shape[2:]
    cols = 2 * width + proj.shape[2] + 128 + out.shape[2]

    def layer_of(shape):
        return pl.BlockSpec((None,) + shape[1:], lambda i: (layer,) + (0,) * (len(shape) - 1))

    return pl.pallas_call(
        lambda *refs: pack_body(layer, *refs),
        name="pack%d" % layer,
        grid=(1,),
        in_specs=[
            layer_of(inner.shape),
            layer_of(proj.shape),
            layer_of(step.shape),
            pl.BlockSpec(gain.shape, lambda i: (0, 0)),
            layer_of(out.shape),
        ],
        out_specs=pl.BlockSpec((rows, cols), lambda i: (0, 0)),
        out_shape=jax.ShapeDtypeStruct((rows, cols), BF),
        compiler_params=pltpu.CompilerParams(
            dimension_semantics=("arbitrary",), vmem_limit_bytes=VMEM_BYTES
        ),
    )(inner, proj, step, gain, out)


def route(q, ints_ref, requests):
    owners, ranges = 2 + requests, 2 + 2 * requests
    request = ints_ref[0] + q
    live = (request >= ints_ref[ranges]) & (request < ints_ref[ranges + 1])
    for k in range(ranges + 2, ints_ref.shape[0], 2):
        live = live | ((request >= ints_ref[k]) & (request < ints_ref[k + 1]))
    owner = ints_ref[owners + q]
    rank = jnp.int32(0)
    for other in range(q):
        rank = rank + jnp.where(ints_ref[owners + other] == owner, 1, 0)
    return live, owner, jnp.minimum(rank, SEND_CAP - 1)


def front_body(
    layer,
    ints_ref,
    floats_ref,
    hidden_ref,
    weight_ref,
    inner_kernel_ref,
    proj_kernel_ref,
    norm_gain_ref,
    inner_cache_ref,
    proj_cache_ref,
    state_ref,
    part_ref,
    dx_ref,
    b_ref,
    dec_ref,
    x_pad,
    p_pad,
    misc_ref,
):
    requests, heads, head_size, state_size = state_ref.shape
    tokens = requests * S
    width = heads * head_size
    model_width = ROWS * hidden_ref.shape[2]
    block_tokens = hidden_ref.shape[1]
    in_cols = 2 * width + 2 * state_size + 128
    lane = lax.broadcasted_iota(jnp.int32, (1, 128), 1)

    def spread(pieces):
        return jnp.concatenate(
            [jnp.where(lane < 64, pieces[2 * k], pieces[2 * k + 1]) for k in range(heads // 2)],
            axis=1,
        )

    total = jnp.zeros((tokens, in_cols), F32)
    squares = jnp.zeros((tokens, 128), F32)
    for r in range(ROWS):
        rows_r = jnp.concatenate([hidden_ref[r], hidden_ref[ROWS + r]], axis=0)
        total = total + jnp.dot(rows_r, weight_ref[r, :, :in_cols], preferred_element_type=F32)
        wide = rows_r.astype(F32)
        wide = wide * wide
        squares = squares + wide[:, :128] + wide[:, 128:]
    inverse = lax.rsqrt(jnp.sum(squares, axis=1, keepdims=True) / model_width + EPSILON)
    total = total * inverse
    z = total[:, :width]
    x_pad[:, 8:24, :] = total[:, width : 2 * width].reshape(requests, S, width)
    p_pad[:, 8:24, :] = total[:, 2 * width : 2 * width + 2 * state_size].reshape(
        requests, S, 2 * state_size
    )
    x_pad[:, 5:8, :] = inner_cache_ref[...].astype(F32)
    p_pad[:, 5:8, :] = proj_cache_ref[...].astype(F32)
    conv_x = x_pad[:, 5 : 5 + S, :] * inner_kernel_ref[0:1, :]
    conv_p = p_pad[:, 5 : 5 + S, :] * proj_kernel_ref[0:1, :]
    for i in range(1, 4):
        conv_x = conv_x + x_pad[:, 5 + i : 5 + i + S, :] * inner_kernel_ref[i : i + 1, :]
        conv_p = conv_p + p_pad[:, 5 + i : 5 + i + S, :] * proj_kernel_ref[i : i + 1, :]
    x_conv = silu(conv_x).reshape(tokens, width)
    p_conv = silu(conv_p).reshape(tokens, 2 * state_size)
    b_conv = p_conv[:, :state_size]
    c_conv = p_conv[:, state_size:].astype(BF)
    b_ref[...] = b_conv
    step_raw = total[:, 2 * width + 2 * state_size :]
    t_now = lax.broadcasted_iota(jnp.int32, (tokens, tokens), 0)
    t_then = lax.broadcasted_iota(jnp.int32, (tokens, tokens), 1)
    causal = (t_now // S == t_then // S) & (t_then <= t_now)
    lower = causal.astype(F32)
    scores = lax.dot_general(
        c_conv, b_conv.astype(BF), (((1,), (1,)), ((), ())), preferred_element_type=F32
    )
    deltas = []
    sums_log = []
    mixes = []
    for h in range(heads):
        raw = jnp.broadcast_to(step_raw[:, h : h + 1], (tokens, 128))
        delta = softplus(raw + floats_ref[layer, h])
        rate = jnp.exp(jnp.full((1, 128), floats_ref[layer, heads + h], F32))
        log_decay = -delta * rate
        dec_ref[:, h * 128 : (h + 1) * 128] = jnp.exp(log_decay)
        cum = jnp.dot(
            lower, log_decay, precision=lax.Precision.HIGHEST, preferred_element_type=F32
        )
        gap = jnp.where(causal, cum - cum.T, 0.0)
        mixes.append((jnp.where(causal, jnp.exp(gap), 0.0) * scores).astype(BF))
        deltas.append(delta)
        sums_log.append(cum)
    dx = x_conv * spread(deltas)
    cum_all = spread(sums_log)
    grown = jnp.exp(cum_all)
    dx_ref[...] = dx
    y_diag = []
    for k in range(heads // 2):
        dx_k = dx[:, 128 * k : 128 * (k + 1)].astype(BF)
        first = jnp.dot(mixes[2 * k], dx_k, preferred_element_type=F32)
        second = jnp.dot(mixes[2 * k + 1], dx_k, preferred_element_type=F32)
        y_diag.append(jnp.where(lane < 64, first, second))
    y_off = []
    for q in range(requests):
        flat = state_ref[q].reshape(width, state_size).astype(BF)
        y_off.append(
            lax.dot_general(
                c_conv[q * S : (q + 1) * S, :], flat, (((1,), (1,)), ((), ())),
                preferred_element_type=F32,
            )
        )
    skip = spread([jnp.full((1, 128), floats_ref[layer, 2 * heads + h], F32) for h in range(heads)])
    y = (
        jnp.concatenate(y_diag, axis=1)
        + grown * jnp.concatenate(y_off, axis=0)
        + skip * x_conv
    )
    g = y * silu(z)
    yg = (g * norm_gain_ref[layer : layer + 1, :]).astype(BF)
    g2 = (g * g).astype(BF)
    ones = jnp.ones((SUM_ROWS, width), BF)
    misc_row = block_tokens + SEND_CAP * S
    line = lax.broadcasted_iota(jnp.int32, (SUM_ROWS, 1), 0)
    part_ref[:, block_tokens:misc_row, :] = jnp.zeros((COLS, SEND_CAP * S, width), BF)
    nothing = jnp.zeros((SUM_ROWS, width - block_tokens), F32)
    for b in range(2):
        sums = lax.dot_general(
            ones,
            g2[b * block_tokens : (b + 1) * block_tokens, :],
            (((1,), (1,)), ((), ())),
            preferred_element_type=F32,
        )
        sums = jnp.where(line == 0, jnp.concatenate([sums, nothing], axis=1), 0.0)
        for r in range(ROWS):
            misc_ref[b * ROWS + r] = sums
    step = lax.broadcasted_iota(jnp.int32, (S, 1), 0)
    column = ints_ref[1]
    for q in range(requests):
        live, owner, rank = route(q, ints_ref, requests)
        taken = ints_ref[2 + q] - 1
        rows = slice(q * S, (q + 1) * S)
        cum_q = cum_all[rows, :]
        cum_end = jnp.sum(jnp.where(step == taken, cum_q, 0.0), axis=0, keepdims=True)
        inside = step <= taken
        weight = jnp.where(inside, jnp.exp(jnp.where(inside, cum_end - cum_q, 0.0)), 0.0)
        scale = jnp.exp(cum_end)
        high = scale.astype(BF).astype(F32)
        low = scale - high
        mine = jnp.sum(jnp.where(step == column, b_conv[rows, :], 0.0), axis=0, keepdims=True)
        mine = jnp.concatenate([mine, jnp.zeros((1, width - state_size), F32)], axis=1)
        at = 1 + 3 * rank
        extra = jnp.where(
            line == at,
            mine,
            jnp.where(line == at + 1, high, jnp.where(line == at + 2, low, 0.0)),
        )
        first = pl.multiple_of(block_tokens + rank * S, S)

        @pl.when(live)
        def _send():
            part_ref[owner, pl.ds(first, S), :] = (dx[rows, :] * weight).astype(BF)
            misc_ref[owner] = misc_ref[owner] + extra

    part_ref[:, misc_row:, :] = misc_ref[...].astype(BF)
    for r in range(ROWS):
        part = jnp.dot(yg, weight_ref[r, :, in_cols:], preferred_element_type=F32).astype(BF)
        for b in range(2):
            part_ref[b * ROWS + r, 0:block_tokens, :] = part[
                b * block_tokens : (b + 1) * block_tokens, :
            ]


def front(layer, ints, floats, hidden, weight, inner_kernel, proj_kernel,
          norm_gain, inner_cache, proj_cache, state):
    layers, requests, heads, head_size, state_size = state.shape
    width = heads * head_size
    tokens = requests * S
    smem = pl.BlockSpec(memory_space=pltpu.SMEM)

    def whole(shape):
        return pl.BlockSpec(shape, lambda i: (0,) * len(shape))

    def layer_of(shape):
        return pl.BlockSpec((None,) + shape[1:], lambda i: (layer,) + (0,) * (len(shape) - 1))

    block_tokens = tokens // 2
    out_shapes = [
        ((COLS, block_tokens + SEND_CAP * S + SUM_ROWS, width), BF),
        ((tokens, width), F32),
        ((tokens, state_size), F32),
        ((tokens, heads * 128), F32),
    ]
    return pl.pallas_call(
        lambda *refs: front_body(layer, *refs),
        name="front%d" % layer,
        grid=(1,),
        in_specs=[
            smem, smem,
            whole(hidden.shape),
            whole(weight.shape),
            layer_of(inner_kernel.shape),
            layer_of(proj_kernel.shape),
            whole(norm_gain.shape),
            layer_of(inner_cache.shape),
            layer_of(proj_cache.shape),
            layer_of(state.shape),
        ],
        out_specs=[whole(shape) for shape, _ in out_shapes],
        out_shape=[jax.ShapeDtypeStruct(shape, kind) for shape, kind in out_shapes],
        scratch_shapes=[
            pltpu.VMEM((requests, 24, width), F32),
            pltpu.VMEM((requests, 24, 2 * state_size), F32),
            pltpu.VMEM((COLS, SUM_ROWS, width), F32),
        ],
        compiler_params=pltpu.CompilerParams(
            dimension_semantics=("arbitrary",), vmem_limit_bytes=VMEM_BYTES
        ),
    )(ints, floats, hidden, weight, inner_kernel, proj_kernel, norm_gain,
      inner_cache, proj_cache, state)


def states_body(dx_ref, b_ref, dec_ref, state_ref, *rest):
    steps_ref = rest[-1]
    heads, head_size, state_size = state_ref.shape
    dx_t = dx_ref[...].T
    for h in range(heads):
        state = state_ref[h]
        columns = dx_t[h * head_size : (h + 1) * head_size, :]
        for t in range(S):
            state = (
                state * dec_ref[t : t + 1, h * 128 : (h + 1) * 128]
                + columns[:, t : t + 1] * b_ref[t : t + 1, :]
            )
            steps_ref[t, h] = state.astype(BF)


def states(layer, dx, b, dec, state, previous):
    layers, requests, heads, head_size, state_size = state.shape
    width = heads * head_size
    in_specs = [
        pl.BlockSpec((S, width), lambda q: (q, 0)),
        pl.BlockSpec((S, state_size), lambda q: (q, 0)),
        pl.BlockSpec((S, heads * 128), lambda q: (q, 0)),
        pl.BlockSpec((None, None, heads, head_size, state_size), lambda q: (layer, q, 0, 0, 0)),
    ]
    operands = [dx, b, dec, state]
    aliases = {}
    if previous is not None:
        in_specs.append(pl.BlockSpec(memory_space=pl.ANY))
        aliases = {len(operands): 0}
        operands.append(previous)
    return pl.pallas_call(
        states_body,
        name="states%d" % layer,
        grid=(requests,),
        in_specs=in_specs,
        out_specs=pl.BlockSpec(
            (None, None, S, heads, head_size, state_size), lambda q: (layer, q, 0, 0, 0, 0)
        ),
        out_shape=jax.ShapeDtypeStruct(
            (layers, requests, S, heads, head_size, state_size), BF
        ),
        input_output_aliases=aliases,
        compiler_params=pltpu.CompilerParams(
            dimension_semantics=("arbitrary",), vmem_limit_bytes=SMALL_VMEM_BYTES
        ),
    )(*operands)


def starts_body(ints_ref, state_ref, send_ref):
    send_ref[...] = jnp.zeros(send_ref.shape, BF)
    requests = state_ref.shape[0]
    for q in range(requests):
        live, owner, rank = route(q, ints_ref, requests)

        @pl.when(live)
        def _put():
            send_ref[owner, rank] = state_ref[q].astype(BF)


def starts(layer, ints, state):
    shape = (COLS, SEND_CAP) + state.shape[2:]
    return pl.pallas_call(
        starts_body,
        name="starts%d" % layer,
        grid=(1,),
        in_specs=[
            pl.BlockSpec(memory_space=pltpu.SMEM),
            pl.BlockSpec((None,) + state.shape[1:], lambda i: (layer, 0, 0, 0, 0)),
        ],
        out_specs=pl.BlockSpec(shape, lambda i: (0, 0, 0, 0, 0)),
        out_shape=jax.ShapeDtypeStruct(shape, BF),
        compiler_params=pltpu.CompilerParams(
            dimension_semantics=("arbitrary",), vmem_limit_bytes=VMEM_BYTES
        ),
    )(ints, state)


def owned_body(layer, starts_ref, received_ref, *rest):
    out_ref, stage, b_s, sems = rest[-4:]
    cols, slots, heads, head_size, state_size = starts_ref.shape
    group = 4
    dx_rows = slots * S
    misc_at = received_ref.shape[1] - SUM_ROWS
    dx_at = misc_at - dx_rows
    b_s[...] = jnp.zeros(b_s.shape, F32)
    scales = []
    for c in range(cols):
        lines = received_ref[c, misc_at:, :].astype(F32)
        for slot in range(slots):
            row = 1 + 3 * slot
            b_s[
                slot * S + c : slot * S + c + 1, slot * state_size : (slot + 1) * state_size
            ] = lines[row : row + 1, 0:state_size]
            scales.append(lines[row + 1 : row + 2, :] + lines[row + 2 : row + 3, :])
    b_all = b_s[...].astype(BF)
    copies = []
    for i in range(cols // group):
        dx = jnp.concatenate(
            [received_ref[i * group + g, dx_at:misc_at, :] for g in range(group)], axis=1
        )
        added = lax.dot_general(dx, b_all, (((0,), (0,)), ((), ())), preferred_element_type=F32)
        for slot in range(slots):
            for g in range(group):
                c = i * group + g
                for h in range(heads):
                    scale = scales[c * slots + slot][:, h * head_size : h * head_size + 1]
                    at = (g * heads + h) * head_size
                    stage[slot, c * heads + h] = (
                        starts_ref[c, slot, h].astype(F32) * scale
                        + added[at : at + head_size, slot * state_size : (slot + 1) * state_size]
                    ).astype(BF)
            span = pl.ds(i * group * heads, group * heads)
            copies.append(
                pltpu.make_async_copy(
                    stage.at[slot, span],
                    out_ref.at[slot, layer, span],
                    sems.at[i * slots + slot],
                )
            )
            copies[-1].start()
    for copy in copies:
        copy.wait()


def owned_states(layer, state, begun, received, previous):
    layers, _, heads, head_size, state_size = state.shape
    resident = pl.BlockSpec(memory_space=pltpu.VMEM)
    anywhere = pl.BlockSpec(memory_space=pl.ANY)
    in_specs = [resident, resident]
    operands = [begun, received]
    aliases = {}
    if previous is not None:
        in_specs.append(anywhere)
        aliases = {len(operands): 0}
        operands.append(previous)
    all_heads = COLS * heads
    return pl.pallas_call(
        lambda *refs: owned_body(layer, *refs),
        name="owned%d" % layer,
        in_specs=in_specs,
        out_specs=anywhere,
        out_shape=jax.ShapeDtypeStruct(
            (SEND_CAP, layers, all_heads, head_size, state_size), BF
        ),
        scratch_shapes=[
            pltpu.VMEM((SEND_CAP, all_heads, head_size, state_size), BF),
            pltpu.VMEM((SEND_CAP * S, SEND_CAP * state_size), F32),
            pltpu.SemaphoreType.DMA((SEND_CAP * COLS // 4,)),
        ],
        input_output_aliases=aliases,
        compiler_params=pltpu.CompilerParams(vmem_limit_bytes=SMALL_VMEM_BYTES),
    )(*operands)


def update_body(inner_width, part_ref, sums_ref, hidden_ref, *outs):
    rows = hidden_ref.shape[0]
    total = part_ref[0].astype(F32)
    sums = sums_ref[0, :, 0:128].astype(F32)
    for c in range(1, COLS):
        total = total + part_ref[c].astype(F32)
        sums = sums + sums_ref[c, :, 0:128].astype(F32)
    scale = lax.rsqrt(sums.T[:rows, 0:1] / inner_width + EPSILON)
    fresh = (hidden_ref[...].astype(F32) + total * scale).astype(BF)
    outs[0][...] = fresh
    for spread_ref in outs[1:]:
        for c in range(COLS):
            spread_ref[c] = fresh


def update(inner_width, received, hidden, spread):
    rows, lanes = hidden.shape
    shapes = [hidden.shape] + ([(COLS,) + hidden.shape] if spread else [])
    sums_at = (rows + SEND_CAP * S) // SUM_ROWS

    def whole(shape):
        return pl.BlockSpec(shape, lambda i: (0,) * len(shape))

    return pl.pallas_call(
        lambda *refs: update_body(inner_width, *refs),
        name="update_spread" if spread else "update_last",
        grid=(1,),
        in_specs=[
            pl.BlockSpec((COLS, rows, lanes), lambda i: (0, 0, 0)),
            pl.BlockSpec((COLS, SUM_ROWS, lanes), lambda i: (0, sums_at, 0)),
            whole(hidden.shape),
        ],
        out_specs=[whole(shape) for shape in shapes],
        out_shape=[jax.ShapeDtypeStruct(shape, BF) for shape in shapes],
        compiler_params=pltpu.CompilerParams(
            dimension_semantics=("arbitrary",), vmem_limit_bytes=SMALL_VMEM_BYTES
        ),
    )(received, received, hidden)


def swap(x):
    return lax.all_to_all(x, "col", 0, 0, tiled=True)


def local(
    hidden_states,
    input_gain,
    inner_weight,
    proj_weight,
    step_weight,
    inner_kernel,
    proj_kernel,
    step_bias,
    decay_log,
    skip_gain,
    norm_gain,
    out_weight,
    inner_cache,
    proj_cache,
    state_cache,
    accepted,
    owners,
    tenant_ranges,
):
    layer_count = inner_weight.shape[0]
    inner_local = inner_weight.shape[3]
    heads_local = step_weight.shape[2]
    requests_local = state_cache.shape[1]
    inner_width = inner_local * COLS
    base = (lax.axis_index("row") * requests_local).astype(jnp.int32).reshape(1)
    column = lax.axis_index("col").astype(jnp.int32).reshape(1)
    ints = jnp.concatenate([base, column, accepted, owners, tenant_ranges.reshape(-1)])
    floats = jnp.concatenate([step_bias, decay_log, skip_gain], axis=1)

    there = []
    for r in range(ROWS):
        for c in range(COLS):
            there.append((r * COLS + c, (c // 2) * COLS + (c % 2) * ROWS + r))
    back = [(b, a) for a, b in there]

    block = lax.ppermute(hidden_states, ("row", "col"), there)
    raw = (
        jnp.transpose(inner_weight, (0, 2, 1, 3)),
        proj_weight,
        jnp.transpose(step_weight, (0, 2, 1)),
        input_gain,
        out_weight,
    )
    first, block = lax.optimization_barrier((pack(0, *raw), block))
    weights = [lax.all_gather(first, "row", axis=0)]
    everything = swap(jnp.broadcast_to(block[None], (COLS,) + block.shape))
    sends = [starts(layer, ints, state_cache) for layer in range(layer_count)]
    sends, raw = lax.optimization_barrier((sends, raw))
    second = pack(1, *raw)
    everything, sends, second = lax.optimization_barrier((everything, sends, second))
    weights.append(lax.all_gather(second, "row", axis=0))
    begun = swap(sends[0])
    send = sends[1]

    steps = None
    owned = None
    for layer in range(layer_count):
        last = layer == layer_count - 1
        part, dx, b_conv, decay = front(
            layer, ints, floats, everything, weights[layer], inner_kernel, proj_kernel,
            norm_gain, inner_cache, proj_cache, state_cache,
        )
        part, begun, owned = lax.optimization_barrier((part, begun, owned))
        received = swap(part)
        steps = states(layer, dx, b_conv, decay, state_cache, steps)
        received, steps = lax.optimization_barrier((received, steps))
        fresh = update(inner_width, received, block, not last)
        owned = owned_states(layer, state_cache, begun, received, owned)
        if not last:
            block = fresh[0]
            everything, send = lax.optimization_barrier((swap(fresh[1]), send))
            begun = swap(send)
    hidden = lax.ppermute(fresh[0], ("row", "col"), back)
    owned_block = owned[None, None]
    return (hidden, steps, owned_block)


def solution(mesh):
    placed = (
        P("col", "row"),
        P(None, "row"),
        P(None, "row", None, "col"),
        P(None, "row", None),
        P(None, "row", "col"),
        P(None, None, "col"),
        P(),
        P(None, "col"),
        P(None, "col"),
        P(None, "col"),
        P(None, "col"),
        P(None, "col", "row"),
        P(None, "row", None, "col"),
        P(None, "row", None, None),
        P(None, "row", "col", None, None),
        P("row"),
        P("row"),
        P(),
    )
    return jax.shard_map(
        local,
        mesh=mesh,
        in_specs=placed,
        out_specs=(
            P("col", "row"),
            P(None, "row", None, "col", None, None),
            P("row", "col", None, None, None, None, None),
        ),
        check_vma=False,
    )
```

```python
import jax
import jax.numpy as jnp
from jax import lax
from jax.experimental import pallas as pl
from jax.experimental.pallas import tpu as pltpu
from jax.sharding import PartitionSpec as P

S = 16
SEND_CAP = 2
EPSILON = 1e-05
ROWS = 8
COLS = 16
BF = jnp.bfloat16
F32 = jnp.float32
SUM_ROWS = 16
VMEM_BYTES = 58 * 1024 * 1024
SMALL_VMEM_BYTES = 12 * 1024 * 1024


def silu(v):
    return v / (1.0 + jnp.exp(-v))


def softplus(v):
    return jnp.maximum(v, 0.0) + jnp.log1p(jnp.exp(-jnp.abs(v)))


def pack_body(layer, inner_ref, proj_ref, step_ref, gain_ref, out_ref, packed_ref):
    rows, width = out_ref.shape
    states = proj_ref.shape[1]
    gain = jnp.broadcast_to(gain_ref[layer : layer + 1, :], (8, rows)).T[:, 0:1]
    step = step_ref[...].astype(F32)
    step = jnp.concatenate([step, jnp.zeros((128 - step.shape[0], rows), F32)], axis=0).T
    at = 0
    for piece in (inner_ref[0], inner_ref[1], proj_ref[...], step):
        end = at + piece.shape[1]
        packed_ref[:, at:end] = (piece.astype(F32) * gain).astype(BF)
        at = end
    packed_ref[:, at:] = out_ref[...]


def pack(layer, inner, proj, step, gain, out):
    rows, width = inner.shape[2:]
    cols = 2 * width + proj.shape[2] + 128 + out.shape[2]

    def layer_of(shape):
        return pl.BlockSpec((None,) + shape[1:], lambda i: (layer,) + (0,) * (len(shape) - 1))

    return pl.pallas_call(
        lambda *refs: pack_body(layer, *refs),
        name="pack%d" % layer,
        grid=(1,),
        in_specs=[
            layer_of(inner.shape),
            layer_of(proj.shape),
            layer_of(step.shape),
            pl.BlockSpec(gain.shape, lambda i: (0, 0)),
            layer_of(out.shape),
        ],
        out_specs=pl.BlockSpec((rows, cols), lambda i: (0, 0)),
        out_shape=jax.ShapeDtypeStruct((rows, cols), BF),
        compiler_params=pltpu.CompilerParams(
            dimension_semantics=("arbitrary",), vmem_limit_bytes=VMEM_BYTES
        ),
    )(inner, proj, step, gain, out)


def route(q, ints_ref, requests):
    owners, ranges = 2 + requests, 2 + 2 * requests
    request = ints_ref[0] + q
    live = (request >= ints_ref[ranges]) & (request < ints_ref[ranges + 1])
    for k in range(ranges + 2, ints_ref.shape[0], 2):
        live = live | ((request >= ints_ref[k]) & (request < ints_ref[k + 1]))
    owner = ints_ref[owners + q]
    rank = jnp.int32(0)
    for other in range(q):
        rank = rank + jnp.where(ints_ref[owners + other] == owner, 1, 0)
    return live, owner, jnp.minimum(rank, SEND_CAP - 1)


def front_body(
    layer,
    ints_ref,
    floats_ref,
    hidden_ref,
    weight_ref,
    inner_kernel_ref,
    proj_kernel_ref,
    norm_gain_ref,
    inner_cache_ref,
    proj_cache_ref,
    state_ref,
    part_ref,
    dx_ref,
    b_ref,
    dec_ref,
    x_pad,
    p_pad,
    misc_ref,
):
    requests, heads, head_size, state_size = state_ref.shape
    tokens = requests * S
    width = heads * head_size
    model_width = ROWS * hidden_ref.shape[2]
    block_tokens = hidden_ref.shape[1]
    in_cols = 2 * width + 2 * state_size + 128
    lane = lax.broadcasted_iota(jnp.int32, (1, 128), 1)

    def spread(pieces):
        return jnp.concatenate(
            [jnp.where(lane < 64, pieces[2 * k], pieces[2 * k + 1]) for k in range(heads // 2)],
            axis=1,
        )

    total = jnp.zeros((tokens, in_cols), F32)
    squares = jnp.zeros((tokens, 128), F32)
    for r in range(ROWS):
        rows_r = jnp.concatenate([hidden_ref[r], hidden_ref[ROWS + r]], axis=0)
        total = total + jnp.dot(rows_r, weight_ref[r, :, :in_cols], preferred_element_type=F32)
        wide = rows_r.astype(F32)
        wide = wide * wide
        squares = squares + wide[:, :128] + wide[:, 128:]
    inverse = lax.rsqrt(jnp.sum(squares, axis=1, keepdims=True) / model_width + EPSILON)
    total = total * inverse
    z = total[:, :width]
    x_pad[:, 8:24, :] = total[:, width : 2 * width].reshape(requests, S, width)
    p_pad[:, 8:24, :] = total[:, 2 * width : 2 * width + 2 * state_size].reshape(
        requests, S, 2 * state_size
    )
    x_pad[:, 5:8, :] = inner_cache_ref[...].astype(F32)
    p_pad[:, 5:8, :] = proj_cache_ref[...].astype(F32)
    conv_x = x_pad[:, 5 : 5 + S, :] * inner_kernel_ref[0:1, :]
    conv_p = p_pad[:, 5 : 5 + S, :] * proj_kernel_ref[0:1, :]
    for i in range(1, 4):
        conv_x = conv_x + x_pad[:, 5 + i : 5 + i + S, :] * inner_kernel_ref[i : i + 1, :]
        conv_p = conv_p + p_pad[:, 5 + i : 5 + i + S, :] * proj_kernel_ref[i : i + 1, :]
    x_conv = silu(conv_x).reshape(tokens, width)
    p_conv = silu(conv_p).reshape(tokens, 2 * state_size)
    b_conv = p_conv[:, :state_size]
    c_conv = p_conv[:, state_size:].astype(BF)
    b_ref[...] = b_conv
    step_raw = total[:, 2 * width + 2 * state_size :]
    t_now = lax.broadcasted_iota(jnp.int32, (tokens, tokens), 0)
    t_then = lax.broadcasted_iota(jnp.int32, (tokens, tokens), 1)
    causal = (t_now // S == t_then // S) & (t_then <= t_now)
    lower = causal.astype(F32)
    scores = lax.dot_general(
        c_conv, b_conv.astype(BF), (((1,), (1,)), ((), ())), preferred_element_type=F32
    )
    deltas = []
    sums_log = []
    mixes = []
    for h in range(heads):
        raw = jnp.broadcast_to(step_raw[:, h : h + 1], (tokens, 128))
        delta = softplus(raw + floats_ref[layer, h])
        rate = jnp.exp(jnp.full((1, 128), floats_ref[layer, heads + h], F32))
        log_decay = -delta * rate
        dec_ref[:, h * 128 : (h + 1) * 128] = jnp.exp(log_decay)
        cum = jnp.dot(
            lower, log_decay, precision=lax.Precision.HIGHEST, preferred_element_type=F32
        )
        gap = jnp.where(causal, cum - cum.T, 0.0)
        mixes.append((jnp.where(causal, jnp.exp(gap), 0.0) * scores).astype(BF))
        deltas.append(delta)
        sums_log.append(cum)
    dx = x_conv * spread(deltas)
    cum_all = spread(sums_log)
    grown = jnp.exp(cum_all)
    dx_ref[...] = dx
    y_diag = []
    for k in range(heads // 2):
        dx_k = dx[:, 128 * k : 128 * (k + 1)].astype(BF)
        first = jnp.dot(mixes[2 * k], dx_k, preferred_element_type=F32)
        second = jnp.dot(mixes[2 * k + 1], dx_k, preferred_element_type=F32)
        y_diag.append(jnp.where(lane < 64, first, second))
    y_off = []
    for q in range(requests):
        flat = state_ref[q].reshape(width, state_size).astype(BF)
        y_off.append(
            lax.dot_general(
                c_conv[q * S : (q + 1) * S, :], flat, (((1,), (1,)), ((), ())),
                preferred_element_type=F32,
            )
        )
    skip = spread([jnp.full((1, 128), floats_ref[layer, 2 * heads + h], F32) for h in range(heads)])
    y = (
        jnp.concatenate(y_diag, axis=1)
        + grown * jnp.concatenate(y_off, axis=0)
        + skip * x_conv
    )
    g = y * silu(z)
    yg = (g * norm_gain_ref[layer : layer + 1, :]).astype(BF)
    g2 = (g * g).astype(BF)
    ones = jnp.ones((SUM_ROWS, width), BF)
    misc_row = block_tokens + SEND_CAP * S
    line = lax.broadcasted_iota(jnp.int32, (SUM_ROWS, 1), 0)
    part_ref[:, block_tokens:misc_row, :] = jnp.zeros((COLS, SEND_CAP * S, width), BF)
    nothing = jnp.zeros((SUM_ROWS, width - block_tokens), F32)
    for b in range(2):
        sums = lax.dot_general(
            ones,
            g2[b * block_tokens : (b + 1) * block_tokens, :],
            (((1,), (1,)), ((), ())),
            preferred_element_type=F32,
        )
        sums = jnp.where(line == 0, jnp.concatenate([sums, nothing], axis=1), 0.0)
        for r in range(ROWS):
            misc_ref[b * ROWS + r] = sums
    step = lax.broadcasted_iota(jnp.int32, (S, 1), 0)
    column = ints_ref[1]
    for q in range(requests):
        live, owner, rank = route(q, ints_ref, requests)
        taken = ints_ref[2 + q] - 1
        rows = slice(q * S, (q + 1) * S)
        cum_q = cum_all[rows, :]
        cum_end = jnp.sum(jnp.where(step == taken, cum_q, 0.0), axis=0, keepdims=True)
        inside = step <= taken
        weight = jnp.where(inside, jnp.exp(jnp.where(inside, cum_end - cum_q, 0.0)), 0.0)
        scale = jnp.exp(cum_end)
        high = scale.astype(BF).astype(F32)
        low = scale - high
        mine = jnp.sum(jnp.where(step == column, b_conv[rows, :], 0.0), axis=0, keepdims=True)
        mine = jnp.concatenate([mine, jnp.zeros((1, width - state_size), F32)], axis=1)
        at = 1 + 3 * rank
        extra = jnp.where(
            line == at,
            mine,
            jnp.where(line == at + 1, high, jnp.where(line == at + 2, low, 0.0)),
        )
        first = pl.multiple_of(block_tokens + rank * S, S)

        @pl.when(live)
        def _send():
            part_ref[owner, pl.ds(first, S), :] = (dx[rows, :] * weight).astype(BF)
            misc_ref[owner] = misc_ref[owner] + extra

    part_ref[:, misc_row:, :] = misc_ref[...].astype(BF)
    for r in range(ROWS):
        part = jnp.dot(yg, weight_ref[r, :, in_cols:], preferred_element_type=F32).astype(BF)
        for b in range(2):
            part_ref[b * ROWS + r, 0:block_tokens, :] = part[
                b * block_tokens : (b + 1) * block_tokens, :
            ]


def front(layer, ints, floats, hidden, weight, inner_kernel, proj_kernel,
          norm_gain, inner_cache, proj_cache, state):
    layers, requests, heads, head_size, state_size = state.shape
    width = heads * head_size
    tokens = requests * S
    smem = pl.BlockSpec(memory_space=pltpu.SMEM)

    def whole(shape):
        return pl.BlockSpec(shape, lambda i: (0,) * len(shape))

    def layer_of(shape):
        return pl.BlockSpec((None,) + shape[1:], lambda i: (layer,) + (0,) * (len(shape) - 1))

    block_tokens = tokens // 2
    out_shapes = [
        ((COLS, block_tokens + SEND_CAP * S + SUM_ROWS, width), BF),
        ((tokens, width), F32),
        ((tokens, state_size), F32),
        ((tokens, heads * 128), F32),
    ]
    return pl.pallas_call(
        lambda *refs: front_body(layer, *refs),
        name="front%d" % layer,
        grid=(1,),
        in_specs=[
            smem, smem,
            whole(hidden.shape),
            whole(weight.shape),
            layer_of(inner_kernel.shape),
            layer_of(proj_kernel.shape),
            whole(norm_gain.shape),
            layer_of(inner_cache.shape),
            layer_of(proj_cache.shape),
            layer_of(state.shape),
        ],
        out_specs=[whole(shape) for shape, _ in out_shapes],
        out_shape=[jax.ShapeDtypeStruct(shape, kind) for shape, kind in out_shapes],
        scratch_shapes=[
            pltpu.VMEM((requests, 24, width), F32),
            pltpu.VMEM((requests, 24, 2 * state_size), F32),
            pltpu.VMEM((COLS, SUM_ROWS, width), F32),
        ],
        compiler_params=pltpu.CompilerParams(
            dimension_semantics=("arbitrary",), vmem_limit_bytes=VMEM_BYTES
        ),
    )(ints, floats, hidden, weight, inner_kernel, proj_kernel, norm_gain,
      inner_cache, proj_cache, state)


def states_body(dx_ref, b_ref, dec_ref, state_ref, *rest):
    steps_ref = rest[-1]
    heads, head_size, state_size = state_ref.shape
    dx_t = dx_ref[...].T
    for h in range(heads):
        state = state_ref[h]
        columns = dx_t[h * head_size : (h + 1) * head_size, :]
        for t in range(S):
            state = (
                state * dec_ref[t : t + 1, h * 128 : (h + 1) * 128]
                + columns[:, t : t + 1] * b_ref[t : t + 1, :]
            )
            steps_ref[t, h] = state.astype(BF)


def states(layer, dx, b, dec, state, previous):
    layers, requests, heads, head_size, state_size = state.shape
    width = heads * head_size
    in_specs = [
        pl.BlockSpec((S, width), lambda q: (q, 0)),
        pl.BlockSpec((S, state_size), lambda q: (q, 0)),
        pl.BlockSpec((S, heads * 128), lambda q: (q, 0)),
        pl.BlockSpec((None, None, heads, head_size, state_size), lambda q: (layer, q, 0, 0, 0)),
    ]
    operands = [dx, b, dec, state]
    aliases = {}
    if previous is not None:
        in_specs.append(pl.BlockSpec(memory_space=pl.ANY))
        aliases = {len(operands): 0}
        operands.append(previous)
    return pl.pallas_call(
        states_body,
        name="states%d" % layer,
        grid=(requests,),
        in_specs=in_specs,
        out_specs=pl.BlockSpec(
            (None, None, S, heads, head_size, state_size), lambda q: (layer, q, 0, 0, 0, 0)
        ),
        out_shape=jax.ShapeDtypeStruct(
            (layers, requests, S, heads, head_size, state_size), BF
        ),
        input_output_aliases=aliases,
        compiler_params=pltpu.CompilerParams(
            dimension_semantics=("arbitrary",), vmem_limit_bytes=SMALL_VMEM_BYTES
        ),
    )(*operands)


def starts_body(ints_ref, state_ref, send_ref):
    send_ref[...] = jnp.zeros(send_ref.shape, BF)
    layers, requests = state_ref.shape[:2]
    for q in range(requests):
        live, owner, rank = route(q, ints_ref, requests)

        @pl.when(live)
        def _put():
            for layer in range(layers):
                send_ref[owner, layer, rank] = state_ref[layer, q].astype(BF)


def starts(ints, state):
    shape = (COLS, state.shape[0], SEND_CAP) + state.shape[2:]
    return pl.pallas_call(
        starts_body,
        name="starts",
        grid=(1,),
        in_specs=[
            pl.BlockSpec(memory_space=pltpu.SMEM),
            pl.BlockSpec(state.shape, lambda i: (0, 0, 0, 0, 0)),
        ],
        out_specs=pl.BlockSpec(shape, lambda i: (0, 0, 0, 0, 0, 0)),
        out_shape=jax.ShapeDtypeStruct(shape, BF),
        compiler_params=pltpu.CompilerParams(
            dimension_semantics=("arbitrary",), vmem_limit_bytes=VMEM_BYTES
        ),
    )(ints, state)


def owned_body(layer, begun_ref, received_ref, *rest):
    out_ref, starts_ref, stage, b_s, sems, in_sems = rest[-6:]
    cols, slots, heads, head_size, state_size = starts_ref.shape
    group = 4
    arrivals = [
        pltpu.make_async_copy(
            begun_ref.at[pl.ds(i * group, group), layer],
            starts_ref.at[pl.ds(i * group, group)],
            in_sems.at[i],
        )
        for i in range(cols // group)
    ]
    for arrival in arrivals:
        arrival.start()
    dx_rows = slots * S
    misc_at = received_ref.shape[1] - SUM_ROWS
    dx_at = misc_at - dx_rows
    b_s[...] = jnp.zeros(b_s.shape, F32)
    scales = []
    for c in range(cols):
        lines = received_ref[c, misc_at:, :].astype(F32)
        for slot in range(slots):
            row = 1 + 3 * slot
            b_s[
                slot * S + c : slot * S + c + 1, slot * state_size : (slot + 1) * state_size
            ] = lines[row : row + 1, 0:state_size]
            scales.append(lines[row + 1 : row + 2, :] + lines[row + 2 : row + 3, :])
    b_all = b_s[...].astype(BF)
    copies = []
    for i in range(cols // group):
        dx = jnp.concatenate(
            [received_ref[i * group + g, dx_at:misc_at, :] for g in range(group)], axis=1
        )
        added = lax.dot_general(dx, b_all, (((0,), (0,)), ((), ())), preferred_element_type=F32)
        arrivals[i].wait()
        for slot in range(slots):
            for g in range(group):
                c = i * group + g
                for h in range(heads):
                    scale = scales[c * slots + slot][:, h * head_size : h * head_size + 1]
                    at = (g * heads + h) * head_size
                    stage[slot, c * heads + h] = (
                        starts_ref[c, slot, h].astype(F32) * scale
                        + added[at : at + head_size, slot * state_size : (slot + 1) * state_size]
                    ).astype(BF)
            span = pl.ds(i * group * heads, group * heads)
            copies.append(
                pltpu.make_async_copy(
                    stage.at[slot, span],
                    out_ref.at[slot, layer, span],
                    sems.at[i * slots + slot],
                )
            )
            copies[-1].start()
    for copy in copies:
        copy.wait()


def owned_states(layer, state, begun, received, previous):
    layers, _, heads, head_size, state_size = state.shape
    resident = pl.BlockSpec(memory_space=pltpu.VMEM)
    anywhere = pl.BlockSpec(memory_space=pl.ANY)
    in_specs = [anywhere, resident]
    operands = [begun, received]
    aliases = {}
    if previous is not None:
        in_specs.append(anywhere)
        aliases = {len(operands): 0}
        operands.append(previous)
    all_heads = COLS * heads
    return pl.pallas_call(
        lambda *refs: owned_body(layer, *refs),
        name="owned%d" % layer,
        in_specs=in_specs,
        out_specs=anywhere,
        out_shape=jax.ShapeDtypeStruct(
            (SEND_CAP, layers, all_heads, head_size, state_size), BF
        ),
        scratch_shapes=[
            pltpu.VMEM((COLS, SEND_CAP, heads, head_size, state_size), BF),
            pltpu.VMEM((SEND_CAP, all_heads, head_size, state_size), BF),
            pltpu.VMEM((SEND_CAP * S, SEND_CAP * state_size), F32),
            pltpu.SemaphoreType.DMA((SEND_CAP * COLS // 4,)),
            pltpu.SemaphoreType.DMA((COLS // 4,)),
        ],
        input_output_aliases=aliases,
        compiler_params=pltpu.CompilerParams(vmem_limit_bytes=SMALL_VMEM_BYTES),
    )(*operands)


def update_body(inner_width, part_ref, sums_ref, hidden_ref, *outs):
    rows = hidden_ref.shape[0]
    total = part_ref[0].astype(F32)
    sums = sums_ref[0, :, 0:128].astype(F32)
    for c in range(1, COLS):
        total = total + part_ref[c].astype(F32)
        sums = sums + sums_ref[c, :, 0:128].astype(F32)
    scale = lax.rsqrt(sums.T[:rows, 0:1] / inner_width + EPSILON)
    fresh = (hidden_ref[...].astype(F32) + total * scale).astype(BF)
    outs[0][...] = fresh
    for spread_ref in outs[1:]:
        for c in range(COLS):
            spread_ref[c] = fresh


def update(inner_width, received, hidden, spread):
    rows, lanes = hidden.shape
    shapes = [hidden.shape] + ([(COLS,) + hidden.shape] if spread else [])
    sums_at = (rows + SEND_CAP * S) // SUM_ROWS

    def whole(shape):
        return pl.BlockSpec(shape, lambda i: (0,) * len(shape))

    return pl.pallas_call(
        lambda *refs: update_body(inner_width, *refs),
        name="update_spread" if spread else "update_last",
        grid=(1,),
        in_specs=[
            pl.BlockSpec((COLS, rows, lanes), lambda i: (0, 0, 0)),
            pl.BlockSpec((COLS, SUM_ROWS, lanes), lambda i: (0, sums_at, 0)),
            whole(hidden.shape),
        ],
        out_specs=[whole(shape) for shape in shapes],
        out_shape=[jax.ShapeDtypeStruct(shape, BF) for shape in shapes],
        compiler_params=pltpu.CompilerParams(
            dimension_semantics=("arbitrary",), vmem_limit_bytes=SMALL_VMEM_BYTES
        ),
    )(received, received, hidden)


def swap(x):
    return lax.all_to_all(x, "col", 0, 0, tiled=True)


def local(
    hidden_states,
    input_gain,
    inner_weight,
    proj_weight,
    step_weight,
    inner_kernel,
    proj_kernel,
    step_bias,
    decay_log,
    skip_gain,
    norm_gain,
    out_weight,
    inner_cache,
    proj_cache,
    state_cache,
    accepted,
    owners,
    tenant_ranges,
):
    layer_count = inner_weight.shape[0]
    inner_local = inner_weight.shape[3]
    heads_local = step_weight.shape[2]
    requests_local = state_cache.shape[1]
    inner_width = inner_local * COLS
    base = (lax.axis_index("row") * requests_local).astype(jnp.int32).reshape(1)
    column = lax.axis_index("col").astype(jnp.int32).reshape(1)
    ints = jnp.concatenate([base, column, accepted, owners, tenant_ranges.reshape(-1)])
    floats = jnp.concatenate([step_bias, decay_log, skip_gain], axis=1)

    there = []
    for r in range(ROWS):
        for c in range(COLS):
            there.append((r * COLS + c, (c // 2) * COLS + (c % 2) * ROWS + r))
    back = [(b, a) for a, b in there]

    block = lax.ppermute(hidden_states, ("row", "col"), there)
    raw = (
        jnp.transpose(inner_weight, (0, 2, 1, 3)),
        proj_weight,
        jnp.transpose(step_weight, (0, 2, 1)),
        input_gain,
        out_weight,
    )
    first, block = lax.optimization_barrier((pack(0, *raw), block))
    weights = [lax.all_gather(first, "row", axis=0)]
    everything = swap(jnp.broadcast_to(block[None], (COLS,) + block.shape))
    send = starts(ints, state_cache)
    send, raw = lax.optimization_barrier((send, raw))
    second = pack(1, *raw)
    everything, send, second = lax.optimization_barrier((everything, send, second))
    weights.append(lax.all_gather(second, "row", axis=0))
    begun = swap(send)

    steps = None
    owned = None
    for layer in range(layer_count):
        last = layer == layer_count - 1
        part, dx, b_conv, decay = front(
            layer, ints, floats, everything, weights[layer], inner_kernel, proj_kernel,
            norm_gain, inner_cache, proj_cache, state_cache,
        )
        part, begun = lax.optimization_barrier((part, begun))
        received = swap(part)
        steps = states(layer, dx, b_conv, decay, state_cache, steps)
        received, steps = lax.optimization_barrier((received, steps))
        fresh = update(inner_width, received, block, not last)
        owned = owned_states(layer, state_cache, begun, received, owned)
        if not last:
            block = fresh[0]
            everything = swap(fresh[1])
            everything, owned = lax.optimization_barrier((everything, owned))
    hidden = lax.ppermute(fresh[0], ("row", "col"), back)
    owned_block = owned[None, None]
    return (hidden, steps, owned_block)


def solution(mesh):
    placed = (
        P("col", "row"),
        P(None, "row"),
        P(None, "row", None, "col"),
        P(None, "row", None),
        P(None, "row", "col"),
        P(None, None, "col"),
        P(),
        P(None, "col"),
        P(None, "col"),
        P(None, "col"),
        P(None, "col"),
        P(None, "col", "row"),
        P(None, "row", None, "col"),
        P(None, "row", None, None),
        P(None, "row", "col", None, None),
        P("row"),
        P("row"),
        P(),
    )
    return jax.shard_map(
        local,
        mesh=mesh,
        in_specs=placed,
        out_specs=(
            P("col", "row"),
            P(None, "row", None, "col", None, None),
            P("row", "col", None, None, None, None, None),
        ),
        check_vma=False,
    )
```

```python
import jax
import jax.numpy as jnp
from jax import lax
from jax.experimental import pallas as pl
from jax.experimental.pallas import tpu as pltpu
from jax.sharding import PartitionSpec as P

S = 16
SEND_CAP = 2
EPSILON = 1e-05
ROWS = 8
COLS = 16
BF = jnp.bfloat16
F32 = jnp.float32
SUM_ROWS = 8
VMEM_BYTES = 58 * 1024 * 1024
SMALL_VMEM_BYTES = 12 * 1024 * 1024


def silu(v):
    return v / (1.0 + jnp.exp(-v))


def softplus(v):
    return jnp.maximum(v, 0.0) + jnp.log1p(jnp.exp(-jnp.abs(v)))


def pack_body(layer, inner_ref, proj_ref, step_ref, gain_ref, out_ref, packed_ref):
    rows, width = out_ref.shape
    states = proj_ref.shape[1]
    gain = jnp.broadcast_to(gain_ref[layer : layer + 1, :], (8, rows)).T[:, 0:1]
    step = step_ref[...].astype(F32)
    step = jnp.concatenate([step, jnp.zeros((128 - step.shape[0], rows), F32)], axis=0).T
    at = 0
    for piece in (inner_ref[0], inner_ref[1], proj_ref[...], step):
        end = at + piece.shape[1]
        packed_ref[:, at:end] = (piece.astype(F32) * gain).astype(BF)
        at = end
    packed_ref[:, at:] = out_ref[...]


def pack(layer, inner, proj, step, gain, out):
    planes = jnp.transpose(inner[layer], (1, 0, 2))
    rows, width = planes.shape[1:]
    cols = 2 * width + proj.shape[2] + 128 + out.shape[2]

    def layer_of(shape):
        return pl.BlockSpec((None,) + shape[1:], lambda i: (layer,) + (0,) * (len(shape) - 1))

    return pl.pallas_call(
        lambda *refs: pack_body(layer, *refs),
        name="pack%d" % layer,
        grid=(1,),
        in_specs=[
            pl.BlockSpec(planes.shape, lambda i: (0, 0, 0)),
            layer_of(proj.shape),
            layer_of(step.shape),
            pl.BlockSpec(gain.shape, lambda i: (0, 0)),
            layer_of(out.shape),
        ],
        out_specs=pl.BlockSpec((rows, cols), lambda i: (0, 0)),
        out_shape=jax.ShapeDtypeStruct((rows, cols), BF),
        compiler_params=pltpu.CompilerParams(
            dimension_semantics=("arbitrary",), vmem_limit_bytes=VMEM_BYTES
        ),
    )(planes, proj, step, gain, out)


def route(q, ints_ref, requests):
    owners, ranges = 2 + requests, 2 + 2 * requests
    request = ints_ref[0] + q
    live = (request >= ints_ref[ranges]) & (request < ints_ref[ranges + 1])
    for k in range(ranges + 2, ints_ref.shape[0], 2):
        live = live | ((request >= ints_ref[k]) & (request < ints_ref[k + 1]))
    owner = ints_ref[owners + q]
    rank = jnp.int32(0)
    for other in range(q):
        rank = rank + jnp.where(ints_ref[owners + other] == owner, 1, 0)
    return live, owner, jnp.minimum(rank, SEND_CAP - 1)


def front_body(
    layer,
    ints_ref,
    floats_ref,
    hidden_ref,
    weight_ref,
    inner_kernel_ref,
    proj_kernel_ref,
    norm_gain_ref,
    inner_cache_ref,
    proj_cache_ref,
    state_ref,
    part_ref,
    dx_ref,
    b_ref,
    dec_ref,
    x_pad,
    p_pad,
    misc_ref,
):
    requests, heads, head_size, state_size = state_ref.shape
    tokens = requests * S
    width = heads * head_size
    model_width = ROWS * hidden_ref.shape[2]
    block_tokens = hidden_ref.shape[1]
    in_cols = 2 * width + 2 * state_size + 128
    lane = lax.broadcasted_iota(jnp.int32, (1, 128), 1)

    def spread(pieces):
        return jnp.concatenate(
            [jnp.where(lane < 64, pieces[2 * k], pieces[2 * k + 1]) for k in range(heads // 2)],
            axis=1,
        )

    total = jnp.zeros((tokens, in_cols), F32)
    squares = jnp.zeros((tokens, 128), F32)
    for r in range(ROWS):
        rows_r = jnp.concatenate([hidden_ref[r], hidden_ref[ROWS + r]], axis=0)
        total = total + jnp.dot(rows_r, weight_ref[r, :, :in_cols], preferred_element_type=F32)
        wide = rows_r.astype(F32)
        wide = wide * wide
        squares = squares + wide[:, :128] + wide[:, 128:]
    inverse = lax.rsqrt(jnp.sum(squares, axis=1, keepdims=True) / model_width + EPSILON)
    total = total * inverse
    z = total[:, :width]
    x_pad[:, 8:24, :] = total[:, width : 2 * width].reshape(requests, S, width)
    p_pad[:, 8:24, :] = total[:, 2 * width : 2 * width + 2 * state_size].reshape(
        requests, S, 2 * state_size
    )
    x_pad[:, 5:8, :] = inner_cache_ref[...].astype(F32)
    p_pad[:, 5:8, :] = proj_cache_ref[...].astype(F32)
    conv_x = x_pad[:, 5 : 5 + S, :] * inner_kernel_ref[0:1, :]
    conv_p = p_pad[:, 5 : 5 + S, :] * proj_kernel_ref[0:1, :]
    for i in range(1, 4):
        conv_x = conv_x + x_pad[:, 5 + i : 5 + i + S, :] * inner_kernel_ref[i : i + 1, :]
        conv_p = conv_p + p_pad[:, 5 + i : 5 + i + S, :] * proj_kernel_ref[i : i + 1, :]
    x_conv = silu(conv_x).reshape(tokens, width)
    p_conv = silu(conv_p).reshape(tokens, 2 * state_size)
    b_conv = p_conv[:, :state_size]
    c_conv = p_conv[:, state_size:].astype(BF)
    b_ref[...] = b_conv
    step_raw = total[:, 2 * width + 2 * state_size :]
    t_now = lax.broadcasted_iota(jnp.int32, (tokens, tokens), 0)
    t_then = lax.broadcasted_iota(jnp.int32, (tokens, tokens), 1)
    causal = (t_now // S == t_then // S) & (t_then <= t_now)
    lower = causal.astype(F32)
    scores = lax.dot_general(
        c_conv, b_conv.astype(BF), (((1,), (1,)), ((), ())), preferred_element_type=F32
    )
    deltas = []
    sums_log = []
    mixes = []
    for h in range(heads):
        raw = jnp.broadcast_to(step_raw[:, h : h + 1], (tokens, 128))
        delta = softplus(raw + floats_ref[layer, h])
        rate = jnp.exp(jnp.full((1, 128), floats_ref[layer, heads + h], F32))
        log_decay = -delta * rate
        dec_ref[:, h * 128 : (h + 1) * 128] = jnp.exp(log_decay)
        cum = jnp.dot(
            lower, log_decay, precision=lax.Precision.HIGHEST, preferred_element_type=F32
        )
        gap = jnp.where(causal, cum - cum.T, 0.0)
        mixes.append((jnp.where(causal, jnp.exp(gap), 0.0) * scores).astype(BF))
        deltas.append(delta)
        sums_log.append(cum)
    dx = x_conv * spread(deltas)
    cum_all = spread(sums_log)
    grown = jnp.exp(cum_all)
    dx_ref[...] = dx
    y_diag = []
    for k in range(heads // 2):
        dx_k = dx[:, 128 * k : 128 * (k + 1)].astype(BF)
        first = jnp.dot(mixes[2 * k], dx_k, preferred_element_type=F32)
        second = jnp.dot(mixes[2 * k + 1], dx_k, preferred_element_type=F32)
        y_diag.append(jnp.where(lane < 64, first, second))
    y_off = []
    for q in range(requests):
        flat = state_ref[q].reshape(width, state_size).astype(BF)
        y_off.append(
            lax.dot_general(
                c_conv[q * S : (q + 1) * S, :], flat, (((1,), (1,)), ((), ())),
                preferred_element_type=F32,
            )
        )
    skip = spread([jnp.full((1, 128), floats_ref[layer, 2 * heads + h], F32) for h in range(heads)])
    y = (
        jnp.concatenate(y_diag, axis=1)
        + grown * jnp.concatenate(y_off, axis=0)
        + skip * x_conv
    )
    g = y * silu(z)
    yg = (g * norm_gain_ref[layer : layer + 1, :]).astype(BF)
    g2 = (g * g).astype(BF)
    ones = jnp.ones((SUM_ROWS, width), BF)
    misc_row = block_tokens + SEND_CAP * S
    line = lax.broadcasted_iota(jnp.int32, (SUM_ROWS, 1), 0)
    part_ref[:, block_tokens:misc_row, :] = jnp.zeros((COLS, SEND_CAP * S, width), BF)
    nothing = jnp.zeros((SUM_ROWS, width - block_tokens), F32)
    for b in range(2):
        sums = lax.dot_general(
            ones,
            g2[b * block_tokens : (b + 1) * block_tokens, :],
            (((1,), (1,)), ((), ())),
            preferred_element_type=F32,
        )
        sums = jnp.where(line == 0, jnp.concatenate([sums, nothing], axis=1), 0.0)
        for r in range(ROWS):
            misc_ref[b * ROWS + r] = sums
    step = lax.broadcasted_iota(jnp.int32, (S, 1), 0)
    column = ints_ref[1]
    for q in range(requests):
        live, owner, rank = route(q, ints_ref, requests)
        taken = ints_ref[2 + q] - 1
        rows = slice(q * S, (q + 1) * S)
        cum_q = cum_all[rows, :]
        cum_end = jnp.sum(jnp.where(step == taken, cum_q, 0.0), axis=0, keepdims=True)
        inside = step <= taken
        weight = jnp.where(inside, jnp.exp(jnp.where(inside, cum_end - cum_q, 0.0)), 0.0)
        scale = jnp.exp(cum_end)
        high = scale.astype(BF).astype(F32)
        low = scale - high
        mine = jnp.sum(jnp.where(step == column, b_conv[rows, :], 0.0), axis=0, keepdims=True)
        mine = jnp.concatenate([mine, jnp.zeros((1, width - state_size), F32)], axis=1)
        at = 1 + 3 * rank
        extra = jnp.where(
            line == at,
            mine,
            jnp.where(line == at + 1, high, jnp.where(line == at + 2, low, 0.0)),
        )
        first = pl.multiple_of(block_tokens + rank * S, S)

        @pl.when(live)
        def _send():
            part_ref[owner, pl.ds(first, S), :] = (dx[rows, :] * weight).astype(BF)
            misc_ref[owner] = misc_ref[owner] + extra

    part_ref[:, misc_row:, :] = misc_ref[...].astype(BF)
    for r in range(ROWS):
        part = jnp.dot(yg, weight_ref[r, :, in_cols:], preferred_element_type=F32).astype(BF)
        for b in range(2):
            part_ref[b * ROWS + r, 0:block_tokens, :] = part[
                b * block_tokens : (b + 1) * block_tokens, :
            ]


def front(layer, ints, floats, hidden, weight, inner_kernel, proj_kernel,
          norm_gain, inner_cache, proj_cache, state):
    layers, requests, heads, head_size, state_size = state.shape
    width = heads * head_size
    tokens = requests * S
    smem = pl.BlockSpec(memory_space=pltpu.SMEM)

    def whole(shape):
        return pl.BlockSpec(shape, lambda i: (0,) * len(shape))

    def layer_of(shape):
        return pl.BlockSpec((None,) + shape[1:], lambda i: (layer,) + (0,) * (len(shape) - 1))

    block_tokens = tokens // 2
    out_shapes = [
        ((COLS, block_tokens + SEND_CAP * S + SUM_ROWS, width), BF),
        ((tokens, width), F32),
        ((tokens, state_size), F32),
        ((tokens, heads * 128), F32),
    ]
    return pl.pallas_call(
        lambda *refs: front_body(layer, *refs),
        name="front%d" % layer,
        grid=(1,),
        in_specs=[
            smem, smem,
            whole(hidden.shape),
            whole(weight.shape),
            layer_of(inner_kernel.shape),
            layer_of(proj_kernel.shape),
            whole(norm_gain.shape),
            layer_of(inner_cache.shape),
            layer_of(proj_cache.shape),
            layer_of(state.shape),
        ],
        out_specs=[whole(shape) for shape, _ in out_shapes],
        out_shape=[jax.ShapeDtypeStruct(shape, kind) for shape, kind in out_shapes],
        scratch_shapes=[
            pltpu.VMEM((requests, 24, width), F32),
            pltpu.VMEM((requests, 24, 2 * state_size), F32),
            pltpu.VMEM((COLS, SUM_ROWS, width), F32),
        ],
        compiler_params=pltpu.CompilerParams(
            dimension_semantics=("arbitrary",), vmem_limit_bytes=VMEM_BYTES
        ),
    )(ints, floats, hidden, weight, inner_kernel, proj_kernel, norm_gain,
      inner_cache, proj_cache, state)


def states_body(dx_ref, b_ref, dec_ref, state_ref, *rest):
    steps_ref = rest[-1]
    heads, head_size, state_size = state_ref.shape
    dx_t = dx_ref[...].T
    for h in range(heads):
        state = state_ref[h]
        columns = dx_t[h * head_size : (h + 1) * head_size, :]
        for t in range(S):
            state = (
                state * dec_ref[t : t + 1, h * 128 : (h + 1) * 128]
                + columns[:, t : t + 1] * b_ref[t : t + 1, :]
            )
            steps_ref[t, h] = state.astype(BF)


def states(layer, dx, b, dec, state, previous):
    layers, requests, heads, head_size, state_size = state.shape
    width = heads * head_size
    in_specs = [
        pl.BlockSpec((S, width), lambda q: (q, 0)),
        pl.BlockSpec((S, state_size), lambda q: (q, 0)),
        pl.BlockSpec((S, heads * 128), lambda q: (q, 0)),
        pl.BlockSpec((None, None, heads, head_size, state_size), lambda q: (layer, q, 0, 0, 0)),
    ]
    operands = [dx, b, dec, state]
    aliases = {}
    if previous is not None:
        in_specs.append(pl.BlockSpec(memory_space=pl.ANY))
        aliases = {len(operands): 0}
        operands.append(previous)
    return pl.pallas_call(
        states_body,
        name="states%d" % layer,
        grid=(requests,),
        in_specs=in_specs,
        out_specs=pl.BlockSpec(
            (None, None, S, heads, head_size, state_size), lambda q: (layer, q, 0, 0, 0, 0)
        ),
        out_shape=jax.ShapeDtypeStruct(
            (layers, requests, S, heads, head_size, state_size), BF
        ),
        input_output_aliases=aliases,
        compiler_params=pltpu.CompilerParams(
            dimension_semantics=("arbitrary",), vmem_limit_bytes=SMALL_VMEM_BYTES
        ),
    )(*operands)


def starts_body(ints_ref, state_ref, send_ref):
    send_ref[...] = jnp.zeros(send_ref.shape, BF)
    requests = state_ref.shape[0]
    for q in range(requests):
        live, owner, rank = route(q, ints_ref, requests)

        @pl.when(live)
        def _put():
            send_ref[owner, rank] = state_ref[q].astype(BF)


def starts(layer, ints, state):
    shape = (COLS, SEND_CAP) + state.shape[2:]
    return pl.pallas_call(
        starts_body,
        name="starts%d" % layer,
        grid=(1,),
        in_specs=[
            pl.BlockSpec(memory_space=pltpu.SMEM),
            pl.BlockSpec((None,) + state.shape[1:], lambda i: (layer, 0, 0, 0, 0)),
        ],
        out_specs=pl.BlockSpec(shape, lambda i: (0, 0, 0, 0, 0)),
        out_shape=jax.ShapeDtypeStruct(shape, BF),
        compiler_params=pltpu.CompilerParams(
            dimension_semantics=("arbitrary",), vmem_limit_bytes=VMEM_BYTES
        ),
    )(ints, state)


def owned_body(layer, starts_ref, received_ref, *rest):
    out_ref, stage, b_s, sems = rest[-4:]
    cols, slots, heads, head_size, state_size = starts_ref.shape
    group = 4
    dx_rows = slots * S
    misc_at = received_ref.shape[1] - SUM_ROWS
    dx_at = misc_at - dx_rows
    b_s[...] = jnp.zeros(b_s.shape, F32)
    scales = []
    for c in range(cols):
        lines = received_ref[c, misc_at:, :].astype(F32)
        for slot in range(slots):
            row = 1 + 3 * slot
            b_s[
                slot * S + c : slot * S + c + 1, slot * state_size : (slot + 1) * state_size
            ] = lines[row : row + 1, 0:state_size]
            scales.append(lines[row + 1 : row + 2, :] + lines[row + 2 : row + 3, :])
    b_all = b_s[...].astype(BF)
    copies = []
    for i in range(cols // group):
        dx = jnp.concatenate(
            [received_ref[i * group + g, dx_at:misc_at, :] for g in range(group)], axis=1
        )
        added = lax.dot_general(dx, b_all, (((0,), (0,)), ((), ())), preferred_element_type=F32)
        for slot in range(slots):
            for g in range(group):
                c = i * group + g
                for h in range(heads):
                    scale = scales[c * slots + slot][:, h * head_size : h * head_size + 1]
                    at = (g * heads + h) * head_size
                    stage[slot, c * heads + h] = (
                        starts_ref[c, slot, h].astype(F32) * scale
                        + added[at : at + head_size, slot * state_size : (slot + 1) * state_size]
                    ).astype(BF)
            span = pl.ds(i * group * heads, group * heads)
            copies.append(
                pltpu.make_async_copy(
                    stage.at[slot, span],
                    out_ref.at[slot, layer, span],
                    sems.at[i * slots + slot],
                )
            )
            copies[-1].start()
    for copy in copies:
        copy.wait()


def owned_states(layer, state, begun, received, previous):
    layers, _, heads, head_size, state_size = state.shape
    resident = pl.BlockSpec(memory_space=pltpu.VMEM)
    anywhere = pl.BlockSpec(memory_space=pl.ANY)
    in_specs = [resident, resident]
    operands = [begun, received]
    aliases = {}
    if previous is not None:
        in_specs.append(anywhere)
        aliases = {len(operands): 0}
        operands.append(previous)
    all_heads = COLS * heads
    return pl.pallas_call(
        lambda *refs: owned_body(layer, *refs),
        name="owned%d" % layer,
        in_specs=in_specs,
        out_specs=anywhere,
        out_shape=jax.ShapeDtypeStruct(
            (SEND_CAP, layers, all_heads, head_size, state_size), BF
        ),
        scratch_shapes=[
            pltpu.VMEM((SEND_CAP, all_heads, head_size, state_size), BF),
            pltpu.VMEM((SEND_CAP * S, SEND_CAP * state_size), F32),
            pltpu.SemaphoreType.DMA((SEND_CAP * COLS // 4,)),
        ],
        input_output_aliases=aliases,
        compiler_params=pltpu.CompilerParams(vmem_limit_bytes=SMALL_VMEM_BYTES),
    )(*operands)


def update_body(inner_width, part_ref, sums_ref, hidden_ref, *outs):
    rows = hidden_ref.shape[0]
    total = part_ref[0].astype(F32)
    sums = sums_ref[0, :, 0:128].astype(F32)
    for c in range(1, COLS):
        total = total + part_ref[c].astype(F32)
        sums = sums + sums_ref[c, :, 0:128].astype(F32)
    scale = lax.rsqrt(sums.T[:rows, 0:1] / inner_width + EPSILON)
    fresh = (hidden_ref[...].astype(F32) + total * scale).astype(BF)
    outs[0][...] = fresh
    for spread_ref in outs[1:]:
        for c in range(COLS):
            spread_ref[c] = fresh


def update(inner_width, received, hidden, spread):
    rows, lanes = hidden.shape
    shapes = [hidden.shape] + ([(COLS,) + hidden.shape] if spread else [])
    sums_at = (rows + SEND_CAP * S) // SUM_ROWS

    def whole(shape):
        return pl.BlockSpec(shape, lambda i: (0,) * len(shape))

    return pl.pallas_call(
        lambda *refs: update_body(inner_width, *refs),
        name="update_spread" if spread else "update_last",
        grid=(1,),
        in_specs=[
            pl.BlockSpec((COLS, rows, lanes), lambda i: (0, 0, 0)),
            pl.BlockSpec((COLS, SUM_ROWS, lanes), lambda i: (0, sums_at, 0)),
            whole(hidden.shape),
        ],
        out_specs=[whole(shape) for shape in shapes],
        out_shape=[jax.ShapeDtypeStruct(shape, BF) for shape in shapes],
        compiler_params=pltpu.CompilerParams(
            dimension_semantics=("arbitrary",), vmem_limit_bytes=SMALL_VMEM_BYTES
        ),
    )(received, received, hidden)


def swap(x):
    return lax.all_to_all(x, "col", 0, 0, tiled=True)


def local(
    hidden_states,
    input_gain,
    inner_weight,
    proj_weight,
    step_weight,
    inner_kernel,
    proj_kernel,
    step_bias,
    decay_log,
    skip_gain,
    norm_gain,
    out_weight,
    inner_cache,
    proj_cache,
    state_cache,
    accepted,
    owners,
    tenant_ranges,
):
    layer_count = inner_weight.shape[0]
    inner_local = inner_weight.shape[3]
    heads_local = step_weight.shape[2]
    requests_local = state_cache.shape[1]
    inner_width = inner_local * COLS
    base = (lax.axis_index("row") * requests_local).astype(jnp.int32).reshape(1)
    column = lax.axis_index("col").astype(jnp.int32).reshape(1)
    ints = jnp.concatenate([base, column, accepted, owners, tenant_ranges.reshape(-1)])
    floats = jnp.concatenate([step_bias, decay_log, skip_gain], axis=1)

    there = []
    for r in range(ROWS):
        for c in range(COLS):
            there.append((r * COLS + c, (c // 2) * COLS + (c % 2) * ROWS + r))
    back = [(b, a) for a, b in there]

    block = lax.ppermute(hidden_states, ("row", "col"), there)
    raw = (
        inner_weight,
        proj_weight,
        jnp.transpose(step_weight, (0, 2, 1)),
        input_gain,
        out_weight,
    )
    first, block = lax.optimization_barrier((pack(0, *raw), block))
    weights = [lax.all_gather(first, "row", axis=0)]
    everything = swap(jnp.broadcast_to(block[None], (COLS,) + block.shape))
    sends = [starts(layer, ints, state_cache) for layer in range(layer_count)]
    sends, raw = lax.optimization_barrier((sends, raw))
    second = pack(1, *raw)
    everything, sends, second = lax.optimization_barrier((everything, sends, second))
    weights.append(lax.all_gather(second, "row", axis=0))
    begun = swap(sends[0])
    send = sends[1]

    steps = None
    owned = None
    for layer in range(layer_count):
        last = layer == layer_count - 1
        part, dx, b_conv, decay = front(
            layer, ints, floats, everything, weights[layer], inner_kernel, proj_kernel,
            norm_gain, inner_cache, proj_cache, state_cache,
        )
        part, begun, owned = lax.optimization_barrier((part, begun, owned))
        received = swap(part)
        steps = states(layer, dx, b_conv, decay, state_cache, steps)
        received, steps = lax.optimization_barrier((received, steps))
        fresh = update(inner_width, received, block, not last)
        owned = owned_states(layer, state_cache, begun, received, owned)
        if not last:
            block = fresh[0]
            everything, send = lax.optimization_barrier((swap(fresh[1]), send))
            begun = swap(send)
    hidden = lax.ppermute(fresh[0], ("row", "col"), back)
    owned_block = owned[None, None]
    return (hidden, steps, owned_block)


def solution(mesh):
    placed = (
        P("col", "row"),
        P(None, "row"),
        P(None, "row", None, "col"),
        P(None, "row", None),
        P(None, "row", "col"),
        P(None, None, "col"),
        P(),
        P(None, "col"),
        P(None, "col"),
        P(None, "col"),
        P(None, "col"),
        P(None, "col", "row"),
        P(None, "row", None, "col"),
        P(None, "row", None, None),
        P(None, "row", "col", None, None),
        P("row"),
        P("row"),
        P(),
    )
    return jax.shard_map(
        local,
        mesh=mesh,
        in_specs=placed,
        out_specs=(
            P("col", "row"),
            P(None, "row", None, "col", None, None),
            P("row", "col", None, None, None, None, None),
        ),
        check_vma=False,
    )
```

```python
import jax
import jax.numpy as jnp
from jax import lax
from jax.experimental import pallas as pl
from jax.experimental.pallas import tpu as pltpu
from jax.sharding import PartitionSpec as P

S = 16
SEND_CAP = 2
EPSILON = 1e-05
ROWS = 8
COLS = 16
BF = jnp.bfloat16
F32 = jnp.float32
SUM_ROWS = 8
VMEM_BYTES = 58 * 1024 * 1024
SMALL_VMEM_BYTES = 12 * 1024 * 1024


def silu(v):
    return v / (1.0 + jnp.exp(-v))


def softplus(v):
    return jnp.maximum(v, 0.0) + jnp.log1p(jnp.exp(-jnp.abs(v)))


def pack_body(layer, inner_ref, proj_ref, step_ref, gain_ref, out_ref, packed_ref):
    rows, width = out_ref.shape
    states = proj_ref.shape[1]
    gain = jnp.broadcast_to(gain_ref[layer : layer + 1, :], (8, rows)).T[:, 0:1]
    step = step_ref[...].astype(F32)
    step = jnp.concatenate([step, jnp.zeros((128 - step.shape[0], rows), F32)], axis=0).T
    at = 0
    for piece in (inner_ref[0], inner_ref[1], proj_ref[...], step):
        end = at + piece.shape[1]
        packed_ref[:, at:end] = (piece.astype(F32) * gain).astype(BF)
        at = end
    packed_ref[:, at:] = out_ref[...]


def pack(layer, inner, proj, step, gain, out):
    planes = jnp.transpose(inner[layer], (1, 0, 2))
    rows, width = planes.shape[1:]
    cols = 2 * width + proj.shape[2] + 128 + out.shape[2]

    def layer_of(shape):
        return pl.BlockSpec((None,) + shape[1:], lambda i: (layer,) + (0,) * (len(shape) - 1))

    return pl.pallas_call(
        lambda *refs: pack_body(layer, *refs),
        name="pack%d" % layer,
        grid=(1,),
        in_specs=[
            pl.BlockSpec(planes.shape, lambda i: (0, 0, 0)),
            layer_of(proj.shape),
            layer_of(step.shape),
            pl.BlockSpec(gain.shape, lambda i: (0, 0)),
            layer_of(out.shape),
        ],
        out_specs=pl.BlockSpec((rows, cols), lambda i: (0, 0)),
        out_shape=jax.ShapeDtypeStruct((rows, cols), BF),
        compiler_params=pltpu.CompilerParams(
            dimension_semantics=("arbitrary",), vmem_limit_bytes=VMEM_BYTES
        ),
    )(planes, proj, step, gain, out)


def route(q, ints_ref, requests):
    owners, ranges = 2 + requests, 2 + 2 * requests
    request = ints_ref[0] + q
    live = (request >= ints_ref[ranges]) & (request < ints_ref[ranges + 1])
    for k in range(ranges + 2, ints_ref.shape[0], 2):
        live = live | ((request >= ints_ref[k]) & (request < ints_ref[k + 1]))
    owner = ints_ref[owners + q]
    rank = jnp.int32(0)
    for other in range(q):
        rank = rank + jnp.where(ints_ref[owners + other] == owner, 1, 0)
    return live, owner, jnp.minimum(rank, SEND_CAP - 1)


def front_body(
    layer,
    ints_ref,
    floats_ref,
    hidden_ref,
    weight_ref,
    inner_kernel_ref,
    proj_kernel_ref,
    norm_gain_ref,
    inner_cache_ref,
    proj_cache_ref,
    state_ref,
    part_ref,
    dx_ref,
    b_ref,
    dec_ref,
    x_pad,
    p_pad,
    misc_ref,
):
    requests, heads, head_size, state_size = state_ref.shape
    tokens = requests * S
    width = heads * head_size
    model_width = ROWS * hidden_ref.shape[2]
    block_tokens = hidden_ref.shape[1]
    in_cols = 2 * width + 2 * state_size + 128
    lane = lax.broadcasted_iota(jnp.int32, (1, 128), 1)

    def spread(pieces):
        return jnp.concatenate(
            [jnp.where(lane < 64, pieces[2 * k], pieces[2 * k + 1]) for k in range(heads // 2)],
            axis=1,
        )

    total = jnp.zeros((tokens, in_cols), F32)
    squares = jnp.zeros((tokens, 128), F32)
    for r in range(ROWS):
        rows_r = jnp.concatenate([hidden_ref[r], hidden_ref[ROWS + r]], axis=0)
        total = total + jnp.dot(rows_r, weight_ref[r, :, :in_cols], preferred_element_type=F32)
        wide = rows_r.astype(F32)
        wide = wide * wide
        squares = squares + wide[:, :128] + wide[:, 128:]
    inverse = lax.rsqrt(jnp.sum(squares, axis=1, keepdims=True) / model_width + EPSILON)
    total = total * inverse
    z = total[:, :width]
    x_pad[:, 8:24, :] = total[:, width : 2 * width].reshape(requests, S, width)
    p_pad[:, 8:24, :] = total[:, 2 * width : 2 * width + 2 * state_size].reshape(
        requests, S, 2 * state_size
    )
    x_pad[:, 5:8, :] = inner_cache_ref[...].astype(F32)
    p_pad[:, 5:8, :] = proj_cache_ref[...].astype(F32)
    conv_x = x_pad[:, 5 : 5 + S, :] * inner_kernel_ref[0:1, :]
    conv_p = p_pad[:, 5 : 5 + S, :] * proj_kernel_ref[0:1, :]
    for i in range(1, 4):
        conv_x = conv_x + x_pad[:, 5 + i : 5 + i + S, :] * inner_kernel_ref[i : i + 1, :]
        conv_p = conv_p + p_pad[:, 5 + i : 5 + i + S, :] * proj_kernel_ref[i : i + 1, :]
    x_conv = silu(conv_x).reshape(tokens, width)
    p_conv = silu(conv_p).reshape(tokens, 2 * state_size)
    b_conv = p_conv[:, :state_size]
    c_conv = p_conv[:, state_size:].astype(BF)
    b_ref[...] = b_conv
    step_raw = total[:, 2 * width + 2 * state_size :]
    t_now = lax.broadcasted_iota(jnp.int32, (tokens, tokens), 0)
    t_then = lax.broadcasted_iota(jnp.int32, (tokens, tokens), 1)
    causal = (t_now // S == t_then // S) & (t_then <= t_now)
    lower = causal.astype(F32)
    scores = lax.dot_general(
        c_conv, b_conv.astype(BF), (((1,), (1,)), ((), ())), preferred_element_type=F32
    )
    deltas = []
    sums_log = []
    mixes = []
    for h in range(heads):
        raw = jnp.broadcast_to(step_raw[:, h : h + 1], (tokens, 128))
        delta = softplus(raw + floats_ref[layer, h])
        rate = jnp.exp(jnp.full((1, 128), floats_ref[layer, heads + h], F32))
        log_decay = -delta * rate
        dec_ref[:, h * 128 : (h + 1) * 128] = jnp.exp(log_decay)
        cum = jnp.dot(
            lower, log_decay, precision=lax.Precision.HIGHEST, preferred_element_type=F32
        )
        gap = jnp.where(causal, cum - cum.T, 0.0)
        mixes.append((jnp.where(causal, jnp.exp(gap), 0.0) * scores).astype(BF))
        deltas.append(delta)
        sums_log.append(cum)
    dx = x_conv * spread(deltas)
    cum_all = spread(sums_log)
    grown = jnp.exp(cum_all)
    dx_ref[...] = dx
    y_diag = []
    for k in range(heads // 2):
        dx_k = dx[:, 128 * k : 128 * (k + 1)].astype(BF)
        first = jnp.dot(mixes[2 * k], dx_k, preferred_element_type=F32)
        second = jnp.dot(mixes[2 * k + 1], dx_k, preferred_element_type=F32)
        y_diag.append(jnp.where(lane < 64, first, second))
    y_off = []
    for q in range(requests):
        flat = state_ref[q].reshape(width, state_size).astype(BF)
        y_off.append(
            lax.dot_general(
                c_conv[q * S : (q + 1) * S, :], flat, (((1,), (1,)), ((), ())),
                preferred_element_type=F32,
            )
        )
    skip = spread([jnp.full((1, 128), floats_ref[layer, 2 * heads + h], F32) for h in range(heads)])
    y = (
        jnp.concatenate(y_diag, axis=1)
        + grown * jnp.concatenate(y_off, axis=0)
        + skip * x_conv
    )
    g = y * silu(z)
    yg = (g * norm_gain_ref[layer : layer + 1, :]).astype(BF)
    g2 = (g * g).astype(BF)
    ones = jnp.ones((SUM_ROWS, width), BF)
    misc_row = block_tokens + SEND_CAP * S
    line = lax.broadcasted_iota(jnp.int32, (SUM_ROWS, 1), 0)
    part_ref[:, block_tokens:misc_row, :] = jnp.zeros((COLS, SEND_CAP * S, width), BF)
    nothing = jnp.zeros((SUM_ROWS, width - block_tokens), F32)
    for b in range(2):
        sums = lax.dot_general(
            ones,
            g2[b * block_tokens : (b + 1) * block_tokens, :],
            (((1,), (1,)), ((), ())),
            preferred_element_type=F32,
        )
        sums = jnp.where(line == 0, jnp.concatenate([sums, nothing], axis=1), 0.0)
        for r in range(ROWS):
            misc_ref[b * ROWS + r] = sums
    step = lax.broadcasted_iota(jnp.int32, (S, 1), 0)
    column = ints_ref[1]
    for q in range(requests):
        live, owner, rank = route(q, ints_ref, requests)
        taken = ints_ref[2 + q] - 1
        rows = slice(q * S, (q + 1) * S)
        cum_q = cum_all[rows, :]
        cum_end = jnp.sum(jnp.where(step == taken, cum_q, 0.0), axis=0, keepdims=True)
        inside = step <= taken
        weight = jnp.where(inside, jnp.exp(jnp.where(inside, cum_end - cum_q, 0.0)), 0.0)
        scale = jnp.exp(cum_end)
        high = scale.astype(BF).astype(F32)
        low = scale - high
        mine = jnp.sum(jnp.where(step == column, b_conv[rows, :], 0.0), axis=0, keepdims=True)
        mine = jnp.concatenate([mine, jnp.zeros((1, width - state_size), F32)], axis=1)
        at = 1 + 3 * rank
        extra = jnp.where(
            line == at,
            mine,
            jnp.where(line == at + 1, high, jnp.where(line == at + 2, low, 0.0)),
        )
        first = pl.multiple_of(block_tokens + rank * S, S)

        @pl.when(live)
        def _send():
            part_ref[owner, pl.ds(first, S), :] = (dx[rows, :] * weight).astype(BF)
            misc_ref[owner] = misc_ref[owner] + extra

    part_ref[:, misc_row:, :] = misc_ref[...].astype(BF)
    for r in range(ROWS):
        part = jnp.dot(yg, weight_ref[r, :, in_cols:], preferred_element_type=F32).astype(BF)
        for b in range(2):
            part_ref[b * ROWS + r, 0:block_tokens, :] = part[
                b * block_tokens : (b + 1) * block_tokens, :
            ]


def front(layer, ints, floats, hidden, weight, inner_kernel, proj_kernel,
          norm_gain, inner_cache, proj_cache, state):
    layers, requests, heads, head_size, state_size = state.shape
    width = heads * head_size
    tokens = requests * S
    smem = pl.BlockSpec(memory_space=pltpu.SMEM)

    def whole(shape):
        return pl.BlockSpec(shape, lambda i: (0,) * len(shape))

    def layer_of(shape):
        return pl.BlockSpec((None,) + shape[1:], lambda i: (layer,) + (0,) * (len(shape) - 1))

    block_tokens = tokens // 2
    out_shapes = [
        ((COLS, block_tokens + SEND_CAP * S + SUM_ROWS, width), BF),
        ((tokens, width), F32),
        ((tokens, state_size), F32),
        ((tokens, heads * 128), F32),
    ]
    return pl.pallas_call(
        lambda *refs: front_body(layer, *refs),
        name="front%d" % layer,
        grid=(1,),
        in_specs=[
            smem, smem,
            whole(hidden.shape),
            whole(weight.shape),
            layer_of(inner_kernel.shape),
            layer_of(proj_kernel.shape),
            whole(norm_gain.shape),
            layer_of(inner_cache.shape),
            layer_of(proj_cache.shape),
            layer_of(state.shape),
        ],
        out_specs=[whole(shape) for shape, _ in out_shapes],
        out_shape=[jax.ShapeDtypeStruct(shape, kind) for shape, kind in out_shapes],
        scratch_shapes=[
            pltpu.VMEM((requests, 24, width), F32),
            pltpu.VMEM((requests, 24, 2 * state_size), F32),
            pltpu.VMEM((COLS, SUM_ROWS, width), F32),
        ],
        compiler_params=pltpu.CompilerParams(
            dimension_semantics=("arbitrary",), vmem_limit_bytes=VMEM_BYTES
        ),
    )(ints, floats, hidden, weight, inner_kernel, proj_kernel, norm_gain,
      inner_cache, proj_cache, state)


def states_body(dx_ref, b_ref, dec_ref, state_ref, *rest):
    steps_ref = rest[-1]
    heads, head_size, state_size = state_ref.shape
    dx_t = dx_ref[...].T
    for h in range(heads):
        state = state_ref[h]
        columns = dx_t[h * head_size : (h + 1) * head_size, :]
        for t in range(S):
            state = (
                state * dec_ref[t : t + 1, h * 128 : (h + 1) * 128]
                + columns[:, t : t + 1] * b_ref[t : t + 1, :]
            )
            steps_ref[t, h] = state.astype(BF)


def states(layer, dx, b, dec, state, previous):
    layers, requests, heads, head_size, state_size = state.shape
    width = heads * head_size
    in_specs = [
        pl.BlockSpec((S, width), lambda q: (q, 0)),
        pl.BlockSpec((S, state_size), lambda q: (q, 0)),
        pl.BlockSpec((S, heads * 128), lambda q: (q, 0)),
        pl.BlockSpec((None, None, heads, head_size, state_size), lambda q: (layer, q, 0, 0, 0)),
    ]
    operands = [dx, b, dec, state]
    aliases = {}
    if previous is not None:
        in_specs.append(pl.BlockSpec(memory_space=pl.ANY))
        aliases = {len(operands): 0}
        operands.append(previous)
    return pl.pallas_call(
        states_body,
        name="states%d" % layer,
        grid=(requests,),
        in_specs=in_specs,
        out_specs=pl.BlockSpec(
            (None, None, S, heads, head_size, state_size), lambda q: (layer, q, 0, 0, 0, 0)
        ),
        out_shape=jax.ShapeDtypeStruct(
            (layers, requests, S, heads, head_size, state_size), BF
        ),
        input_output_aliases=aliases,
        compiler_params=pltpu.CompilerParams(
            dimension_semantics=("arbitrary",), vmem_limit_bytes=SMALL_VMEM_BYTES
        ),
    )(*operands)


def starts_body(ints_ref, state_ref, send_ref):
    send_ref[...] = jnp.zeros(send_ref.shape, BF)
    requests = state_ref.shape[0]
    for q in range(requests):
        live, owner, rank = route(q, ints_ref, requests)

        @pl.when(live)
        def _put():
            send_ref[owner, rank] = state_ref[q].astype(BF)


def starts(layer, ints, state):
    shape = (COLS, SEND_CAP) + state.shape[2:]
    return pl.pallas_call(
        starts_body,
        name="starts%d" % layer,
        grid=(1,),
        in_specs=[
            pl.BlockSpec(memory_space=pltpu.SMEM),
            pl.BlockSpec((None,) + state.shape[1:], lambda i: (layer, 0, 0, 0, 0)),
        ],
        out_specs=pl.BlockSpec(shape, lambda i: (0, 0, 0, 0, 0)),
        out_shape=jax.ShapeDtypeStruct(shape, BF),
        compiler_params=pltpu.CompilerParams(
            dimension_semantics=("arbitrary",), vmem_limit_bytes=VMEM_BYTES
        ),
    )(ints, state)


def owned_body(layer, starts_ref, received_ref, *rest):
    out_ref, stage, b_s, sems = rest[-4:]
    cols, slots, heads, head_size, state_size = starts_ref.shape
    group = 2
    dx_rows = slots * S
    misc_at = received_ref.shape[1] - SUM_ROWS
    dx_at = misc_at - dx_rows
    b_s[...] = jnp.zeros(b_s.shape, F32)
    scales = []
    for c in range(cols):
        lines = received_ref[c, misc_at:, :].astype(F32)
        for slot in range(slots):
            row = 1 + 3 * slot
            b_s[
                slot * S + c : slot * S + c + 1, slot * state_size : (slot + 1) * state_size
            ] = lines[row : row + 1, 0:state_size]
            scales.append(lines[row + 1 : row + 2, :] + lines[row + 2 : row + 3, :])
    b_all = b_s[...].astype(BF)
    copies = []
    for i in range(cols // group):
        dx = jnp.concatenate(
            [received_ref[i * group + g, dx_at:misc_at, :] for g in range(group)], axis=1
        )
        added = lax.dot_general(dx, b_all, (((0,), (0,)), ((), ())), preferred_element_type=F32)
        for slot in range(slots):
            for g in range(group):
                c = i * group + g
                for h in range(heads):
                    scale = scales[c * slots + slot][:, h * head_size : h * head_size + 1]
                    at = (g * heads + h) * head_size
                    stage[slot, c * heads + h] = (
                        starts_ref[c, slot, h].astype(F32) * scale
                        + added[at : at + head_size, slot * state_size : (slot + 1) * state_size]
                    ).astype(BF)
            span = pl.ds(i * group * heads, group * heads)
            copies.append(
                pltpu.make_async_copy(
                    stage.at[slot, span],
                    out_ref.at[slot, layer, span],
                    sems.at[i * slots + slot],
                )
            )
            copies[-1].start()
    for copy in copies:
        copy.wait()


def owned_states(layer, state, begun, received, previous):
    layers, _, heads, head_size, state_size = state.shape
    resident = pl.BlockSpec(memory_space=pltpu.VMEM)
    anywhere = pl.BlockSpec(memory_space=pl.ANY)
    in_specs = [resident, resident]
    operands = [begun, received]
    aliases = {}
    if previous is not None:
        in_specs.append(anywhere)
        aliases = {len(operands): 0}
        operands.append(previous)
    all_heads = COLS * heads
    return pl.pallas_call(
        lambda *refs: owned_body(layer, *refs),
        name="owned%d" % layer,
        in_specs=in_specs,
        out_specs=anywhere,
        out_shape=jax.ShapeDtypeStruct(
            (SEND_CAP, layers, all_heads, head_size, state_size), BF
        ),
        scratch_shapes=[
            pltpu.VMEM((SEND_CAP, all_heads, head_size, state_size), BF),
            pltpu.VMEM((SEND_CAP * S, SEND_CAP * state_size), F32),
            pltpu.SemaphoreType.DMA((SEND_CAP * COLS // 2,)),
        ],
        input_output_aliases=aliases,
        compiler_params=pltpu.CompilerParams(vmem_limit_bytes=SMALL_VMEM_BYTES),
    )(*operands)


def update_body(inner_width, part_ref, sums_ref, hidden_ref, *outs):
    rows = hidden_ref.shape[0]
    total = part_ref[0].astype(F32)
    sums = sums_ref[0, :, 0:128].astype(F32)
    for c in range(1, COLS):
        total = total + part_ref[c].astype(F32)
        sums = sums + sums_ref[c, :, 0:128].astype(F32)
    scale = lax.rsqrt(sums.T[:rows, 0:1] / inner_width + EPSILON)
    fresh = (hidden_ref[...].astype(F32) + total * scale).astype(BF)
    outs[0][...] = fresh
    for spread_ref in outs[1:]:
        for c in range(COLS):
            spread_ref[c] = fresh


def update(inner_width, received, hidden, spread):
    rows, lanes = hidden.shape
    shapes = [hidden.shape] + ([(COLS,) + hidden.shape] if spread else [])
    sums_at = (rows + SEND_CAP * S) // SUM_ROWS

    def whole(shape):
        return pl.BlockSpec(shape, lambda i: (0,) * len(shape))

    return pl.pallas_call(
        lambda *refs: update_body(inner_width, *refs),
        name="update_spread" if spread else "update_last",
        grid=(1,),
        in_specs=[
            pl.BlockSpec((COLS, rows, lanes), lambda i: (0, 0, 0)),
            pl.BlockSpec((COLS, SUM_ROWS, lanes), lambda i: (0, sums_at, 0)),
            whole(hidden.shape),
        ],
        out_specs=[whole(shape) for shape in shapes],
        out_shape=[jax.ShapeDtypeStruct(shape, BF) for shape in shapes],
        compiler_params=pltpu.CompilerParams(
            dimension_semantics=("arbitrary",), vmem_limit_bytes=SMALL_VMEM_BYTES
        ),
    )(received, received, hidden)


def swap(x):
    return lax.all_to_all(x, "col", 0, 0, tiled=True)


def local(
    hidden_states,
    input_gain,
    inner_weight,
    proj_weight,
    step_weight,
    inner_kernel,
    proj_kernel,
    step_bias,
    decay_log,
    skip_gain,
    norm_gain,
    out_weight,
    inner_cache,
    proj_cache,
    state_cache,
    accepted,
    owners,
    tenant_ranges,
):
    layer_count = inner_weight.shape[0]
    inner_local = inner_weight.shape[3]
    heads_local = step_weight.shape[2]
    requests_local = state_cache.shape[1]
    inner_width = inner_local * COLS
    base = (lax.axis_index("row") * requests_local).astype(jnp.int32).reshape(1)
    column = lax.axis_index("col").astype(jnp.int32).reshape(1)
    ints = jnp.concatenate([base, column, accepted, owners, tenant_ranges.reshape(-1)])
    floats = jnp.concatenate([step_bias, decay_log, skip_gain], axis=1)

    there = []
    for r in range(ROWS):
        for c in range(COLS):
            there.append((r * COLS + c, (c // 2) * COLS + (c % 2) * ROWS + r))
    back = [(b, a) for a, b in there]

    block = lax.ppermute(hidden_states, ("row", "col"), there)
    raw = (
        inner_weight,
        proj_weight,
        jnp.transpose(step_weight, (0, 2, 1)),
        input_gain,
        out_weight,
    )
    first, block = lax.optimization_barrier((pack(0, *raw), block))
    weights = [lax.all_gather(first, "row", axis=0)]
    everything = swap(jnp.broadcast_to(block[None], (COLS,) + block.shape))
    sends = [starts(layer, ints, state_cache) for layer in range(layer_count)]
    sends, raw = lax.optimization_barrier((sends, raw))
    second = pack(1, *raw)
    everything, sends, second = lax.optimization_barrier((everything, sends, second))
    weights.append(lax.all_gather(second, "row", axis=0))
    begun = swap(sends[0])
    send = sends[1]

    steps = None
    owned = None
    for layer in range(layer_count):
        last = layer == layer_count - 1
        part, dx, b_conv, decay = front(
            layer, ints, floats, everything, weights[layer], inner_kernel, proj_kernel,
            norm_gain, inner_cache, proj_cache, state_cache,
        )
        part, begun, owned = lax.optimization_barrier((part, begun, owned))
        received = swap(part)
        steps = states(layer, dx, b_conv, decay, state_cache, steps)
        received, steps = lax.optimization_barrier((received, steps))
        fresh = update(inner_width, received, block, not last)
        owned = owned_states(layer, state_cache, begun, received, owned)
        if not last:
            block = fresh[0]
            everything, send = lax.optimization_barrier((swap(fresh[1]), send))
            begun = swap(send)
    hidden = lax.ppermute(fresh[0], ("row", "col"), back)
    owned_block = owned[None, None]
    return (hidden, steps, owned_block)


def solution(mesh):
    placed = (
        P("col", "row"),
        P(None, "row"),
        P(None, "row", None, "col"),
        P(None, "row", None),
        P(None, "row", "col"),
        P(None, None, "col"),
        P(),
        P(None, "col"),
        P(None, "col"),
        P(None, "col"),
        P(None, "col"),
        P(None, "col", "row"),
        P(None, "row", None, "col"),
        P(None, "row", None, None),
        P(None, "row", "col", None, None),
        P("row"),
        P("row"),
        P(),
    )
    return jax.shard_map(
        local,
        mesh=mesh,
        in_specs=placed,
        out_specs=(
            P("col", "row"),
            P(None, "row", None, "col", None, None),
            P("row", "col", None, None, None, None, None),
        ),
        check_vma=False,
    )
```
